32 devices in a mesh: dp: 8 (over z, y), seq: 4 (over x, core).
Axes of the slice: x: 2, y: 2, z: 4, core: 2. Of those that a mesh axis runs over, the one named last changes fastest.
Arguments:
- signal: bfloat16 [8, 512, 2048], P('dp', 'seq'), may hold values from -6 to 6
- gate_weight: bfloat16 [2048, 2048], P('dp'), may hold values from -0.125 to 0.125
- pos_weight: float32 [33, 64], replicated, may hold values from -4 to 4
- pos_bias: float32 [64], replicated, may hold values from -3.140625 to 3.140625
- filter_weight: float32 [64, 2048], replicated, may hold values from -0.75 to 0.75
- decay_rate: float32 [2048], replicated, as said below
- skip_gain: float32 [2048], replicated, may hold values from -4 to 4
- grad_out: bfloat16 [8, 512, 2048], P('dp', 'seq'), may hold values from -6 to 6
Outputs:
- output: bfloat16 [8, 512, 2048], P('dp', 'seq')
- grad_signal: bfloat16 [8, 512, 2048], P('dp', 'seq')
- grad_gate_weight: float32 [2048, 2048], P('dp')
- grad_pos_weight: float32 [33, 64], replicated
- grad_pos_bias: float32 [64], replicated
- grad_filter_weight: float32 [64, 2048], replicated
- grad_skip: float32 [2048], replicated
The draws below stay inside these ranges and needn't reach their ends.
Inputs may be any that keep to these rules, and one draw needn't show every extreme that they name: `decay_rate`: every rate is positive and at most 1/30.
All inputs are finite; a program needn't handle non-finite values.
Results may differ from the reference program's by a relative error of at most 0.015.
Values may be sent and summed in bfloat16 or wider, within the bound.
No kernel may reach another device: no remote copies, remote signals or barrier semaphores. Data moves between devices by JAX's collectives and lax.ppermute only.
A program may use at most 192 MiB of HBM per device.

```python
import math
import jax
import jax.numpy as jnp
from jax import lax

C = 2048
ORDER = 64
EMB = 33
SEQ_LEN = 512
SEQS = 8


def draw_decay_rate(key, part):
    key_slow = jax.random.fold_in(jax.random.fold_in(key, 7), 0)
    return jnp.exp(jax.random.uniform(key_slow, (C,), jnp.float32, math.log(0.05 / SEQ_LEN), math.log(1.0 / 30.0)))


def with_spikes(result, key, source, target, parts, factor):
    def block_of(dim):
        return (jnp.arange(result.shape[dim]) // (result.shape[dim] // parts)).reshape((-1,) + (1,) * (result.ndim - 1 - dim))

    first = jax.random.permutation(key, parts)[block_of(target)]
    second = (block_of(target) + parts // 2) % parts
    return jnp.where((block_of(source) == first) | (block_of(source) == second), factor * result, result)


def block_levels(key, extent, shards, least, top_value):
    def one(position, shards_of):
        heights = jax.random.uniform(jax.random.fold_in(jax.random.fold_in(key, 6), position), (shards_of,), jnp.float32, least / len(shards), top_value / len(shards))
        return jnp.repeat(jnp.exp(heights), extent[position] // shards_of).reshape((-1,) + (1,) * (len(extent) - position - 1))

    gain = one(*shards[0])
    for cut in shards[1:]:
        gain = gain * one(*cut)
    return gain


def gaussian(key, shape, deviation, limit, shards=(), kind=jnp.bfloat16):
    factor_of = block_levels(key, shape, shards, -0.22, 0.18) if shards else 1.0
    result = jax.random.normal(key, shape, jnp.float32) * deviation * factor_of
    return jnp.minimum(jnp.maximum(result, -limit), limit).astype(kind)


def heavy_noise(own_key, shape, spread, reach, cuts, heavy, held_as=jnp.bfloat16):
    array = spread * jax.random.normal(own_key, shape, jnp.float32)
    if cuts:
        array = array * block_levels(own_key, shape, cuts, -0.22, 0.18)
    return jnp.clip(with_spikes(array, jax.random.fold_in(own_key, 3), *heavy), -reach, reach).astype(held_as)


def setup_inputs(seed: int = 0) -> dict:
    arg_keys = jax.random.split(jax.random.key(seed), 9)
    return {
        "signal": heavy_noise(arg_keys[0], (SEQS, SEQ_LEN, C), 1.0, 6.0, ((0, 8), (1, 4)), (0, 2, 8, 2.0)),
        "gate_weight": gaussian(arg_keys[1], (C, C), C ** -0.5, 0.125, ((0, 8),)),
        "pos_weight": gaussian(arg_keys[2], (EMB, ORDER), 1.0, 4.0, (), jnp.float32),
        "pos_bias": jnp.clip(jax.random.uniform(arg_keys[3], (ORDER,), jnp.float32, -3.140625, 3.140625), -3.140625, 3.140625),
        "filter_weight": gaussian(arg_keys[4], (ORDER, C), ORDER ** -0.5, 0.75, (), jnp.float32),
        "decay_rate": draw_decay_rate(jax.random.fold_in(arg_keys[8], 71), 0),
        "skip_gain": gaussian(arg_keys[6], (C,), 1.0, 4.0, (), jnp.float32),
        "grad_out": gaussian(arg_keys[7], (SEQS, SEQ_LEN, C), 1.0, 6.0, ((0, 8), (1, 4))),
    }


def features(positions, length, emb_count):
    bands = jnp.arange(1, (emb_count - 1) // 2 + 1, dtype=jnp.int32)
    phase = positions[:, None] * bands[None, :] % length
    angle = phase.astype(jnp.float32) * (2.0 * math.pi / length)
    scaled = positions.astype(jnp.float32)[:, None] / length
    return jnp.concatenate([scaled, jnp.cos(angle), jnp.sin(angle)], axis=1)

def envelope(rates, positions, length):
    total = jnp.expm1(-2.0 * rates * length) / jnp.expm1(-2.0 * rates)
    decayed = jnp.exp(-rates[None, :] * positions.astype(jnp.float32)[:, None])
    return decayed / jnp.sqrt(total)[None, :]

def reference(signal, gate_weight, pos_weight, pos_bias, filter_weight, decay_rate, skip_gain, grad_out):
    highest = lax.Precision.HIGHEST
    positions = jnp.arange(SEQ_LEN, dtype=jnp.int32)
    table = features(positions, SEQ_LEN, EMB)
    pre = jnp.dot(table, pos_weight, precision=highest) + pos_bias
    hidden = jnp.sin(pre)
    shape_env = envelope(decay_rate, positions, SEQ_LEN)
    filt = (jnp.dot(hidden, filter_weight, precision=highest) * shape_env).astype(jnp.bfloat16)
    fft_len = 2 * SEQ_LEN
    filt_spec = jnp.fft.rfft(filt.astype(jnp.float32), n=fft_len, axis=0)

    def transcript(carry, inputs):
        weight_grad, skip_grad, filt_grad = carry
        signal_one, cot_one = inputs
        gate = jnp.dot(signal_one, gate_weight, preferred_element_type=jnp.float32)
        signal_wide = signal_one.astype(jnp.float32)
        signal_spec = jnp.fft.rfft(signal_wide, n=fft_len, axis=0)
        conv = jnp.fft.irfft(signal_spec * filt_spec, n=fft_len, axis=0)[:SEQ_LEN].astype(jnp.bfloat16)
        inner = conv.astype(jnp.float32) + skip_gain * signal_wide
        output = (gate * inner).astype(jnp.bfloat16)
        cot_wide = cot_one.astype(jnp.float32)
        gate_grad = (cot_wide * inner).astype(jnp.bfloat16)
        inner_grad = cot_wide * gate
        conv_grad = inner_grad.astype(jnp.bfloat16)
        grad_spec = jnp.fft.rfft(conv_grad.astype(jnp.float32), n=fft_len, axis=0)
        conv_back = jnp.fft.irfft(jnp.conj(filt_spec) * grad_spec, n=fft_len, axis=0)[:SEQ_LEN].astype(jnp.bfloat16)
        filt_part = jnp.fft.irfft(jnp.conj(signal_spec) * grad_spec, n=fft_len, axis=0)[:SEQ_LEN].astype(jnp.bfloat16)
        grad_signal = jnp.dot(gate_grad, gate_weight.T, preferred_element_type=jnp.float32)
        grad_signal = (grad_signal + inner_grad * skip_gain + conv_back.astype(jnp.float32)).astype(jnp.bfloat16)
        weight_grad = weight_grad + jnp.dot(signal_one.T, gate_grad, preferred_element_type=jnp.float32)
        skip_grad = skip_grad + lax.optimization_barrier(jnp.sum(inner_grad * signal_wide, axis=0))
        filt_grad = filt_grad + filt_part.astype(jnp.float32)
        return ((weight_grad, skip_grad, filt_grad), (output, grad_signal))
    start = (jnp.zeros((C, C), jnp.float32), jnp.zeros((C,), jnp.float32), jnp.zeros((SEQ_LEN, C), jnp.float32))
    sums, outputs = lax.scan(transcript, start, (signal, grad_out))
    weight_grad, skip_grad, filt_grad = sums
    output, grad_signal = outputs
    filt_pre_grad = filt_grad * shape_env
    grad_filter_weight = jnp.dot(hidden.T, filt_pre_grad, precision=highest)
    act_grad = jnp.dot(filt_pre_grad, filter_weight.T, precision=highest) * jnp.cos(pre)
    grad_pos_weight = jnp.dot(table.T, act_grad, precision=highest)
    grad_pos_bias = lax.optimization_barrier(jnp.sum(act_grad, axis=0))
    return (output, grad_signal, weight_grad, grad_pos_weight, grad_pos_bias, grad_filter_weight, skip_grad)
```

```python
import functools
import math

import jax
import jax.numpy as jnp
import numpy as np
from jax import lax
from jax.experimental import pallas as pl
from jax.experimental.pallas import tpu as pltpu
from jax.sharding import PartitionSpec as P


f32 = jnp.float32
bf16 = jnp.bfloat16
VMEM = pltpu.VMEM


BASE = 16


@functools.lru_cache(maxsize=None)
def feature_table(length, emb_count):
    positions = np.arange(length)
    bands = np.arange(1, (emb_count - 1) // 2 + 1)
    angle = positions[:, None] * bands[None, :] % length * (2.0 * math.pi / length)
    table = np.concatenate(
        [positions[:, None] / length, np.cos(angle), np.sin(angle), np.ones((length, 1))], axis=1
    )
    rows = -(-table.shape[1] // 8) * 8
    return np.pad(table, ((0, 0), (0, rows - table.shape[1]))).astype(np.float32)


@functools.lru_cache(maxsize=None)
def angle_factors(length):
    step = 4 * length
    lane = np.arange(length)[None, :]
    coarse = np.arange(length // BASE)[:, None]
    fine = np.arange(BASE)[:, None]
    found = []
    for phase in (
        coarse * lane * (4 * BASE),
        (4 * fine + 1) * lane,
        coarse * BASE * (4 * lane + 1),
        fine * (4 * lane + 1),
    ):
        angle = phase % step * (2.0 * math.pi / step)
        found.append(np.stack([np.cos(angle), np.sin(angle)]).astype(np.float32))
    return found


def dot(a, b):
    return jnp.dot(a, b, preferred_element_type=f32)


def dot_first(a, b):
    return lax.dot_general(a, b, (((0,), (0,)), ((), ())), preferred_element_type=f32)


def dot_last(a, b):
    return lax.dot_general(a, b, (((1,), (1,)), ((), ())), preferred_element_type=f32)


def split(x):
    high = x.astype(bf16)
    return high, (x - high.astype(f32)).astype(bf16)


def careful(product, a, b):
    a_high, a_low = split(a)
    b_high, b_low = split(b)
    return product(a_high, b_high) + (product(a_low, b_high) + product(a_high, b_low))


def to_spectrum(a_high, a_low, part, x):
    return dot(a_high[part], x) + dot(a_low[part], x)


def from_spectrum(t_high, re, im, length):
    total = dot(t_high[0], re.astype(bf16)) + dot(t_high[1], im.astype(bf16))
    return total * (1.0 / length)


def struct(shape, kind):
    return jax.ShapeDtypeStruct(shape, kind)


def whole(shape):
    return pl.BlockSpec(shape, lambda i, *_: (0,) * len(shape))


def table_specs(length, block):
    by_row = pl.BlockSpec((2, block, length), lambda i, *_: (0, i, 0))
    by_col = pl.BlockSpec((2, length, block), lambda i, *_: (0, 0, i))
    return by_row, by_col


def spectrum_block(length, width, block):
    return pl.BlockSpec((2, block, width), lambda i, *_: (0, i, 0))


def generate(place, table, factors, pos_weight, pos_bias, filter_weight, rates, norm, width, block):
    highest = lax.Precision.HIGHEST
    length, table_rows = table.shape
    order = pos_weight.shape[1]
    emb_count = pos_weight.shape[0]

    def body(
        place_ref, tab, ac, af, tc, tf, pw, pb, fw, rate, norm_ref,
        ah, al, th, spec, env_out, hidden_out, cos_out, filt,
    ):
        step = pl.program_id(0)

        @pl.when(step == 0)
        def _():
            pre = jnp.dot(tab[:, :emb_count], pw[...], precision=highest) + pb[...]
            hidden = jnp.sin(pre)
            hidden_out[...] = hidden
            cos_out[...] = jnp.cos(pre)
            at = lax.broadcasted_iota(jnp.int32, (length, width), 0).astype(f32)
            env = jnp.exp(-rate[...] * at) / norm_ref[...]
            env_out[...] = env
            filt[...] = (jnp.dot(hidden, fw[...], precision=highest) * env).astype(bf16)

        def rows(coarse, fine, store):
            def one(i, carry):
                here = pl.ds(step * (block // BASE) + i, 1)
                out = pl.ds(pl.multiple_of(i * BASE, BASE), BASE)
                cos, sin = coarse[0, here, :], coarse[1, here, :]
                store(out, 0, cos * fine[0] - sin * fine[1])
                store(out, 1, sin * fine[0] + cos * fine[1])
                return carry

            lax.fori_loop(0, block // BASE, one, 0)

        def store_both(out, part, value):
            high, low = split(value)
            ah[part, out, :] = high
            al[part, out, :] = low

        def store_high(out, part, value):
            th[part, out, :] = value.astype(bf16)

        rows(ac, af, store_both)
        rows(tc, tf, store_high)
        spec[0] = to_spectrum(ah, al, 0, filt[...])
        spec[1] = to_spectrum(ah, al, 1, filt[...])

    by_row = pl.BlockSpec((2, block, length), lambda i, *_: (0, i, 0))
    cols = lambda n: pl.BlockSpec((n, width), lambda i, place_ref: (0, place_ref[0]))
    return pl.pallas_call(
        body,
        grid_spec=pltpu.PrefetchScalarGridSpec(
            num_scalar_prefetch=1,
            grid=(length // block,),
            in_specs=[whole(table.shape)]
            + [whole(f.shape) for f in factors]
            + [whole(pos_weight.shape), whole(pos_bias.shape), cols(order), cols(1), cols(1)],
            out_specs=[by_row, by_row, by_row, spectrum_block(length, width, block)]
            + [whole((length, width)), whole((length, order)), whole((length, order))],
            scratch_shapes=[VMEM((length, width), bf16)],
        ),
        out_shape=[struct((2, length, length), bf16)] * 3
        + [struct((2, length, width), f32), struct((length, width), f32)]
        + [struct((length, order), f32)] * 2,
        name="generate",
    )(place, table, *factors, pos_weight, pos_bias, filter_weight, rates, norm)


def piece(place_ref, r, rows):
    return pl.ds(pl.multiple_of((place_ref[0] ^ r) * rows, rows), rows)


def convolve(place, signal_rel, cot_rel, filt_spec, tables, skip, block):
    a_high, a_low, t_high = tables
    count = len(signal_rel)
    local_len, width = cot_rel[0].shape
    length = local_len * count

    def body(place_ref, *refs):
        sig = refs[:count]
        cot = refs[count : 2 * count]
        fs, ah, al, th, skip_ref = refs[2 * count : 2 * count + 5]
        spec, inner_out, grad_out, x, acc = refs[2 * count + 5 :]
        step = pl.program_id(0)

        @pl.when(step == 0)
        def _():
            for r in range(count):
                x[piece(place_ref, r, local_len), :] = sig[r][...]

        re = to_spectrum(ah, al, 0, x[...])
        im = to_spectrum(ah, al, 1, x[...])
        spec[0] = re
        spec[1] = im
        part = from_spectrum(th, re * fs[0] - im * fs[1], re * fs[1] + im * fs[0], length)

        @pl.when(step == 0)
        def _():
            acc[...] = part

        @pl.when(step != 0)
        def _():
            acc[...] += part

        @pl.when(step == pl.num_programs(0) - 1)
        def _():
            conv = acc[...].astype(bf16).astype(f32)
            inner_out[...] = conv + skip_ref[...] * x[...].astype(f32)
            for r in range(count):
                rows = piece(place_ref, r, local_len)
                grad_out[rows, :] = (cot[r][...].astype(f32) * inner_out[rows, :]).astype(bf16)

    by_row, by_col = table_specs(length, block)
    cols = pl.BlockSpec((local_len, width), lambda i, place_ref: (0, place_ref[0]))
    return pl.pallas_call(
        body,
        grid_spec=pltpu.PrefetchScalarGridSpec(
            num_scalar_prefetch=1,
            grid=(length // block,),
            in_specs=[cols] * count
            + [whole((local_len, width))] * count
            + [spectrum_block(length, width, block), by_row, by_row, by_col]
            + [pl.BlockSpec((1, width), lambda i, place_ref: (0, place_ref[0]))],
            out_specs=[
                spectrum_block(length, width, block),
                whole((length, width)),
                whole((length, width)),
            ],
            scratch_shapes=[VMEM((length, width), bf16), VMEM((length, width), f32)],
        ),
        out_shape=[
            struct((2, length, width), f32),
            struct((length, width), f32),
            struct((length, width), bf16),
        ],
        name="convolve",
    )(place, *signal_rel, *cot_rel, filt_spec, a_high, a_low, t_high, skip)


def smem():
    return pl.BlockSpec(memory_space=pltpu.SMEM)


def weight_grads(place, signal_rel, gate_grad, groups):
    count = len(signal_rel)
    local_len, channels = signal_rel[0].shape
    width = gate_grad.shape[1]
    rows = channels // sum(len(group) for group in groups)

    def body(place_ref, *refs):
        sig = refs[:count]
        grad = refs[count]
        outs = refs[count + 1 :]
        right = jnp.concatenate(
            [grad[piece(place_ref, r, local_len), :] for r in range(count)], axis=0
        )
        for out, group in zip(outs, groups):
            for at, k in enumerate(group):
                start = pl.multiple_of((place_ref[1] ^ k) * rows, rows)
                left = jnp.concatenate(
                    [sig[r][:, pl.ds(start, rows)] for r in range(count)], axis=0
                )
                out[at] = dot_first(left, right).astype(bf16)

    return pl.pallas_call(
        body,
        in_specs=[smem()] + [pl.BlockSpec(memory_space=VMEM)] * (count + 1),
        out_specs=[pl.BlockSpec(memory_space=VMEM)] * len(groups),
        out_shape=[struct((len(group), rows, width), bf16) for group in groups],
        name="weight_grads",
    )(place, *signal_rel, gate_grad)


def gating(place, signal_rel, weight_rel, cot_rel, inner):
    count = len(signal_rel)
    dp_count = len(weight_rel)
    local_len, channels = signal_rel[0].shape
    rows, width = weight_rel[0].shape
    length = local_len * count

    def body(place_ref, *refs):
        sig = refs[:count]
        weight = refs[count : count + dp_count]
        cot = refs[count + dp_count : 2 * count + dp_count]
        inner_ref = refs[2 * count + dp_count]
        outs = refs[2 * count + dp_count + 1 : -1]
        full = refs[-1]
        inner_grad_out, conv_grad_out, skip_out = outs[count:]
        for k in range(dp_count):
            start = pl.multiple_of((place_ref[1] ^ k) * rows, rows)
            full[pl.ds(start, rows), :] = weight[k][...]
        left = jnp.concatenate([sig[r][...] for r in range(count)], axis=0)
        gates = dot(left, full[...])
        skip_sum = jnp.zeros((1, width), f32)
        own = pl.multiple_of(place_ref[0] * width, width)
        for r in range(count):
            here = piece(place_ref, r, local_len)
            gate = gates[r * local_len : (r + 1) * local_len]
            outs[r][...] = (gate * inner_ref[here, :]).astype(bf16)
            inner_grad = cot[r][...].astype(f32) * gate
            inner_grad_out[here, :] = inner_grad
            conv_grad_out[here, :] = inner_grad.astype(bf16)
            signal = sig[r][:, pl.ds(own, width)].astype(f32)
            skip_sum += jnp.sum(inner_grad * signal, axis=0, keepdims=True)
        skip_out[...] = jnp.broadcast_to(skip_sum, (8, width))

    return pl.pallas_call(
        body,
        in_specs=[smem()] + [pl.BlockSpec(memory_space=VMEM)] * (2 * count + dp_count + 1),
        out_specs=[pl.BlockSpec(memory_space=VMEM)] * (count + 3),
        out_shape=[struct((local_len, width), bf16)] * count
        + [
            struct((length, width), f32),
            struct((length, width), bf16),
            struct((8, width), f32),
        ],
        scratch_shapes=[VMEM((channels, width), bf16)],
        name="gating",
    )(place, *signal_rel, *weight_rel, *cot_rel, inner)


def packed_rows(order, table_rows, width):
    per_group = width // order
    groups = -(-(table_rows // 8) // per_group)
    return order + 8 + 8 * groups, per_group


def correlate(
    place, conv_grad, inner_grad, skip_sum, filt_spec, signal_spec, tables, skip, env, hidden,
    filter_weight, cos_pre, table_t, block,
):
    a_high, a_low, t_high = tables
    length, width = conv_grad.shape
    order = filter_weight.shape[0]
    table_rows = table_t.shape[0]
    total_rows, per_group = packed_rows(order, table_rows, width)

    def body(
        place_ref, cg, ig, skip_sum_ref, fs, ss, ah, al, th, skip_ref, env_ref, hid, fw, cp, tab,
        direct_out, packed, back, part,
    ):
        step = pl.program_id(0)
        re = to_spectrum(ah, al, 0, cg[...])
        im = to_spectrum(ah, al, 1, cg[...])
        part_term = from_spectrum(th, ss[0] * re + ss[1] * im, ss[0] * im - ss[1] * re, length)
        back_term = from_spectrum(th, fs[0] * re + fs[1] * im, fs[0] * im - fs[1] * re, length)

        @pl.when(step == 0)
        def _():
            back[...] = back_term
            part[...] = part_term

        @pl.when(step != 0)
        def _():
            back[...] += back_term
            part[...] += part_term

        @pl.when(step == pl.num_programs(0) - 1)
        def _():
            direct_out[...] = ig[...] * skip_ref[...] + back[...].astype(bf16).astype(f32)
            pre_grad = part[...].astype(bf16).astype(f32) * env_ref[...]
            packed[...] = jnp.zeros((total_rows, width), f32)
            packed[:order, :] = careful(dot_first, hid[...], pre_grad)
            packed[order : order + 8, :] = skip_sum_ref[...]
            act = careful(dot_last, pre_grad, fw[...]) * cp[...]
            small = careful(dot, tab[...], act)
            for b in range(table_rows // 8):
                row = order + 8 + 8 * (b // per_group)
                col = order * (b % per_group)
                packed[row : row + 8, col : col + order] = small[8 * b : 8 * b + 8]

    by_row, by_col = table_specs(length, block)
    spec_block = spectrum_block(length, width, block)
    return pl.pallas_call(
        body,
        grid_spec=pltpu.PrefetchScalarGridSpec(
            num_scalar_prefetch=1,
            grid=(length // block,),
            in_specs=[
                whole((length, width)),
                whole((length, width)),
                whole((8, width)),
                spec_block,
                spec_block,
                by_row,
                by_row,
                by_col,
                pl.BlockSpec((1, width), lambda i, place_ref: (0, place_ref[0])),
                whole((length, width)),
                whole(hidden.shape),
                pl.BlockSpec((order, width), lambda i, place_ref: (0, place_ref[0])),
                whole(cos_pre.shape),
                whole(table_t.shape),
            ],
            out_specs=[whole((length, width)), whole((total_rows, width))],
            scratch_shapes=[VMEM((length, width), f32), VMEM((length, width), f32)],
        ),
        out_shape=[struct((length, width), f32), struct((total_rows, width), f32)],
        name="correlate",
    )(
        place, conv_grad, inner_grad, skip_sum, filt_spec, signal_spec, a_high, a_low, t_high,
        skip, env, hidden, filter_weight, cos_pre, table_t,
    )


def through_gate(place, gate_grad, weight_rel, direct, count):
    dp_count = len(weight_rel)
    rows, width = weight_rel[0].shape
    length = gate_grad.shape[0]
    local_len = length // count
    channels = rows * dp_count

    def body(place_ref, *refs):
        grad = refs[0]
        weight = refs[1 : 1 + dp_count]
        direct_ref = refs[1 + dp_count]
        outs = refs[2 + dp_count :]
        left = jnp.concatenate(
            [grad[piece(place_ref, r, local_len), :] for r in range(count)], axis=0
        )
        for k in range(dp_count):
            start = pl.multiple_of((place_ref[1] ^ k) * rows, rows)
            shift = start - place_ref[0] * width
            inside = jnp.logical_and(shift >= 0, shift < width)
            shift = pl.multiple_of(jnp.clip(shift, 0, width - rows), rows)
            scale = jnp.where(inside, 1.0, 0.0).astype(f32)
            terms = dot_last(left, weight[k][...])
            for r in range(count):
                term = terms[r * local_len : (r + 1) * local_len]
                term += scale * direct_ref[piece(place_ref, r, local_len), pl.ds(shift, rows)]
                outs[r][:, pl.ds(start, rows)] = term.astype(bf16)

    return pl.pallas_call(
        body,
        in_specs=[smem()] + [pl.BlockSpec(memory_space=VMEM)] * (dp_count + 2),
        out_specs=[pl.BlockSpec(memory_space=VMEM)] * count,
        out_shape=[struct((local_len, channels), bf16)] * count,
        name="through_gate",
    )(place, gate_grad, *weight_rel, direct)


def assemble(place, pieces, kind):
    count = len(pieces)
    rows, width = pieces[0].shape

    def body(place_ref, *refs):
        out = refs[count]
        for r in range(count):
            start = pl.multiple_of((place_ref[0] ^ r) * width, width)
            out[:, pl.ds(start, width)] = refs[r][...].astype(kind)

    return pl.pallas_call(
        body,
        in_specs=[smem()] + [pl.BlockSpec(memory_space=VMEM)] * count,
        out_specs=pl.BlockSpec(memory_space=VMEM),
        out_shape=struct((rows, width * count), kind),
        name="assemble",
    )(place, *pieces)


def finish(place, pieces, order, emb_count):
    count = len(pieces)
    rows, width = pieces[0].shape
    table_rows = -(-(emb_count + 1) // 8) * 8
    _, per_group = packed_rows(order, table_rows, width)

    def body(place_ref, *refs):
        filter_out, skip_out, pos_out, bias_out = refs[count:]
        for r in range(count):
            cols = pl.ds(pl.multiple_of((place_ref[0] ^ r) * width, width), width)
            filter_out[:, cols] = refs[r][:order, :]
            skip_out[:, cols] = refs[r][order : order + 1, :]
        tails = [refs[r][order + 8 :, :] for r in range(count)]
        while len(tails) > 1:
            tails = [tails[i] + tails[i + 1] for i in range(0, len(tails), 2)]
        for b in range(table_rows // 8):
            row = 8 * (b // per_group)
            col = order * (b % per_group)
            found = tails[0][row : row + 8, col : col + order]
            low = 8 * b
            high = min(low + 8, emb_count)
            if high > low:
                pos_out[low:high, :] = found[: high - low]
            if low <= emb_count < low + 8:
                bias_out[...] = found[emb_count - low : emb_count - low + 1]

    return pl.pallas_call(
        body,
        in_specs=[smem()] + [pl.BlockSpec(memory_space=VMEM)] * count,
        out_specs=[pl.BlockSpec(memory_space=VMEM)] * 4,
        out_shape=[
            struct((order, width * count), f32),
            struct((1, width * count), f32),
            struct((emb_count, order), f32),
            struct((1, order), f32),
        ],
        name="finish",
    )(place, *pieces)


def swap(value, axis, offset):
    count = lax.axis_size(axis)
    return lax.ppermute(value, axis, [(i, i ^ offset) for i in range(count)])


def gather_rel(own, axis):
    count = lax.axis_size(axis)
    found = {0: own}
    bit = count // 2
    while bit:
        for r in list(found):
            found[r | bit] = swap(found[r], axis, bit)
        bit //= 2
    return [found[r] for r in range(count)]


def add_round(*terms):
    total = terms[0].astype(f32)
    for term in terms[1:]:
        total = total + term.astype(f32)
    return total.astype(bf16)


def shards(
    signal, gate_weight, pos_weight, pos_bias, filter_weight, decay_rate, skip_gain, grad_out
):
    seq_count = lax.axis_size("seq")
    dp_count = lax.axis_size("dp")
    signal_tok = signal[0]
    cot_tok = grad_out[0]
    local_len, channels = signal_tok.shape
    length = local_len * seq_count
    width = channels // seq_count
    emb_count, order = pos_weight.shape
    seq_at = lax.axis_index("seq")
    dp_at = lax.axis_index("dp")
    place = jnp.stack([seq_at, dp_at]).astype(jnp.int32)
    block = min(256, length)

    def own_cols(x, r=0):
        return lax.dynamic_slice_in_dim(x, (seq_at ^ r) * width, width, axis=x.ndim - 1)

    signal_rel = gather_rel(signal_tok, "seq")
    weight_rel = {0: own_cols(gate_weight)}
    for k in range(2, dp_count, 2):
        weight_rel[k] = swap(weight_rel[0], "dp", k)
    for k in range(0, dp_count, 2):
        weight_rel[k + 1] = swap(weight_rel[k], "dp", 1)
    weight_rel = [weight_rel[k] for k in range(dp_count)]
    cot_rel = [own_cols(cot_tok)] + [
        swap(own_cols(cot_tok, r), "seq", r) for r in range(1, seq_count)
    ]

    table = feature_table(length, emb_count)
    rates = decay_rate[None]
    norm = jnp.sqrt(jnp.expm1(-2.0 * rates * length) / jnp.expm1(-2.0 * rates))
    skip = skip_gain[None]
    a_high, a_low, t_high, filt_spec, env, hidden, cos_pre = generate(
        place, jnp.asarray(table), [jnp.asarray(f) for f in angle_factors(length)], pos_weight,
        pos_bias[None], filter_weight, rates, norm, width, block,
    )
    tables = (a_high, a_low, t_high)

    signal_spec, inner, gate_grad = convolve(
        place, signal_rel, cot_rel, filt_spec, tables, skip, block
    )

    far = list(reversed(range(0, dp_count, 2)))
    pairs = [far[i : i + 2] for i in range(0, len(far), 2)]
    groups = [[k + 1 for k in pair] for pair in pairs] + pairs
    weight_parts = weight_grads(place, signal_rel, gate_grad, groups)
    sums = {}
    for i, pair in enumerate(pairs):
        met = swap(weight_parts[i], "dp", 1)
        for at, k in enumerate(pair):
            sums[k] = add_round(weight_parts[len(pairs) + i][at], met[at])
    row_sum = add_round(sums[0], *[swap(sums[k], "dp", k) for k in far[:-1]])
    grad_gate_weight = assemble(place, gather_rel(row_sum, "seq"), f32)

    gated = gating(place, signal_rel, weight_rel, cot_rel, inner)
    out_rel = gated[:seq_count]
    inner_grad, conv_grad, skip_sum = gated[seq_count:]
    output = assemble(
        place,
        [out_rel[0]] + [swap(out_rel[r], "seq", r) for r in range(1, seq_count)],
        bf16,
    )

    direct, packed = correlate(
        place, conv_grad, inner_grad, skip_sum, filt_spec, signal_spec, tables, skip, env, hidden,
        filter_weight, cos_pre, jnp.asarray(table.T), block,
    )
    back_rel = through_gate(place, gate_grad, weight_rel, direct, seq_count)

    live = {r: back_rel[r] for r in range(seq_count)}
    bit = 1
    while bit < seq_count:
        live = {
            r: add_round(live[r], swap(live[r | bit], "seq", bit))
            for r in live
            if not r & bit
        }
        bit *= 2
    grad_signal = live[0]

    bit = 1
    while bit < dp_count:
        packed = packed + swap(packed, "dp", bit)
        bit *= 2
    grad_filter_weight, grad_skip, grad_pos_weight, grad_pos_bias = finish(
        place, gather_rel(packed, "seq"), order, emb_count
    )
    return (
        output[None],
        grad_signal[None],
        grad_gate_weight,
        grad_pos_weight,
        grad_pos_bias[0],
        grad_filter_weight,
        grad_skip[0],
    )


def solution(mesh):
    return jax.shard_map(
        shards,
        mesh=mesh,
        in_specs=(
            P("dp", "seq", None),
            P("dp", None),
            P(),
            P(),
            P(),
            P(),
            P(),
            P("dp", "seq", None),
        ),
        out_specs=(P("dp", "seq", None), P("dp", "seq", None), P("dp", None), P(), P(), P(), P()),
        check_vma=False,
    )
```

```python
import functools
import math

import jax
import jax.numpy as jnp
import numpy as np
from jax import lax
from jax.experimental import pallas as pl
from jax.experimental.pallas import tpu as pltpu
from jax.sharding import PartitionSpec as P


f32 = jnp.float32
bf16 = jnp.bfloat16
VMEM = pltpu.VMEM


BASE = 16


@functools.lru_cache(maxsize=None)
def feature_table(length, emb_count):
    positions = np.arange(length)
    bands = np.arange(1, (emb_count - 1) // 2 + 1)
    angle = positions[:, None] * bands[None, :] % length * (2.0 * math.pi / length)
    table = np.concatenate(
        [positions[:, None] / length, np.cos(angle), np.sin(angle), np.ones((length, 1))], axis=1
    )
    rows = -(-table.shape[1] // 8) * 8
    return np.pad(table, ((0, 0), (0, rows - table.shape[1]))).astype(np.float32)


@functools.lru_cache(maxsize=None)
def angle_factors(length):
    step = 4 * length
    lane = np.arange(length)[None, :]
    coarse = np.arange(length // BASE)[:, None]
    fine = np.arange(BASE)[:, None]
    found = []
    for phase in (
        coarse * lane * (4 * BASE),
        (4 * fine + 1) * lane,
        coarse * BASE * (4 * lane + 1),
        fine * (4 * lane + 1),
    ):
        angle = phase % step * (2.0 * math.pi / step)
        found.append(np.stack([np.cos(angle), np.sin(angle)]).astype(np.float32))
    return found


def dot(a, b):
    return jnp.dot(a, b, preferred_element_type=f32)


def dot_first(a, b):
    return lax.dot_general(a, b, (((0,), (0,)), ((), ())), preferred_element_type=f32)


def dot_last(a, b):
    return lax.dot_general(a, b, (((1,), (1,)), ((), ())), preferred_element_type=f32)


def split(x):
    high = x.astype(bf16)
    return high, (x - high.astype(f32)).astype(bf16)


def careful(product, a, b):
    a_high, a_low = split(a)
    b_high, b_low = split(b)
    return product(a_high, b_high) + (product(a_low, b_high) + product(a_high, b_low))


def to_spectrum(a_high, a_low, part, x):
    return dot(a_high[part], x) + dot(a_low[part], x)


def from_spectrum(t_high, re, im, length):
    total = dot(t_high[0], re.astype(bf16)) + dot(t_high[1], im.astype(bf16))
    return total * (1.0 / length)


def struct(shape, kind):
    return jax.ShapeDtypeStruct(shape, kind)


def whole(shape):
    return pl.BlockSpec(shape, lambda i, *_: (0,) * len(shape))


def table_specs(length, block):
    by_row = pl.BlockSpec((2, block, length), lambda i, *_: (0, i, 0))
    by_col = pl.BlockSpec((2, length, block), lambda i, *_: (0, 0, i))
    return by_row, by_col


def spectrum_block(width, block):
    return pl.BlockSpec((2, block, width), lambda i, *_: (0, i, 0))


def generate(place, table, factors, pos_weight, pos_bias, filter_weight, rates, norm, width, block):
    highest = lax.Precision.HIGHEST
    length, _ = table.shape
    order = pos_weight.shape[1]
    emb_count = pos_weight.shape[0]

    def body(
        place_ref, tab, ac, af, tc, tf, pw, pb, fw, rate, norm_ref,
        ah, al, th, spec, env_out, hidden_out, cos_out, filt,
    ):
        step = pl.program_id(0)

        @pl.when(step == 0)
        def _():
            pre = jnp.dot(tab[:, :emb_count], pw[...], precision=highest) + pb[...]
            hidden = jnp.sin(pre)
            hidden_out[...] = hidden
            cos_out[...] = jnp.cos(pre)
            at = lax.broadcasted_iota(jnp.int32, (length, width), 0).astype(f32)
            env = jnp.exp(-rate[...] * at) / norm_ref[...]
            env_out[...] = env
            filt[...] = (jnp.dot(hidden, fw[...], precision=highest) * env).astype(bf16)

        def rows(coarse, fine, store):
            def one(i, carry):
                here = pl.ds(step * (block // BASE) + i, 1)
                out = pl.ds(pl.multiple_of(i * BASE, BASE), BASE)
                cos, sin = coarse[0, here, :], coarse[1, here, :]
                store(out, 0, cos * fine[0] - sin * fine[1])
                store(out, 1, sin * fine[0] + cos * fine[1])
                return carry

            lax.fori_loop(0, block // BASE, one, 0)

        def store_both(out, part, value):
            high, low = split(value)
            ah[part, out, :] = high
            al[part, out, :] = low

        def store_high(out, part, value):
            th[part, out, :] = value.astype(bf16)

        rows(ac, af, store_both)
        rows(tc, tf, store_high)
        spec[0] = to_spectrum(ah, al, 0, filt[...])
        spec[1] = to_spectrum(ah, al, 1, filt[...])

    by_row = pl.BlockSpec((2, block, length), lambda i, *_: (0, i, 0))
    cols = lambda n: pl.BlockSpec((n, width), lambda i, place_ref: (0, place_ref[0]))
    return pl.pallas_call(
        body,
        grid_spec=pltpu.PrefetchScalarGridSpec(
            num_scalar_prefetch=1,
            grid=(length // block,),
            in_specs=[whole(table.shape)]
            + [whole(f.shape) for f in factors]
            + [whole(pos_weight.shape), whole(pos_bias.shape), cols(order), cols(1), cols(1)],
            out_specs=[by_row, by_row, by_row, spectrum_block(width, block)]
            + [whole((length, width)), whole((length, order)), whole((length, order))],
            scratch_shapes=[VMEM((length, width), bf16)],
        ),
        out_shape=[struct((2, length, length), bf16)] * 3
        + [struct((2, length, width), f32), struct((length, width), f32)]
        + [struct((length, order), f32)] * 2,
        name="generate",
    )(place, table, *factors, pos_weight, pos_bias, filter_weight, rates, norm)


def piece(place_ref, r, rows):
    return pl.ds(pl.multiple_of((place_ref[0] ^ r) * rows, rows), rows)


def convolve(place, signal_rel, cot_rel, filt_spec, tables, skip, block):
    a_high, a_low, t_high = tables
    count = len(signal_rel)
    local_len, width = cot_rel[0].shape
    length = local_len * count

    def body(place_ref, *refs):
        sig = refs[:count]
        cot = refs[count : 2 * count]
        fs, ah, al, th, skip_ref = refs[2 * count : 2 * count + 5]
        spec, inner_out, grad_out, x, acc = refs[2 * count + 5 :]
        step = pl.program_id(0)

        @pl.when(step == 0)
        def _():
            for r in range(count):
                x[piece(place_ref, r, local_len), :] = sig[r][...]

        re = to_spectrum(ah, al, 0, x[...])
        im = to_spectrum(ah, al, 1, x[...])
        spec[0] = re
        spec[1] = im
        part = from_spectrum(th, re * fs[0] - im * fs[1], re * fs[1] + im * fs[0], length)

        @pl.when(step == 0)
        def _():
            acc[...] = part

        @pl.when(step != 0)
        def _():
            acc[...] += part

        @pl.when(step == pl.num_programs(0) - 1)
        def _():
            conv = acc[...].astype(bf16).astype(f32)
            inner_out[...] = conv + skip_ref[...] * x[...].astype(f32)
            for r in range(count):
                rows = piece(place_ref, r, local_len)
                grad_out[rows, :] = (cot[r][...].astype(f32) * inner_out[rows, :]).astype(bf16)

    by_row, by_col = table_specs(length, block)
    cols = pl.BlockSpec((local_len, width), lambda i, place_ref: (0, place_ref[0]))
    return pl.pallas_call(
        body,
        grid_spec=pltpu.PrefetchScalarGridSpec(
            num_scalar_prefetch=1,
            grid=(length // block,),
            in_specs=[cols] * count
            + [whole((local_len, width))] * count
            + [spectrum_block(width, block), by_row, by_row, by_col]
            + [pl.BlockSpec((1, width), lambda i, place_ref: (0, place_ref[0]))],
            out_specs=[
                spectrum_block(width, block),
                whole((length, width)),
                whole((length, width)),
            ],
            scratch_shapes=[VMEM((length, width), bf16), VMEM((length, width), f32)],
        ),
        out_shape=[
            struct((2, length, width), f32),
            struct((length, width), f32),
            struct((length, width), bf16),
        ],
        name="convolve",
    )(place, *signal_rel, *cot_rel, filt_spec, a_high, a_low, t_high, skip)


def smem():
    return pl.BlockSpec(memory_space=pltpu.SMEM)


def weight_grads(place, signal_rel, gate_grad, groups):
    count = len(signal_rel)
    local_len, channels = signal_rel[0].shape
    width = gate_grad.shape[1]
    rows = channels // sum(len(group) for group in groups)

    def body(place_ref, *refs):
        sig = refs[:count]
        grad = refs[count]
        outs = refs[count + 1 :]
        right = jnp.concatenate(
            [grad[piece(place_ref, r, local_len), :] for r in range(count)], axis=0
        )
        for out, group in zip(outs, groups):
            for at, k in enumerate(group):
                start = pl.multiple_of((place_ref[1] ^ k) * rows, rows)
                left = jnp.concatenate(
                    [sig[r][:, pl.ds(start, rows)] for r in range(count)], axis=0
                )
                out[at] = dot_first(left, right).astype(bf16)

    return pl.pallas_call(
        body,
        in_specs=[smem()] + [pl.BlockSpec(memory_space=VMEM)] * (count + 1),
        out_specs=[pl.BlockSpec(memory_space=VMEM)] * len(groups),
        out_shape=[struct((len(group), rows, width), bf16) for group in groups],
        name="weight_grads",
    )(place, *signal_rel, gate_grad)


def gating(place, signal_rel, weight_rel, cot_rel, inner):
    count = len(signal_rel)
    dp_count = len(weight_rel)
    local_len, channels = signal_rel[0].shape
    rows, width = weight_rel[0].shape
    length = local_len * count

    def body(place_ref, *refs):
        sig = refs[:count]
        weight = refs[count : count + dp_count]
        cot = refs[count + dp_count : 2 * count + dp_count]
        inner_ref = refs[2 * count + dp_count]
        outs = refs[2 * count + dp_count + 1 : -1]
        full = refs[-1]
        inner_grad_out, conv_grad_out, skip_out = outs[count:]
        for k in range(dp_count):
            start = pl.multiple_of((place_ref[1] ^ k) * rows, rows)
            full[pl.ds(start, rows), :] = weight[k][...]
        left = jnp.concatenate([sig[r][...] for r in range(count)], axis=0)
        gates = dot(left, full[...])
        skip_sum = jnp.zeros((1, width), f32)
        own = pl.multiple_of(place_ref[0] * width, width)
        for r in range(count):
            here = piece(place_ref, r, local_len)
            gate = gates[r * local_len : (r + 1) * local_len]
            outs[r][...] = (gate * inner_ref[here, :]).astype(bf16)
            inner_grad = cot[r][...].astype(f32) * gate
            inner_grad_out[here, :] = inner_grad
            conv_grad_out[here, :] = inner_grad.astype(bf16)
            signal = sig[r][:, pl.ds(own, width)].astype(f32)
            skip_sum += jnp.sum(inner_grad * signal, axis=0, keepdims=True)
        skip_out[...] = jnp.broadcast_to(skip_sum, (8, width))

    return pl.pallas_call(
        body,
        in_specs=[smem()] + [pl.BlockSpec(memory_space=VMEM)] * (2 * count + dp_count + 1),
        out_specs=[pl.BlockSpec(memory_space=VMEM)] * (count + 3),
        out_shape=[struct((local_len, width), bf16)] * count
        + [
            struct((length, width), f32),
            struct((length, width), bf16),
            struct((8, width), f32),
        ],
        scratch_shapes=[VMEM((channels, width), bf16)],
        name="gating",
    )(place, *signal_rel, *weight_rel, *cot_rel, inner)


def packed_rows(order, table_rows, width):
    per_group = width // order
    groups = -(-(table_rows // 8) // per_group)
    return order + 8 + 8 * groups, per_group


def correlate_back(place, conv_grad, inner_grad, filt_spec, tables, skip, block):
    a_high, a_low, t_high = tables
    length, width = conv_grad.shape

    def body(place_ref, cg, ig, fs, ah, al, th, skip_ref, direct_out, spec, back):
        step = pl.program_id(0)
        re = to_spectrum(ah, al, 0, cg[...])
        im = to_spectrum(ah, al, 1, cg[...])
        spec[0] = re
        spec[1] = im
        term = from_spectrum(th, fs[0] * re + fs[1] * im, fs[0] * im - fs[1] * re, length)

        @pl.when(step == 0)
        def _():
            back[...] = term

        @pl.when(step != 0)
        def _():
            back[...] += term

        @pl.when(step == pl.num_programs(0) - 1)
        def _():
            direct_out[...] = ig[...] * skip_ref[...] + back[...].astype(bf16).astype(f32)

    by_row, by_col = table_specs(length, block)
    spec_block = spectrum_block(width, block)
    return pl.pallas_call(
        body,
        grid_spec=pltpu.PrefetchScalarGridSpec(
            num_scalar_prefetch=1,
            grid=(length // block,),
            in_specs=[
                whole((length, width)),
                whole((length, width)),
                spec_block,
                by_row,
                by_row,
                by_col,
                pl.BlockSpec((1, width), lambda i, place_ref: (0, place_ref[0])),
            ],
            out_specs=[whole((length, width)), spec_block],
            scratch_shapes=[VMEM((length, width), f32)],
        ),
        out_shape=[struct((length, width), f32), struct((2, length, width), f32)],
        name="correlate_back",
    )(place, conv_grad, inner_grad, filt_spec, a_high, a_low, t_high, skip)


def correlate_part(
    place, grad_spec, skip_sum, signal_spec, tables, env, hidden, filter_weight, cos_pre, table_t,
    block,
):
    t_high = tables[2]
    length, width = env.shape
    order = filter_weight.shape[0]
    table_rows = table_t.shape[0]
    total_rows, per_group = packed_rows(order, table_rows, width)

    def body(
        place_ref, gs, skip_sum_ref, ss, th, env_ref, hid, fw, cp, tab, packed, part,
    ):
        step = pl.program_id(0)
        term = from_spectrum(
            th, ss[0] * gs[0] + ss[1] * gs[1], ss[0] * gs[1] - ss[1] * gs[0], length
        )

        @pl.when(step == 0)
        def _():
            part[...] = term

        @pl.when(step != 0)
        def _():
            part[...] += term

        @pl.when(step == pl.num_programs(0) - 1)
        def _():
            pre_grad = part[...].astype(bf16).astype(f32) * env_ref[...]
            packed[...] = jnp.zeros((total_rows, width), f32)
            packed[:order, :] = careful(dot_first, hid[...], pre_grad)
            packed[order : order + 8, :] = skip_sum_ref[...]
            act = careful(dot_last, pre_grad, fw[...]) * cp[...]
            small = careful(dot, tab[...], act)
            for b in range(table_rows // 8):
                row = order + 8 + 8 * (b // per_group)
                col = order * (b % per_group)
                packed[row : row + 8, col : col + order] = small[8 * b : 8 * b + 8]

    _, by_col = table_specs(length, block)
    spec_block = spectrum_block(width, block)
    return pl.pallas_call(
        body,
        grid_spec=pltpu.PrefetchScalarGridSpec(
            num_scalar_prefetch=1,
            grid=(length // block,),
            in_specs=[
                spec_block,
                whole((8, width)),
                spec_block,
                by_col,
                whole((length, width)),
                whole(hidden.shape),
                pl.BlockSpec((order, width), lambda i, place_ref: (0, place_ref[0])),
                whole(cos_pre.shape),
                whole(table_t.shape),
            ],
            out_specs=whole((total_rows, width)),
            scratch_shapes=[VMEM((length, width), f32)],
        ),
        out_shape=struct((total_rows, width), f32),
        name="correlate_part",
    )(
        place, grad_spec, skip_sum, signal_spec, t_high, env, hidden, filter_weight, cos_pre,
        table_t,
    )


def through_gate(place, gate_grad, weight_rel, direct, count):
    dp_count = len(weight_rel)
    rows, width = weight_rel[0].shape
    length = gate_grad.shape[0]
    local_len = length // count
    channels = rows * dp_count

    def body(place_ref, *refs):
        grad = refs[0]
        weight = refs[1 : 1 + dp_count]
        direct_ref = refs[1 + dp_count]
        outs = refs[2 + dp_count :]
        left = jnp.concatenate(
            [grad[piece(place_ref, r, local_len), :] for r in range(count)], axis=0
        )
        for k in range(dp_count):
            start = pl.multiple_of((place_ref[1] ^ k) * rows, rows)
            shift = start - place_ref[0] * width
            inside = jnp.logical_and(shift >= 0, shift < width)
            shift = pl.multiple_of(jnp.clip(shift, 0, width - rows), rows)
            scale = jnp.where(inside, 1.0, 0.0).astype(f32)
            terms = dot_last(left, weight[k][...])
            for r in range(count):
                term = terms[r * local_len : (r + 1) * local_len]
                term += scale * direct_ref[piece(place_ref, r, local_len), pl.ds(shift, rows)]
                outs[r][:, pl.ds(start, rows)] = term.astype(bf16)

    return pl.pallas_call(
        body,
        in_specs=[smem()] + [pl.BlockSpec(memory_space=VMEM)] * (dp_count + 2),
        out_specs=[pl.BlockSpec(memory_space=VMEM)] * count,
        out_shape=[struct((local_len, channels), bf16)] * count,
        name="through_gate",
    )(place, gate_grad, *weight_rel, direct)


def assemble(place, pieces, kind):
    count = len(pieces)
    rows, width = pieces[0].shape

    def body(place_ref, *refs):
        out = refs[count]
        for r in range(count):
            start = pl.multiple_of((place_ref[0] ^ r) * width, width)
            out[:, pl.ds(start, width)] = refs[r][...].astype(kind)

    return pl.pallas_call(
        body,
        in_specs=[smem()] + [pl.BlockSpec(memory_space=VMEM)] * count,
        out_specs=pl.BlockSpec(memory_space=VMEM),
        out_shape=struct((rows, width * count), kind),
        name="assemble",
    )(place, *pieces)


def finish(place, pieces, order, emb_count):
    count = len(pieces)
    _, width = pieces[0].shape
    table_rows = -(-(emb_count + 1) // 8) * 8
    _, per_group = packed_rows(order, table_rows, width)

    def body(place_ref, *refs):
        filter_out, skip_out, pos_out, bias_out = refs[count:]
        for r in range(count):
            cols = pl.ds(pl.multiple_of((place_ref[0] ^ r) * width, width), width)
            values = refs[r][...].astype(f32)
            filter_out[:, cols] = values[:order, :]
            skip_out[:, cols] = values[order : order + 1, :]
        tails = [refs[r][...].astype(f32)[order + 8 :, :] for r in range(count)]
        while len(tails) > 1:
            tails = [tails[i] + tails[i + 1] for i in range(0, len(tails), 2)]
        for b in range(table_rows // 8):
            row = 8 * (b // per_group)
            col = order * (b % per_group)
            found = tails[0][row : row + 8, col : col + order]
            low = 8 * b
            high = min(low + 8, emb_count)
            if high > low:
                pos_out[low:high, :] = found[: high - low]
            if low <= emb_count < low + 8:
                bias_out[...] = found[emb_count - low : emb_count - low + 1]

    return pl.pallas_call(
        body,
        in_specs=[smem()] + [pl.BlockSpec(memory_space=VMEM)] * count,
        out_specs=[pl.BlockSpec(memory_space=VMEM)] * 4,
        out_shape=[
            struct((order, width * count), f32),
            struct((1, width * count), f32),
            struct((emb_count, order), f32),
            struct((1, order), f32),
        ],
        name="finish",
    )(place, *pieces)


def swap(value, axis, offset):
    count = lax.axis_size(axis)
    return lax.ppermute(value, axis, [(i, i ^ offset) for i in range(count)])


def gather_rel(own, axis):
    count = lax.axis_size(axis)
    found = {0: own}
    bit = count // 2
    while bit:
        for r in list(found):
            found[r | bit] = swap(found[r], axis, bit)
        bit //= 2
    return [found[r] for r in range(count)]


def add_round(*terms):
    total = terms[0].astype(f32)
    for term in terms[1:]:
        total = total + term.astype(f32)
    return total.astype(bf16)


def shards(
    signal, gate_weight, pos_weight, pos_bias, filter_weight, decay_rate, skip_gain, grad_out
):
    seq_count = lax.axis_size("seq")
    dp_count = lax.axis_size("dp")
    signal_tok = signal[0]
    cot_tok = grad_out[0]
    local_len, channels = signal_tok.shape
    length = local_len * seq_count
    width = channels // seq_count
    emb_count, order = pos_weight.shape
    seq_at = lax.axis_index("seq")
    dp_at = lax.axis_index("dp")
    place = jnp.stack([seq_at, dp_at]).astype(jnp.int32)
    block = min(256, length)

    def own_cols(x, r=0):
        return lax.dynamic_slice_in_dim(x, (seq_at ^ r) * width, width, axis=x.ndim - 1)

    signal_rel = gather_rel(signal_tok, "seq")
    weight_rel = {0: own_cols(gate_weight)}
    for k in range(2, dp_count, 2):
        weight_rel[k] = swap(weight_rel[0], "dp", k)
    for k in range(0, dp_count, 2):
        weight_rel[k + 1] = swap(weight_rel[k], "dp", 1)
    weight_rel = [weight_rel[k] for k in range(dp_count)]
    cot_rel = [own_cols(cot_tok)] + [
        swap(own_cols(cot_tok, r), "seq", r) for r in range(1, seq_count)
    ]

    table = feature_table(length, emb_count)
    rates = decay_rate[None]
    norm = jnp.sqrt(jnp.expm1(-2.0 * rates * length) / jnp.expm1(-2.0 * rates))
    skip = skip_gain[None]
    a_high, a_low, t_high, filt_spec, env, hidden, cos_pre = generate(
        place, jnp.asarray(table), [jnp.asarray(f) for f in angle_factors(length)],
        pos_weight, pos_bias[None], filter_weight, rates, norm, width, block,
    )
    tables = (a_high, a_low, t_high)

    signal_spec, inner, gate_grad = convolve(
        place, signal_rel, cot_rel, filt_spec, tables, skip, block
    )

    far = list(reversed(range(0, dp_count, 2)))
    pairs = [far[i : i + 2] for i in range(0, len(far), 2)]
    groups = [[k + 1 for k in pair] for pair in pairs] + pairs
    weight_parts = weight_grads(place, signal_rel, gate_grad, groups)
    sums = {}
    for i, pair in enumerate(pairs):
        met = swap(weight_parts[i], "dp", 1)
        for at, k in enumerate(pair):
            sums[k] = add_round(weight_parts[len(pairs) + i][at], met[at])
    row_sum = add_round(sums[0], *[swap(sums[k], "dp", k) for k in far[:-1]])
    row_rel = gather_rel(row_sum, "seq")
    grad_gate_weight = assemble(place, row_rel, f32)

    gated = gating(place, signal_rel, weight_rel, cot_rel, inner)
    out_rel = gated[:seq_count]
    inner_grad, conv_grad, skip_sum = gated[seq_count:]
    out_rel = [out_rel[0]] + [swap(out_rel[r], "seq", r) for r in range(1, seq_count)]
    output = assemble(place, out_rel, bf16)

    direct, grad_spec = correlate_back(place, conv_grad, inner_grad, filt_spec, tables, skip, block)
    packed = correlate_part(
        place, grad_spec, skip_sum, signal_spec, tables, env, hidden, filter_weight, cos_pre,
        jnp.asarray(table.T), block,
    )
    back_rel = through_gate(place, gate_grad, weight_rel, direct, seq_count)

    live = {r: back_rel[r] for r in range(seq_count)}
    bit = 1
    while bit < seq_count:
        met = {r: swap(live[r | bit], "seq", bit) for r in live if not r & bit}
        live = {r: add_round(live[r], met[r]) for r in met}
        bit *= 2
    grad_signal = live[0]

    packed = (packed + swap(packed, "dp", 1)).astype(bf16)
    terms = [packed] + [swap(packed, "dp", k) for k in range(2, dp_count, 2)]
    terms = [term.astype(f32) for term in terms]
    while len(terms) > 1:
        terms = [terms[i] + terms[i + 1] for i in range(0, len(terms), 2)]
    packed_rel = gather_rel(terms[0].astype(bf16), "seq")
    grad_filter_weight, grad_skip, grad_pos_weight, grad_pos_bias = finish(
        place, packed_rel, order, emb_count
    )
    return (
        output[None],
        grad_signal[None],
        grad_gate_weight,
        grad_pos_weight,
        grad_pos_bias[0],
        grad_filter_weight,
        grad_skip[0],
    )


def solution(mesh):
    step = mapped(shards, mesh)
    return step


def mapped(body, mesh):
    return jax.shard_map(
        body,
        mesh=mesh,
        in_specs=(
            P("dp", "seq", None),
            P("dp", None),
            P(),
            P(),
            P(),
            P(),
            P(),
            P("dp", "seq", None),
        ),
        out_specs=(P("dp", "seq", None), P("dp", "seq", None), P("dp", None), P(), P(), P(), P()),
        check_vma=False,
    )
```

```python
import functools
import math

import jax
import jax.numpy as jnp
import numpy as np
from jax import lax
from jax.experimental import pallas as pl
from jax.experimental.pallas import tpu as pltpu
from jax.sharding import PartitionSpec as P


f32 = jnp.float32
bf16 = jnp.bfloat16
VMEM = pltpu.VMEM


BASE = 16


@functools.lru_cache(maxsize=None)
def feature_table(length, emb_count):
    positions = np.arange(length)
    bands = np.arange(1, (emb_count - 1) // 2 + 1)
    angle = positions[:, None] * bands[None, :] % length * (2.0 * math.pi / length)
    table = np.concatenate(
        [positions[:, None] / length, np.cos(angle), np.sin(angle), np.ones((length, 1))], axis=1
    )
    rows = -(-table.shape[1] // 8) * 8
    return np.pad(table, ((0, 0), (0, rows - table.shape[1]))).astype(np.float32)


@functools.lru_cache(maxsize=None)
def angle_factors(length):
    step = 4 * length
    lane = np.arange(length)[None, :]
    coarse = np.arange(length // BASE)[:, None]
    fine = np.arange(BASE)[:, None]
    found = []
    for phase in (
        coarse * lane * (4 * BASE),
        (4 * fine + 1) * lane,
        coarse * BASE * (4 * lane + 1),
        fine * (4 * lane + 1),
    ):
        angle = phase % step * (2.0 * math.pi / step)
        found.append(np.stack([np.cos(angle), np.sin(angle)]).astype(np.float32))
    return found


def dot(a, b):
    return jnp.dot(a, b, preferred_element_type=f32)


def dot_first(a, b):
    return lax.dot_general(a, b, (((0,), (0,)), ((), ())), preferred_element_type=f32)


def dot_last(a, b):
    return lax.dot_general(a, b, (((1,), (1,)), ((), ())), preferred_element_type=f32)


def split(x):
    high = x.astype(bf16)
    return high, (x - high.astype(f32)).astype(bf16)


def careful(product, a, b):
    a_high, a_low = split(a)
    b_high, b_low = split(b)
    return product(a_high, b_high) + (product(a_low, b_high) + product(a_high, b_low))


def to_spectrum(a_high, a_low, part, x):
    return dot(a_high[part], x) + dot(a_low[part], x)


def from_spectrum(t_high, re, im, length):
    total = dot(t_high[0], re.astype(bf16)) + dot(t_high[1], im.astype(bf16))
    return total * (1.0 / length)


def struct(shape, kind):
    return jax.ShapeDtypeStruct(shape, kind)


def whole(shape):
    return pl.BlockSpec(shape, lambda i, *_: (0,) * len(shape))


def table_specs(length, block):
    by_row = pl.BlockSpec((2, block, length), lambda i, *_: (0, i, 0))
    by_col = pl.BlockSpec((2, length, block), lambda i, *_: (0, 0, i))
    return by_row, by_col


def spectrum_block(width, block):
    return pl.BlockSpec((2, block, width), lambda i, *_: (0, i, 0))


def generate(place, table, factors, pos_weight, pos_bias, filter_weight, rates, norm, width, block):
    highest = lax.Precision.HIGHEST
    length, _ = table.shape
    order = pos_weight.shape[1]
    emb_count = pos_weight.shape[0]

    def body(
        place_ref, tab, ac, af, tc, tf, pw, pb, fw, rate, norm_ref,
        ah, al, th, spec, env_out, hidden_out, cos_out, filt,
    ):
        step = pl.program_id(0)

        @pl.when(step == 0)
        def _():
            pre = jnp.dot(tab[:, :emb_count], pw[...], precision=highest) + pb[...]
            hidden = jnp.sin(pre)
            hidden_out[...] = hidden
            cos_out[...] = jnp.cos(pre)
            at = lax.broadcasted_iota(jnp.int32, (length, width), 0).astype(f32)
            env = jnp.exp(-rate[...] * at) / norm_ref[...]
            env_out[...] = env
            filt[...] = (jnp.dot(hidden, fw[...], precision=highest) * env).astype(bf16)

        def rows(coarse, fine, store):
            def one(i, carry):
                here = pl.ds(step * (block // BASE) + i, 1)
                out = pl.ds(pl.multiple_of(i * BASE, BASE), BASE)
                cos, sin = coarse[0, here, :], coarse[1, here, :]
                store(out, 0, cos * fine[0] - sin * fine[1])
                store(out, 1, sin * fine[0] + cos * fine[1])
                return carry

            lax.fori_loop(0, block // BASE, one, 0)

        def store_both(out, part, value):
            high, low = split(value)
            ah[part, out, :] = high
            al[part, out, :] = low

        def store_high(out, part, value):
            th[part, out, :] = value.astype(bf16)

        rows(ac, af, store_both)
        rows(tc, tf, store_high)
        spec[0] = to_spectrum(ah, al, 0, filt[...])
        spec[1] = to_spectrum(ah, al, 1, filt[...])

    by_row = pl.BlockSpec((2, block, length), lambda i, *_: (0, i, 0))
    cols = lambda n: pl.BlockSpec((n, width), lambda i, place_ref: (0, place_ref[0]))
    return pl.pallas_call(
        body,
        grid_spec=pltpu.PrefetchScalarGridSpec(
            num_scalar_prefetch=1,
            grid=(length // block,),
            in_specs=[whole(table.shape)]
            + [whole(f.shape) for f in factors]
            + [whole(pos_weight.shape), whole(pos_bias.shape), cols(order), cols(1), cols(1)],
            out_specs=[by_row, by_row, by_row, spectrum_block(width, block)]
            + [whole((length, width)), whole((length, order)), whole((length, order))],
            scratch_shapes=[VMEM((length, width), bf16)],
        ),
        out_shape=[struct((2, length, length), bf16)] * 3
        + [struct((2, length, width), f32), struct((length, width), f32)]
        + [struct((length, order), f32)] * 2,
        name="generate",
        compiler_params=grant(
            [((6, block, length), 2), ((4, block, width), 4), ((2, length, width), 4)], length, width
        ),
    )(place, table, *factors, pos_weight, pos_bias, filter_weight, rates, norm)


def piece(place_ref, r, rows):
    return pl.ds(pl.multiple_of((place_ref[0] ^ r) * rows, rows), rows)


def convolve(place, signal_rel, cot_rel, filt_spec, tables, skip, block):
    a_high, a_low, t_high = tables
    count = len(signal_rel)
    local_len, width = cot_rel[0].shape
    length = local_len * count

    def body(place_ref, *refs):
        sig = refs[:count]
        cot = refs[count : 2 * count]
        fs, ah, al, th, skip_ref = refs[2 * count : 2 * count + 5]
        spec, inner_out, grad_out, x, acc = refs[2 * count + 5 :]
        step = pl.program_id(0)

        @pl.when(step == 0)
        def _():
            for r in range(count):
                x[piece(place_ref, r, local_len), :] = sig[r][...]

        re = to_spectrum(ah, al, 0, x[...])
        im = to_spectrum(ah, al, 1, x[...])
        spec[0] = re
        spec[1] = im
        part = from_spectrum(th, re * fs[0] - im * fs[1], re * fs[1] + im * fs[0], length)

        @pl.when(step == 0)
        def _():
            acc[...] = part

        @pl.when(step != 0)
        def _():
            acc[...] += part

        @pl.when(step == pl.num_programs(0) - 1)
        def _():
            conv = acc[...].astype(bf16).astype(f32)
            inner_out[...] = conv + skip_ref[...] * x[...].astype(f32)
            for r in range(count):
                rows = piece(place_ref, r, local_len)
                grad_out[rows, :] = (cot[r][...].astype(f32) * inner_out[rows, :]).astype(bf16)

    by_row, by_col = table_specs(length, block)
    cols = pl.BlockSpec((local_len, width), lambda i, place_ref: (0, place_ref[0]))
    return pl.pallas_call(
        body,
        grid_spec=pltpu.PrefetchScalarGridSpec(
            num_scalar_prefetch=1,
            grid=(length // block,),
            in_specs=[cols] * count
            + [whole((local_len, width))] * count
            + [spectrum_block(width, block), by_row, by_row, by_col]
            + [pl.BlockSpec((1, width), lambda i, place_ref: (0, place_ref[0]))],
            out_specs=[
                spectrum_block(width, block),
                whole((length, width)),
                whole((length, width)),
            ],
            scratch_shapes=[VMEM((length, width), bf16), VMEM((length, width), f32)],
        ),
        out_shape=[
            struct((2, length, width), f32),
            struct((length, width), f32),
            struct((length, width), bf16),
        ],
        name="convolve",
        compiler_params=grant(
            [((6, block, length), 2), ((4, block, width), 4), ((3, length, width), 4)], length, width
        ),
    )(place, *signal_rel, *cot_rel, filt_spec, a_high, a_low, t_high, skip)


def grant(blocks, length, width):
    held = sum(math.prod(shape) * size for shape, size in blocks)
    need = 2 * held + 8 * length * width * 4 + (4 << 20)
    return pltpu.CompilerParams(vmem_limit_bytes=min(need, 60 << 20))


def smem():
    return pl.BlockSpec(memory_space=pltpu.SMEM)


def weight_grads(place, signal_rel, gate_grad, groups):
    count = len(signal_rel)
    local_len, channels = signal_rel[0].shape
    width = gate_grad.shape[1]
    rows = channels // sum(len(group) for group in groups)
    length = local_len * count

    def body(place_ref, *refs):
        sig = refs[:count]
        grad = refs[count]
        outs = refs[count + 1 :]
        right = jnp.concatenate(
            [grad[piece(place_ref, r, local_len), :] for r in range(count)], axis=0
        )
        for out, group in zip(outs, groups):
            for at, k in enumerate(group):
                start = pl.multiple_of((place_ref[1] ^ k) * rows, rows)
                left = jnp.concatenate(
                    [sig[r][:, pl.ds(start, rows)] for r in range(count)], axis=0
                )
                out[at] = dot_first(left, right).astype(bf16)

    return pl.pallas_call(
        body,
        in_specs=[smem()] + [pl.BlockSpec(memory_space=VMEM)] * (count + 1),
        out_specs=[pl.BlockSpec(memory_space=VMEM)] * len(groups),
        out_shape=[struct((len(group), rows, width), bf16) for group in groups],
        name="weight_grads",
        compiler_params=grant([((length, channels), 2), ((2, channels, width), 2)], length, width),
    )(place, *signal_rel, gate_grad)


def gating(place, signal_rel, weight_rel, cot_rel, inner):
    count = len(signal_rel)
    dp_count = len(weight_rel)
    local_len, channels = signal_rel[0].shape
    rows, width = weight_rel[0].shape
    length = local_len * count

    def body(place_ref, *refs):
        sig = refs[:count]
        weight = refs[count : count + dp_count]
        cot = refs[count + dp_count : 2 * count + dp_count]
        inner_ref = refs[2 * count + dp_count]
        outs = refs[2 * count + dp_count + 1 : -1]
        full = refs[-1]
        inner_grad_out, conv_grad_out, skip_out = outs[count:]
        for k in range(dp_count):
            start = pl.multiple_of((place_ref[1] ^ k) * rows, rows)
            full[pl.ds(start, rows), :] = weight[k][...]
        left = jnp.concatenate([sig[r][...] for r in range(count)], axis=0)
        gates = dot(left, full[...])
        skip_sum = jnp.zeros((1, width), f32)
        own = pl.multiple_of(place_ref[0] * width, width)
        for r in range(count):
            here = piece(place_ref, r, local_len)
            gate = gates[r * local_len : (r + 1) * local_len]
            outs[r][...] = (gate * inner_ref[here, :]).astype(bf16)
            inner_grad = cot[r][...].astype(f32) * gate
            inner_grad_out[here, :] = inner_grad
            conv_grad_out[here, :] = inner_grad.astype(bf16)
            signal = sig[r][:, pl.ds(own, width)].astype(f32)
            skip_sum += jnp.sum(inner_grad * signal, axis=0, keepdims=True)
        skip_out[...] = jnp.broadcast_to(skip_sum, (8, width))

    return pl.pallas_call(
        body,
        in_specs=[smem()] + [pl.BlockSpec(memory_space=VMEM)] * (2 * count + dp_count + 1),
        out_specs=[pl.BlockSpec(memory_space=VMEM)] * (count + 3),
        out_shape=[struct((local_len, width), bf16)] * count
        + [
            struct((length, width), f32),
            struct((length, width), bf16),
            struct((8, width), f32),
        ],
        scratch_shapes=[VMEM((channels, width), bf16)],
        name="gating",
        compiler_params=grant([((length, channels), 2), ((2, channels, width), 2)], length, width),
    )(place, *signal_rel, *weight_rel, *cot_rel, inner)


def packed_rows(order, table_rows, width):
    per_group = width // order
    groups = -(-(table_rows // 8) // per_group)
    return order + 8 + 8 * groups, per_group


def correlate_back(place, conv_grad, inner_grad, filt_spec, tables, skip, block):
    a_high, a_low, t_high = tables
    length, width = conv_grad.shape

    def body(place_ref, cg, ig, fs, ah, al, th, skip_ref, direct_out, spec, back):
        step = pl.program_id(0)
        re = to_spectrum(ah, al, 0, cg[...])
        im = to_spectrum(ah, al, 1, cg[...])
        spec[0] = re
        spec[1] = im
        term = from_spectrum(th, fs[0] * re + fs[1] * im, fs[0] * im - fs[1] * re, length)

        @pl.when(step == 0)
        def _():
            back[...] = term

        @pl.when(step != 0)
        def _():
            back[...] += term

        @pl.when(step == pl.num_programs(0) - 1)
        def _():
            direct_out[...] = ig[...] * skip_ref[...] + back[...].astype(bf16).astype(f32)

    by_row, by_col = table_specs(length, block)
    spec_block = spectrum_block(width, block)
    return pl.pallas_call(
        body,
        grid_spec=pltpu.PrefetchScalarGridSpec(
            num_scalar_prefetch=1,
            grid=(length // block,),
            in_specs=[
                whole((length, width)),
                whole((length, width)),
                spec_block,
                by_row,
                by_row,
                by_col,
                pl.BlockSpec((1, width), lambda i, place_ref: (0, place_ref[0])),
            ],
            out_specs=[whole((length, width)), spec_block],
            scratch_shapes=[VMEM((length, width), f32)],
        ),
        out_shape=[struct((length, width), f32), struct((2, length, width), f32)],
        name="correlate_back",
        compiler_params=grant(
            [((6, block, length), 2), ((4, block, width), 4), ((3, length, width), 4)], length, width
        ),
    )(place, conv_grad, inner_grad, filt_spec, a_high, a_low, t_high, skip)


def correlate_part(
    place, grad_spec, skip_sum, signal_spec, tables, env, hidden, filter_weight, cos_pre, table_t,
    block,
):
    t_high = tables[2]
    length, width = env.shape
    order = filter_weight.shape[0]
    table_rows = table_t.shape[0]
    total_rows, per_group = packed_rows(order, table_rows, width)

    def body(
        place_ref, gs, skip_sum_ref, ss, th, env_ref, hid, fw, cp, tab, packed, part,
    ):
        step = pl.program_id(0)
        term = from_spectrum(
            th, ss[0] * gs[0] + ss[1] * gs[1], ss[0] * gs[1] - ss[1] * gs[0], length
        )

        @pl.when(step == 0)
        def _():
            part[...] = term

        @pl.when(step != 0)
        def _():
            part[...] += term

        @pl.when(step == pl.num_programs(0) - 1)
        def _():
            pre_grad = part[...].astype(bf16).astype(f32) * env_ref[...]
            packed[...] = jnp.zeros((total_rows, width), f32)
            packed[:order, :] = careful(dot_first, hid[...], pre_grad)
            packed[order : order + 8, :] = skip_sum_ref[...]
            act = careful(dot_last, pre_grad, fw[...]) * cp[...]
            small = careful(dot, tab[...], act)
            for b in range(table_rows // 8):
                row = order + 8 + 8 * (b // per_group)
                col = order * (b % per_group)
                packed[row : row + 8, col : col + order] = small[8 * b : 8 * b + 8]

    _, by_col = table_specs(length, block)
    spec_block = spectrum_block(width, block)
    return pl.pallas_call(
        body,
        grid_spec=pltpu.PrefetchScalarGridSpec(
            num_scalar_prefetch=1,
            grid=(length // block,),
            in_specs=[
                spec_block,
                whole((8, width)),
                spec_block,
                by_col,
                whole((length, width)),
                whole(hidden.shape),
                pl.BlockSpec((order, width), lambda i, place_ref: (0, place_ref[0])),
                whole(cos_pre.shape),
                whole(table_t.shape),
            ],
            out_specs=whole((total_rows, width)),
            scratch_shapes=[VMEM((length, width), f32)],
        ),
        out_shape=struct((total_rows, width), f32),
        name="correlate_part",
        compiler_params=grant(
            [((2, block, length), 2), ((4, block, width), 4), ((2, length, width), 4)], length, width
        ),
    )(
        place, grad_spec, skip_sum, signal_spec, t_high, env, hidden, filter_weight, cos_pre,
        table_t,
    )


def through_gate(place, gate_grad, weight_rel, direct, count):
    dp_count = len(weight_rel)
    rows, width = weight_rel[0].shape
    length = gate_grad.shape[0]
    local_len = length // count
    channels = rows * dp_count

    def body(place_ref, *refs):
        grad = refs[0]
        weight = refs[1 : 1 + dp_count]
        direct_ref = refs[1 + dp_count]
        outs = refs[2 + dp_count :]
        left = jnp.concatenate(
            [grad[piece(place_ref, r, local_len), :] for r in range(count)], axis=0
        )
        for k in range(dp_count):
            start = pl.multiple_of((place_ref[1] ^ k) * rows, rows)
            shift = start - place_ref[0] * width
            inside = jnp.logical_and(shift >= 0, shift < width)
            shift = pl.multiple_of(jnp.clip(shift, 0, width - rows), rows)
            scale = jnp.where(inside, 1.0, 0.0).astype(f32)
            terms = dot_last(left, weight[k][...])
            for r in range(count):
                term = terms[r * local_len : (r + 1) * local_len]
                term += scale * direct_ref[piece(place_ref, r, local_len), pl.ds(shift, rows)]
                outs[r][:, pl.ds(start, rows)] = term.astype(bf16)

    return pl.pallas_call(
        body,
        in_specs=[smem()] + [pl.BlockSpec(memory_space=VMEM)] * (dp_count + 2),
        out_specs=[pl.BlockSpec(memory_space=VMEM)] * count,
        out_shape=[struct((local_len, channels), bf16)] * count,
        name="through_gate",
        compiler_params=grant([((length, channels), 2), ((channels, width), 2)], length, width),
    )(place, gate_grad, *weight_rel, direct)


def assemble(place, pieces, kind):
    count = len(pieces)
    rows, width = pieces[0].shape

    def body(place_ref, *refs):
        out = refs[count]
        for r in range(count):
            start = pl.multiple_of((place_ref[0] ^ r) * width, width)
            out[:, pl.ds(start, width)] = refs[r][...].astype(kind)

    return pl.pallas_call(
        body,
        in_specs=[smem()] + [pl.BlockSpec(memory_space=VMEM)] * count,
        out_specs=pl.BlockSpec(memory_space=VMEM),
        out_shape=struct((rows, width * count), kind),
        name="assemble",
        compiler_params=grant([((rows, 2 * width * count), 4)], rows, width),
    )(place, *pieces)


def finish(place, pieces, order, emb_count):
    count = len(pieces)
    rows, width = pieces[0].shape
    table_rows = -(-(emb_count + 1) // 8) * 8
    _, per_group = packed_rows(order, table_rows, width)

    def body(place_ref, *refs):
        filter_out, skip_out, pos_out, bias_out = refs[count:]
        for r in range(count):
            cols = pl.ds(pl.multiple_of((place_ref[0] ^ r) * width, width), width)
            values = refs[r][...].astype(f32)
            filter_out[:, cols] = values[:order, :]
            skip_out[:, cols] = values[order : order + 1, :]
        tails = [refs[r][...].astype(f32)[order + 8 :, :] for r in range(count)]
        while len(tails) > 1:
            tails = [tails[i] + tails[i + 1] for i in range(0, len(tails), 2)]
        for b in range(table_rows // 8):
            row = 8 * (b // per_group)
            col = order * (b % per_group)
            found = tails[0][row : row + 8, col : col + order]
            low = 8 * b
            high = min(low + 8, emb_count)
            if high > low:
                pos_out[low:high, :] = found[: high - low]
            if low <= emb_count < low + 8:
                bias_out[...] = found[emb_count - low : emb_count - low + 1]

    return pl.pallas_call(
        body,
        in_specs=[smem()] + [pl.BlockSpec(memory_space=VMEM)] * count,
        out_specs=[pl.BlockSpec(memory_space=VMEM)] * 4,
        out_shape=[
            struct((order, width * count), f32),
            struct((1, width * count), f32),
            struct((emb_count, order), f32),
            struct((1, order), f32),
        ],
        name="finish",
        compiler_params=grant([((rows, 2 * width * count), 4)], rows, width),
    )(place, *pieces)


def swap(value, axis, offset):
    count = lax.axis_size(axis)
    return lax.ppermute(value, axis, [(i, i ^ offset) for i in range(count)])


def gather_rel(own, axis):
    count = lax.axis_size(axis)
    found = {0: own}
    bit = count // 2
    while bit:
        for r in list(found):
            found[r | bit] = swap(found[r], axis, bit)
        bit //= 2
    return [found[r] for r in range(count)]


def add_round(*terms):
    total = terms[0].astype(f32)
    for term in terms[1:]:
        total = total + term.astype(f32)
    return total.astype(bf16)


def shards(
    signal, gate_weight, pos_weight, pos_bias, filter_weight, decay_rate, skip_gain, grad_out
):
    seq_count = lax.axis_size("seq")
    dp_count = lax.axis_size("dp")
    signal_tok = signal[0]
    cot_tok = grad_out[0]
    local_len, channels = signal_tok.shape
    length = local_len * seq_count
    width = channels // seq_count
    emb_count, order = pos_weight.shape
    seq_at = lax.axis_index("seq")
    dp_at = lax.axis_index("dp")
    place = jnp.stack([seq_at, dp_at]).astype(jnp.int32)
    block = min(256, length)

    def own_cols(x, r=0):
        return lax.dynamic_slice_in_dim(x, (seq_at ^ r) * width, width, axis=x.ndim - 1)

    signal_rel = gather_rel(signal_tok, "seq")
    weight_rel = {0: own_cols(gate_weight)}
    for k in range(2, dp_count, 2):
        weight_rel[k] = swap(weight_rel[0], "dp", k)
    for k in range(0, dp_count, 2):
        weight_rel[k + 1] = swap(weight_rel[k], "dp", 1)
    weight_rel = [weight_rel[k] for k in range(dp_count)]
    cot_rel = [own_cols(cot_tok)] + [
        swap(own_cols(cot_tok, r), "seq", r) for r in range(1, seq_count)
    ]

    table = feature_table(length, emb_count)
    rates = decay_rate[None]
    norm = jnp.sqrt(jnp.expm1(-2.0 * rates * length) / jnp.expm1(-2.0 * rates))
    skip = skip_gain[None]
    a_high, a_low, t_high, filt_spec, env, hidden, cos_pre = generate(
        place, jnp.asarray(table), [jnp.asarray(f) for f in angle_factors(length)],
        pos_weight, pos_bias[None], filter_weight, rates, norm, width, block,
    )
    tables = (a_high, a_low, t_high)

    signal_spec, inner, gate_grad = convolve(
        place, signal_rel, cot_rel, filt_spec, tables, skip, block
    )

    far = list(reversed(range(0, dp_count, 2)))
    pairs = [far[i : i + 2] for i in range(0, len(far), 2)]
    groups = [[k + 1 for k in pair] for pair in pairs] + pairs
    weight_parts = weight_grads(place, signal_rel, gate_grad, groups)
    sums = {}
    for i, pair in enumerate(pairs):
        met = swap(weight_parts[i], "dp", 1)
        for at, k in enumerate(pair):
            sums[k] = add_round(weight_parts[len(pairs) + i][at], met[at])
    row_sum = add_round(sums[0], *[swap(sums[k], "dp", k) for k in far[:-1]])
    row_rel = gather_rel(row_sum, "seq")
    grad_gate_weight = assemble(place, row_rel, f32)

    gated = gating(place, signal_rel, weight_rel, cot_rel, inner)
    out_rel = gated[:seq_count]
    inner_grad, conv_grad, skip_sum = gated[seq_count:]
    out_rel = [out_rel[0]] + [swap(out_rel[r], "seq", r) for r in range(1, seq_count)]
    output = assemble(place, out_rel, bf16)

    direct, grad_spec = correlate_back(place, conv_grad, inner_grad, filt_spec, tables, skip, block)
    packed = correlate_part(
        place, grad_spec, skip_sum, signal_spec, tables, env, hidden, filter_weight, cos_pre,
        jnp.asarray(table.T), block,
    )
    back_rel = through_gate(place, gate_grad, weight_rel, direct, seq_count)

    live = {r: back_rel[r] for r in range(seq_count)}
    bit = 1
    while bit < seq_count:
        met = {r: swap(live[r | bit], "seq", bit) for r in live if not r & bit}
        live = {r: add_round(live[r], met[r]) for r in met}
        bit *= 2
    grad_signal = live[0]

    packed = (packed + swap(packed, "dp", 1)).astype(bf16)
    terms = [packed] + [swap(packed, "dp", k) for k in range(2, dp_count, 2)]
    terms = [term.astype(f32) for term in terms]
    while len(terms) > 1:
        terms = [terms[i] + terms[i + 1] for i in range(0, len(terms), 2)]
    packed_rel = gather_rel(terms[0].astype(bf16), "seq")
    grad_filter_weight, grad_skip, grad_pos_weight, grad_pos_bias = finish(
        place, packed_rel, order, emb_count
    )
    return (
        output[None],
        grad_signal[None],
        grad_gate_weight,
        grad_pos_weight,
        grad_pos_bias[0],
        grad_filter_weight,
        grad_skip[0],
    )


def solution(mesh):
    step = mapped(shards, mesh)
    return step


def mapped(body, mesh):
    return jax.shard_map(
        body,
        mesh=mesh,
        in_specs=(
            P("dp", "seq", None),
            P("dp", None),
            P(),
            P(),
            P(),
            P(),
            P(),
            P("dp", "seq", None),
        ),
        out_specs=(P("dp", "seq", None), P("dp", "seq", None), P("dp", None), P(), P(), P(), P()),
        check_vma=False,
    )
```

```python
import functools
import math

import jax
import jax.numpy as jnp
import numpy as np
from jax import lax
from jax.experimental import pallas as pl
from jax.experimental.pallas import tpu as pltpu
from jax.sharding import PartitionSpec as P


f32 = jnp.float32
bf16 = jnp.bfloat16
VMEM = pltpu.VMEM


BASE = 16


@functools.lru_cache(maxsize=None)
def constants(length, emb_count):
    step = 4 * length
    lane = np.arange(length)[None, :]
    coarse = np.arange(length // BASE)[:, None]
    fine = np.arange(BASE)[:, None]
    found = []
    for phase in (
        coarse * lane * (4 * BASE),
        (4 * fine + 1) * lane,
        coarse * BASE * (4 * lane + 1),
        fine * (4 * lane + 1),
    ):
        angle = phase % step * (2.0 * math.pi / step)
        found += [np.cos(angle), np.sin(angle)]
    bands = np.arange(1, (emb_count - 1) // 2 + 1)[:, None]
    angle = bands * lane % length * (2.0 * math.pi / length)
    rows = 8 * (emb_count // 8 + 1)
    found += [lane / length, np.cos(angle), np.sin(angle), np.ones((1, length))]
    found += [np.zeros((rows - emb_count - 1, length))]
    return np.concatenate(found).astype(np.float32)


def constant_rows(length):
    sizes = [length // BASE, length // BASE, BASE, BASE]
    starts = np.cumsum([0] + sizes + sizes).tolist()
    return starts


def dot(a, b):
    return jnp.dot(a, b, preferred_element_type=f32)


def dot_first(a, b):
    return lax.dot_general(a, b, (((0,), (0,)), ((), ())), preferred_element_type=f32)


def dot_last(a, b):
    return lax.dot_general(a, b, (((1,), (1,)), ((), ())), preferred_element_type=f32)


def split(x):
    high = x.astype(bf16)
    return high, (x - high.astype(f32)).astype(bf16)


def careful(product, a, b):
    a_high, a_low = split(a)
    b_high, b_low = split(b)
    return product(a_high, b_high) + (product(a_low, b_high) + product(a_high, b_low))


def to_spectrum(a_high, a_low, part, x):
    return dot(a_high[part], x) + dot(a_low[part], x)


def from_spectrum(t_high, re, im, length):
    total = dot(t_high[0], re.astype(bf16)) + dot(t_high[1], im.astype(bf16))
    return total * (1.0 / length)


def struct(shape, kind):
    return jax.ShapeDtypeStruct(shape, kind)


def whole(shape):
    return pl.BlockSpec(shape, lambda i, *_: (0,) * len(shape))


def table_specs(length, block):
    by_row = pl.BlockSpec((2, block, length), lambda i, *_: (0, i, 0))
    by_col = pl.BlockSpec((2, length, block), lambda i, *_: (0, 0, i))
    return by_row, by_col


def spectrum_block(width, block):
    return pl.BlockSpec((2, block, width), lambda i, *_: (0, i, 0))


def generate(place, table, pos_weight, pos_bias, filter_weight, rows_of, width, block):
    highest = lax.Precision.HIGHEST
    length = table.shape[1]
    emb_count, order = pos_weight.shape
    starts = constant_rows(length)

    def body(
        place_ref, tab, pw, pb, fw, vec, ah, al, th, spec, env_out, hidden_out, cos_out, filt,
    ):
        step = pl.program_id(0)

        @pl.when(step == 0)
        def _():
            feat = tab[starts[8] : starts[8] + emb_count, :]
            pre = pb[...] + lax.dot_general(
                feat, pw[...], (((0,), (0,)), ((), ())), precision=highest,
                preferred_element_type=f32,
            )
            hidden = jnp.sin(pre)
            hidden_out[...] = hidden
            cos_out[...] = jnp.cos(pre)
            at = lax.broadcasted_iota(jnp.int32, (length, width), 0).astype(f32)
            env = jnp.exp(-vec[0:1, :] * at) / vec[1:2, :]
            env_out[...] = env
            filt[...] = (jnp.dot(hidden, fw[...], precision=highest) * env).astype(bf16)

        def rows(at, store):
            cos_start, sin_start, fine_cos, fine_sin = starts[at : at + 4]
            cos_fine = tab[fine_cos : fine_cos + BASE, :]
            sin_fine = tab[fine_sin : fine_sin + BASE, :]

            def one(i, carry):
                here = step * (block // BASE) + i
                out = pl.ds(pl.multiple_of(i * BASE, BASE), BASE)
                cos = tab[pl.ds(cos_start + here, 1), :]
                sin = tab[pl.ds(sin_start + here, 1), :]
                store(out, 0, cos * cos_fine - sin * sin_fine)
                store(out, 1, sin * cos_fine + cos * sin_fine)
                return carry

            lax.fori_loop(0, block // BASE, one, 0)

        def store_both(out, part, value):
            high, low = split(value)
            ah[part, out, :] = high
            al[part, out, :] = low

        def store_high(out, part, value):
            th[part, out, :] = value.astype(bf16)

        rows(0, store_both)
        rows(4, store_high)
        spec[0] = to_spectrum(ah, al, 0, filt[...])
        spec[1] = to_spectrum(ah, al, 1, filt[...])

    by_row = pl.BlockSpec((2, block, length), lambda i, *_: (0, i, 0))
    cols = lambda n: pl.BlockSpec((n, width), lambda i, place_ref: (0, place_ref[0]))
    return pl.pallas_call(
        body,
        grid_spec=pltpu.PrefetchScalarGridSpec(
            num_scalar_prefetch=1,
            grid=(length // block,),
            in_specs=[whole(table.shape), whole(pos_weight.shape), whole(pos_bias.shape)]
            + [cols(order), cols(rows_of.shape[0])],
            out_specs=[by_row, by_row, by_row, spectrum_block(width, block)]
            + [whole((length, width)), whole((length, order)), whole((length, order))],
            scratch_shapes=[VMEM((length, width), bf16)],
        ),
        out_shape=[struct((2, length, length), bf16)] * 3
        + [struct((2, length, width), f32), struct((length, width), f32)]
        + [struct((length, order), f32)] * 2,
        name="generate",
        compiler_params=grant(
            [((6, block, length), 2), ((4, block, width), 4), ((2, length, width), 4)]
            + [(table.shape, 4)], length, width
        ),
    )(place, table, pos_weight, pos_bias, filter_weight, rows_of)


def piece(place_ref, r, rows):
    return pl.ds(pl.multiple_of((place_ref[0] ^ r) * rows, rows), rows)


def convolve(place, signal_rel, cot_rel, filt_spec, tables, rows_of, block):
    a_high, a_low, t_high = tables
    count = len(signal_rel)
    local_len, width = cot_rel[0].shape
    length = local_len * count

    def body(place_ref, *refs):
        sig = refs[:count]
        cot = refs[count : 2 * count]
        fs, ah, al, th, skip_ref = refs[2 * count : 2 * count + 5]
        spec, inner_out, grad_out, x, acc = refs[2 * count + 5 :]
        step = pl.program_id(0)

        @pl.when(step == 0)
        def _():
            for r in range(count):
                x[piece(place_ref, r, local_len), :] = sig[r][...]

        re = to_spectrum(ah, al, 0, x[...])
        im = to_spectrum(ah, al, 1, x[...])
        spec[0] = re
        spec[1] = im
        part = from_spectrum(th, re * fs[0] - im * fs[1], re * fs[1] + im * fs[0], length)

        @pl.when(step == 0)
        def _():
            acc[...] = part

        @pl.when(step != 0)
        def _():
            acc[...] += part

        @pl.when(step == pl.num_programs(0) - 1)
        def _():
            conv = acc[...].astype(bf16).astype(f32)
            inner_out[...] = conv + skip_ref[2:3, :] * x[...].astype(f32)
            for r in range(count):
                rows = piece(place_ref, r, local_len)
                grad_out[rows, :] = (cot[r][...].astype(f32) * inner_out[rows, :]).astype(bf16)

    by_row, by_col = table_specs(length, block)
    cols = pl.BlockSpec((local_len, width), lambda i, place_ref: (0, place_ref[0]))
    return pl.pallas_call(
        body,
        grid_spec=pltpu.PrefetchScalarGridSpec(
            num_scalar_prefetch=1,
            grid=(length // block,),
            in_specs=[cols] * count
            + [whole((local_len, width))] * count
            + [spectrum_block(width, block), by_row, by_row, by_col]
            + [pl.BlockSpec((3, width), lambda i, place_ref: (0, place_ref[0]))],
            out_specs=[
                spectrum_block(width, block),
                whole((length, width)),
                whole((length, width)),
            ],
            scratch_shapes=[VMEM((length, width), bf16), VMEM((length, width), f32)],
        ),
        out_shape=[
            struct((2, length, width), f32),
            struct((length, width), f32),
            struct((length, width), bf16),
        ],
        name="convolve",
        compiler_params=grant(
            [((6, block, length), 2), ((4, block, width), 4), ((3, length, width), 4)], length, width
        ),
    )(place, *signal_rel, *cot_rel, filt_spec, a_high, a_low, t_high, rows_of)


def grant(blocks, length, width):
    held = sum(math.prod(shape) * size for shape, size in blocks)
    need = 2 * held + 8 * length * width * 4 + (4 << 20)
    return pltpu.CompilerParams(vmem_limit_bytes=min(need, 60 << 20))


def smem():
    return pl.BlockSpec(memory_space=pltpu.SMEM)


def weight_grads(place, signal_rel, gate_grad, groups):
    count = len(signal_rel)
    local_len, channels = signal_rel[0].shape
    width = gate_grad.shape[1]
    rows = channels // sum(len(group) for group in groups)
    length = local_len * count

    def body(place_ref, *refs):
        sig = refs[:count]
        grad = refs[count]
        outs = refs[count + 1 :]
        right = jnp.concatenate(
            [grad[piece(place_ref, r, local_len), :] for r in range(count)], axis=0
        )
        for out, group in zip(outs, groups):
            for at, k in enumerate(group):
                start = pl.multiple_of((place_ref[1] ^ k) * rows, rows)
                left = jnp.concatenate(
                    [sig[r][:, pl.ds(start, rows)] for r in range(count)], axis=0
                )
                out[at] = dot_first(left, right).astype(bf16)

    return pl.pallas_call(
        body,
        in_specs=[smem()] + [pl.BlockSpec(memory_space=VMEM)] * (count + 1),
        out_specs=[pl.BlockSpec(memory_space=VMEM)] * len(groups),
        out_shape=[struct((len(group), rows, width), bf16) for group in groups],
        name="weight_grads",
        compiler_params=grant([((length, channels), 2), ((2, channels, width), 2)], length, width),
    )(place, *signal_rel, gate_grad)


def gating(place, signal_rel, weight_rel, cot_rel, inner):
    count = len(signal_rel)
    dp_count = len(weight_rel)
    local_len, channels = signal_rel[0].shape
    rows, width = weight_rel[0].shape
    length = local_len * count

    def body(place_ref, *refs):
        sig = refs[:count]
        weight = refs[count : count + dp_count]
        cot = refs[count + dp_count : 2 * count + dp_count]
        inner_ref = refs[2 * count + dp_count]
        outs = refs[2 * count + dp_count + 1 : -1]
        full = refs[-1]
        inner_grad_out, conv_grad_out, skip_out = outs[count:]
        for k in range(dp_count):
            start = pl.multiple_of((place_ref[1] ^ k) * rows, rows)
            full[pl.ds(start, rows), :] = weight[k][...]
        left = jnp.concatenate([sig[r][...] for r in range(count)], axis=0)
        gates = dot(left, full[...])
        skip_sum = jnp.zeros((1, width), f32)
        own = pl.multiple_of(place_ref[0] * width, width)
        for r in range(count):
            here = piece(place_ref, r, local_len)
            gate = gates[r * local_len : (r + 1) * local_len]
            outs[r][...] = (gate * inner_ref[here, :]).astype(bf16)
            inner_grad = cot[r][...].astype(f32) * gate
            inner_grad_out[here, :] = inner_grad
            conv_grad_out[here, :] = inner_grad.astype(bf16)
            signal = sig[r][:, pl.ds(own, width)].astype(f32)
            skip_sum += jnp.sum(inner_grad * signal, axis=0, keepdims=True)
        skip_out[...] = jnp.broadcast_to(skip_sum, (8, width))

    return pl.pallas_call(
        body,
        in_specs=[smem()] + [pl.BlockSpec(memory_space=VMEM)] * (2 * count + dp_count + 1),
        out_specs=[pl.BlockSpec(memory_space=VMEM)] * (count + 3),
        out_shape=[struct((local_len, width), bf16)] * count
        + [
            struct((length, width), f32),
            struct((length, width), bf16),
            struct((8, width), f32),
        ],
        scratch_shapes=[VMEM((channels, width), bf16)],
        name="gating",
        compiler_params=grant([((length, channels), 2), ((2, channels, width), 2)], length, width),
    )(place, *signal_rel, *weight_rel, *cot_rel, inner)


def packed_rows(order, table_rows, width):
    per_group = width // order
    groups = -(-(table_rows // 8) // per_group)
    return order + 8 + 8 * groups, per_group


def correlate_back(place, conv_grad, inner_grad, filt_spec, tables, rows_of, block):
    a_high, a_low, t_high = tables
    length, width = conv_grad.shape

    def body(place_ref, cg, ig, fs, ah, al, th, skip_ref, direct_out, spec, back):
        step = pl.program_id(0)
        re = to_spectrum(ah, al, 0, cg[...])
        im = to_spectrum(ah, al, 1, cg[...])
        spec[0] = re
        spec[1] = im
        term = from_spectrum(th, fs[0] * re + fs[1] * im, fs[0] * im - fs[1] * re, length)

        @pl.when(step == 0)
        def _():
            back[...] = term

        @pl.when(step != 0)
        def _():
            back[...] += term

        @pl.when(step == pl.num_programs(0) - 1)
        def _():
            direct_out[...] = ig[...] * skip_ref[2:3, :] + back[...].astype(bf16).astype(f32)

    by_row, by_col = table_specs(length, block)
    spec_block = spectrum_block(width, block)
    return pl.pallas_call(
        body,
        grid_spec=pltpu.PrefetchScalarGridSpec(
            num_scalar_prefetch=1,
            grid=(length // block,),
            in_specs=[
                whole((length, width)),
                whole((length, width)),
                spec_block,
                by_row,
                by_row,
                by_col,
                pl.BlockSpec((3, width), lambda i, place_ref: (0, place_ref[0])),
            ],
            out_specs=[whole((length, width)), spec_block],
            scratch_shapes=[VMEM((length, width), f32)],
        ),
        out_shape=[struct((length, width), f32), struct((2, length, width), f32)],
        name="correlate_back",
        compiler_params=grant(
            [((6, block, length), 2), ((4, block, width), 4), ((3, length, width), 4)], length, width
        ),
    )(place, conv_grad, inner_grad, filt_spec, a_high, a_low, t_high, rows_of)


def correlate_part(
    place, grad_spec, skip_sum, signal_spec, tables, env, hidden, filter_weight, cos_pre, table,
    block,
):
    t_high = tables[2]
    length, width = env.shape
    order = filter_weight.shape[0]
    feature_start = constant_rows(length)[8]
    table_rows = table.shape[0] - feature_start
    total_rows, per_group = packed_rows(order, table_rows, width)

    def body(
        place_ref, gs, skip_sum_ref, ss, th, env_ref, hid, fw, cp, tab, packed, part,
    ):
        step = pl.program_id(0)
        term = from_spectrum(
            th, ss[0] * gs[0] + ss[1] * gs[1], ss[0] * gs[1] - ss[1] * gs[0], length
        )

        @pl.when(step == 0)
        def _():
            part[...] = term

        @pl.when(step != 0)
        def _():
            part[...] += term

        @pl.when(step == pl.num_programs(0) - 1)
        def _():
            pre_grad = part[...].astype(bf16).astype(f32) * env_ref[...]
            packed[...] = jnp.zeros((total_rows, width), f32)
            packed[:order, :] = careful(dot_first, hid[...], pre_grad)
            packed[order : order + 8, :] = skip_sum_ref[...]
            act = careful(dot_last, pre_grad, fw[...]) * cp[...]
            small = careful(dot, tab[feature_start:, :], act)
            for b in range(table_rows // 8):
                row = order + 8 + 8 * (b // per_group)
                col = order * (b % per_group)
                packed[row : row + 8, col : col + order] = small[8 * b : 8 * b + 8]

    _, by_col = table_specs(length, block)
    spec_block = spectrum_block(width, block)
    return pl.pallas_call(
        body,
        grid_spec=pltpu.PrefetchScalarGridSpec(
            num_scalar_prefetch=1,
            grid=(length // block,),
            in_specs=[
                spec_block,
                whole((8, width)),
                spec_block,
                by_col,
                whole((length, width)),
                whole(hidden.shape),
                pl.BlockSpec((order, width), lambda i, place_ref: (0, place_ref[0])),
                whole(cos_pre.shape),
                whole(table.shape),
            ],
            out_specs=whole((total_rows, width)),
            scratch_shapes=[VMEM((length, width), f32)],
        ),
        out_shape=struct((total_rows, width), f32),
        name="correlate_part",
        compiler_params=grant(
            [((2, block, length), 2), ((4, block, width), 4), ((2, length, width), 4)], length, width
        ),
    )(
        place, grad_spec, skip_sum, signal_spec, t_high, env, hidden, filter_weight, cos_pre,
        table,
    )


def through_gate(place, gate_grad, weight_rel, direct, count):
    dp_count = len(weight_rel)
    rows, width = weight_rel[0].shape
    length = gate_grad.shape[0]
    local_len = length // count
    channels = rows * dp_count

    def body(place_ref, *refs):
        grad = refs[0]
        weight = refs[1 : 1 + dp_count]
        direct_ref = refs[1 + dp_count]
        outs = refs[2 + dp_count :]
        left = jnp.concatenate(
            [grad[piece(place_ref, r, local_len), :] for r in range(count)], axis=0
        )
        for k in range(dp_count):
            start = pl.multiple_of((place_ref[1] ^ k) * rows, rows)
            shift = start - place_ref[0] * width
            inside = jnp.logical_and(shift >= 0, shift < width)
            shift = pl.multiple_of(jnp.clip(shift, 0, width - rows), rows)
            scale = jnp.where(inside, 1.0, 0.0).astype(f32)
            terms = dot_last(left, weight[k][...])
            for r in range(count):
                term = terms[r * local_len : (r + 1) * local_len]
                term += scale * direct_ref[piece(place_ref, r, local_len), pl.ds(shift, rows)]
                outs[r][:, pl.ds(start, rows)] = term.astype(bf16)

    return pl.pallas_call(
        body,
        in_specs=[smem()] + [pl.BlockSpec(memory_space=VMEM)] * (dp_count + 2),
        out_specs=[pl.BlockSpec(memory_space=VMEM)] * count,
        out_shape=[struct((local_len, channels), bf16)] * count,
        name="through_gate",
        compiler_params=grant([((length, channels), 2), ((channels, width), 2)], length, width),
    )(place, gate_grad, *weight_rel, direct)


def assemble(place, pieces, kind):
    count = len(pieces)
    rows, width = pieces[0].shape

    def body(place_ref, *refs):
        out = refs[count]
        for r in range(count):
            start = pl.multiple_of((place_ref[0] ^ r) * width, width)
            out[:, pl.ds(start, width)] = refs[r][...].astype(kind)

    return pl.pallas_call(
        body,
        in_specs=[smem()] + [pl.BlockSpec(memory_space=VMEM)] * count,
        out_specs=pl.BlockSpec(memory_space=VMEM),
        out_shape=struct((rows, width * count), kind),
        name="assemble",
        compiler_params=grant([((rows, 2 * width * count), 4)], rows, width),
    )(place, *pieces)


def finish(place, pieces, order, emb_count):
    count = len(pieces)
    rows, width = pieces[0].shape
    table_rows = 8 * (emb_count // 8 + 1)
    _, per_group = packed_rows(order, table_rows, width)

    def body(place_ref, *refs):
        filter_out, skip_out, pos_out, bias_out = refs[count:]
        for r in range(count):
            cols = pl.ds(pl.multiple_of((place_ref[0] ^ r) * width, width), width)
            values = refs[r][...].astype(f32)
            filter_out[:, cols] = values[:order, :]
            skip_out[:, cols] = values[order : order + 1, :]
        tails = [refs[r][...].astype(f32)[order + 8 :, :] for r in range(count)]
        while len(tails) > 1:
            tails = [tails[i] + tails[i + 1] for i in range(0, len(tails), 2)]
        for b in range(table_rows // 8):
            row = 8 * (b // per_group)
            col = order * (b % per_group)
            found = tails[0][row : row + 8, col : col + order]
            low = 8 * b
            high = min(low + 8, emb_count)
            if high > low:
                pos_out[low:high, :] = found[: high - low]
            if low <= emb_count < low + 8:
                bias_out[...] = found[emb_count - low : emb_count - low + 1]

    return pl.pallas_call(
        body,
        in_specs=[smem()] + [pl.BlockSpec(memory_space=VMEM)] * count,
        out_specs=[pl.BlockSpec(memory_space=VMEM)] * 4,
        out_shape=[
            struct((order, width * count), f32),
            struct((1, width * count), f32),
            struct((emb_count, order), f32),
            struct((1, order), f32),
        ],
        name="finish",
        compiler_params=grant([((rows, 2 * width * count), 4)], rows, width),
    )(place, *pieces)


def swap(value, axis, offset):
    count = lax.axis_size(axis)
    return lax.ppermute(value, axis, [(i, i ^ offset) for i in range(count)])


def gather_rel(own, axis):
    count = lax.axis_size(axis)
    found = {0: own}
    bit = count // 2
    while bit:
        for r in list(found):
            found[r | bit] = swap(found[r], axis, bit)
        bit //= 2
    return [found[r] for r in range(count)]


def add_round(*terms):
    total = terms[0].astype(f32)
    for term in terms[1:]:
        total = total + term.astype(f32)
    return total.astype(bf16)


def shards(
    signal, gate_weight, pos_weight, pos_bias, filter_weight, decay_rate, skip_gain, grad_out
):
    seq_count = lax.axis_size("seq")
    dp_count = lax.axis_size("dp")
    signal_tok = signal[0]
    cot_tok = grad_out[0]
    local_len, channels = signal_tok.shape
    length = local_len * seq_count
    width = channels // seq_count
    emb_count, order = pos_weight.shape
    seq_at = lax.axis_index("seq")
    dp_at = lax.axis_index("dp")
    place = jnp.stack([seq_at, dp_at]).astype(jnp.int32)
    block = min(256, length)

    def own_cols(x, r=0):
        return lax.dynamic_slice_in_dim(x, (seq_at ^ r) * width, width, axis=x.ndim - 1)

    signal_rel = gather_rel(signal_tok, "seq")
    weight_rel = {0: own_cols(gate_weight)}
    for k in range(2, dp_count, 2):
        weight_rel[k] = swap(weight_rel[0], "dp", k)
    for k in range(0, dp_count, 2):
        weight_rel[k + 1] = swap(weight_rel[k], "dp", 1)
    weight_rel = [weight_rel[k] for k in range(dp_count)]
    cot_rel = [own_cols(cot_tok)] + [
        swap(own_cols(cot_tok, r), "seq", r) for r in range(1, seq_count)
    ]

    table = jnp.asarray(constants(length, emb_count))
    rates = decay_rate[None]
    norm = jnp.sqrt(jnp.expm1(-2.0 * rates * length) / jnp.expm1(-2.0 * rates))
    rows_of = jnp.concatenate([rates, norm, skip_gain[None]])
    a_high, a_low, t_high, filt_spec, env, hidden, cos_pre = generate(
        place, table, pos_weight, pos_bias[None], filter_weight, rows_of, width, block
    )
    tables = (a_high, a_low, t_high)

    signal_spec, inner, gate_grad = convolve(
        place, signal_rel, cot_rel, filt_spec, tables, rows_of, block
    )

    far = list(reversed(range(0, dp_count, 2)))
    pairs = stages(dp_count)
    groups = [[k + 1 for k in pair] for pair in pairs] + pairs
    weight_parts = weight_grads(place, signal_rel, gate_grad, groups)
    sums = {}
    for i, pair in enumerate(pairs):
        met = swap(weight_parts[i], "dp", 1)
        for at, k in enumerate(pair):
            sums[k] = add_round(weight_parts[len(pairs) + i][at], met[at])
    row_sum = add_round(sums[0], *[swap(sums[k], "dp", k) for k in far[:-1]])
    row_rel = gather_rel(row_sum, "seq")
    grad_gate_weight = assemble(place, row_rel, f32)

    gated = gating(place, signal_rel, weight_rel, cot_rel, inner)
    out_rel = gated[:seq_count]
    inner_grad, conv_grad, skip_sum = gated[seq_count:]
    out_rel = [out_rel[0]] + [swap(out_rel[r], "seq", r) for r in range(1, seq_count)]
    output = assemble(place, out_rel, bf16)

    direct, grad_spec = correlate_back(
        place, conv_grad, inner_grad, filt_spec, tables, rows_of, block
    )
    packed = correlate_part(
        place, grad_spec, skip_sum, signal_spec, tables, env, hidden, filter_weight, cos_pre,
        table, block,
    )
    back_rel = through_gate(place, gate_grad, weight_rel, direct, seq_count)

    live = {r: back_rel[r] for r in range(seq_count)}
    bit = 1
    while bit < seq_count:
        met = {r: swap(live[r | bit], "seq", bit) for r in live if not r & bit}
        live = {r: add_round(live[r], met[r]) for r in met}
        bit *= 2
    grad_signal = live[0]

    met = swap(packed, "dp", 1)
    packed = (packed + met).astype(bf16)
    terms = [packed] + [swap(packed, "dp", k) for k in range(2, dp_count, 2)]
    terms = [term.astype(f32) for term in terms]
    while len(terms) > 1:
        terms = [terms[i] + terms[i + 1] for i in range(0, len(terms), 2)]
    packed_rel = gather_rel(terms[0].astype(bf16), "seq")
    grad_filter_weight, grad_skip, grad_pos_weight, grad_pos_bias = finish(
        place, packed_rel, order, emb_count
    )
    return (
        output[None],
        grad_signal[None],
        grad_gate_weight,
        grad_pos_weight,
        grad_pos_bias[0],
        grad_filter_weight,
        grad_skip[0],
    )


def stages(dp_count):
    far = list(reversed(range(0, dp_count, 2)))
    return [[k] for k in far[:-2]] + [far[-2:]]


def solution(mesh):
    step = mapped(shards, mesh)
    return step


def mapped(body, mesh):
    return jax.shard_map(
        body,
        mesh=mesh,
        in_specs=(
            P("dp", "seq", None),
            P("dp", None),
            P(),
            P(),
            P(),
            P(),
            P(),
            P("dp", "seq", None),
        ),
        out_specs=(P("dp", "seq", None), P("dp", "seq", None), P("dp", None), P(), P(), P(), P()),
        check_vma=False,
    )
```

```python
import functools
import math

import jax
import jax.numpy as jnp
import numpy as np
from jax import lax
from jax.experimental import pallas as pl
from jax.experimental.pallas import tpu as pltpu
from jax.sharding import PartitionSpec as P


f32 = jnp.float32
bf16 = jnp.bfloat16
VMEM = pltpu.VMEM


BASE = 16


@functools.lru_cache(maxsize=None)
def constants(length, emb_count):
    step = 4 * length
    lane = np.arange(length)[None, :]
    coarse = np.arange(length // BASE)[:, None]
    fine = np.arange(BASE)[:, None]
    found = []
    for phase in (
        coarse * lane * (4 * BASE),
        (4 * fine + 1) * lane,
        coarse * BASE * (4 * lane + 1),
        fine * (4 * lane + 1),
    ):
        angle = phase % step * (2.0 * math.pi / step)
        found += [np.cos(angle), np.sin(angle)]
    bands = np.arange(1, (emb_count - 1) // 2 + 1)[:, None]
    angle = bands * lane % length * (2.0 * math.pi / length)
    rows = 8 * (emb_count // 8 + 1)
    found += [lane / length, np.cos(angle), np.sin(angle), np.ones((1, length))]
    found += [np.zeros((rows - emb_count - 1, length))]
    return np.concatenate(found).astype(np.float32)


def constant_rows(length):
    sizes = [length // BASE, length // BASE, BASE, BASE]
    starts = np.cumsum([0] + sizes + sizes).tolist()
    return starts


def dot(a, b):
    return jnp.dot(a, b, preferred_element_type=f32)


def dot_first(a, b):
    return lax.dot_general(a, b, (((0,), (0,)), ((), ())), preferred_element_type=f32)


def dot_last(a, b):
    return lax.dot_general(a, b, (((1,), (1,)), ((), ())), preferred_element_type=f32)


def split(x):
    high = x.astype(bf16)
    return high, (x - high.astype(f32)).astype(bf16)


def careful(product, a, b):
    a_high, a_low = split(a)
    b_high, b_low = split(b)
    return product(a_high, b_high) + (product(a_low, b_high) + product(a_high, b_low))


def to_spectrum(a_high, a_low, part, x):
    return dot(a_high[part], x) + dot(a_low[part], x)


def from_spectrum(t_high, re, im, length):
    total = dot(t_high[0], re.astype(bf16)) + dot(t_high[1], im.astype(bf16))
    return total * (1.0 / length)


def struct(shape, kind):
    return jax.ShapeDtypeStruct(shape, kind)


def whole(shape):
    return pl.BlockSpec(shape, lambda i, *_: (0,) * len(shape))


def table_specs(length, block):
    by_row = pl.BlockSpec((2, block, length), lambda i, *_: (0, i, 0))
    by_col = pl.BlockSpec((2, length, block), lambda i, *_: (0, 0, i))
    return by_row, by_col


def spectrum_block(width, block):
    return pl.BlockSpec((2, block, width), lambda i, *_: (0, i, 0))


def generate(place, table, pos_weight, pos_bias, filter_weight, rows_of, width, block):
    highest = lax.Precision.HIGHEST
    length = table.shape[1]
    emb_count, order = pos_weight.shape
    starts = constant_rows(length)

    def body(place_ref, *refs):
        sources = refs[:5]
        ah, al, th, spec, env_out, hidden_out, cos_out, rows_out, filt, *held, done = refs[5:]
        tab, pw, pb, fw, vec = held
        step = pl.program_id(0)

        @pl.when(step == 0)
        def _():
            mine = pl.ds(pl.multiple_of(place_ref[0] * width, width), width)
            copies = [
                pltpu.make_async_copy(
                    source if i < 3 else source.at[:, mine], target, done.at[i]
                )
                for i, (source, target) in enumerate(zip(sources, held))
            ]
            for copy in copies:
                copy.start()
            for copy in copies:
                copy.wait()
            rows_out[...] = vec[...]
            feat = tab[starts[8] : starts[8] + emb_count, :]
            pre = pb[...] + lax.dot_general(
                feat, pw[...], (((0,), (0,)), ((), ())), precision=highest,
                preferred_element_type=f32,
            )
            hidden = jnp.sin(pre)
            hidden_out[...] = hidden
            cos_out[...] = jnp.cos(pre)
            at = lax.broadcasted_iota(jnp.int32, (length, width), 0).astype(f32)
            env = jnp.exp(-vec[0:1, :] * at) / vec[1:2, :]
            env_out[...] = env
            filt[...] = (jnp.dot(hidden, fw[...], precision=highest) * env).astype(bf16)

        def rows(at, store):
            cos_start, sin_start, fine_cos, fine_sin = starts[at : at + 4]
            cos_fine = tab[fine_cos : fine_cos + BASE, :]
            sin_fine = tab[fine_sin : fine_sin + BASE, :]

            def one(i, carry):
                here = step * (block // BASE) + i
                out = pl.ds(pl.multiple_of(i * BASE, BASE), BASE)
                cos = tab[pl.ds(cos_start + here, 1), :]
                sin = tab[pl.ds(sin_start + here, 1), :]
                store(out, 0, cos * cos_fine - sin * sin_fine)
                store(out, 1, sin * cos_fine + cos * sin_fine)
                return carry

            lax.fori_loop(0, block // BASE, one, 0)

        def store_both(out, part, value):
            high, low = split(value)
            ah[part, out, :] = high
            al[part, out, :] = low

        def store_high(out, part, value):
            th[part, out, :] = value.astype(bf16)

        rows(0, store_both)
        rows(4, store_high)
        spec[0] = to_spectrum(ah, al, 0, filt[...])
        spec[1] = to_spectrum(ah, al, 1, filt[...])

    by_row = pl.BlockSpec((2, block, length), lambda i, *_: (0, i, 0))
    return pl.pallas_call(
        body,
        grid_spec=pltpu.PrefetchScalarGridSpec(
            num_scalar_prefetch=1,
            grid=(length // block,),
            in_specs=[pl.BlockSpec(memory_space=pltpu.HBM)] * 5,
            out_specs=[by_row, by_row, by_row, spectrum_block(width, block)]
            + [whole((length, width)), whole((length, order)), whole((length, order))]
            + [whole((rows_of.shape[0], width))],
            scratch_shapes=[VMEM((length, width), bf16)]
            + [VMEM(x.shape, f32) for x in (table, pos_weight, pos_bias)]
            + [VMEM((order, width), f32), VMEM((rows_of.shape[0], width), f32)]
            + [pltpu.SemaphoreType.DMA((5,))],
        ),
        out_shape=[struct((2, length, length), bf16)] * 3
        + [struct((2, length, width), f32), struct((length, width), f32)]
        + [struct((length, order), f32)] * 2
        + [struct((rows_of.shape[0], width), f32)],
        name="generate",
        compiler_params=grant(
            [((6, block, length), 2), ((4, block, width), 4), ((2, length, width), 4)]
            + [(table.shape, 4)], length, width
        ),
    )(
        place,
        *[
            pltpu.with_memory_space_constraint(x, pltpu.HBM)
            for x in (table, pos_weight, pos_bias, filter_weight, rows_of)
        ],
    )


def piece(place_ref, r, rows):
    return pl.ds(pl.multiple_of((place_ref[0] ^ r) * rows, rows), rows)


def convolve(place, signal_rel, cot_rel, filt_spec, tables, rows_of, block):
    a_high, a_low, t_high = tables
    count = len(signal_rel)
    local_len, width = cot_rel[0].shape
    length = local_len * count

    def body(place_ref, *refs):
        sig = refs[:count]
        cot = refs[count : 2 * count]
        fs, ah, al, th, skip_ref = refs[2 * count : 2 * count + 5]
        spec, inner_out, grad_out, x, acc = refs[2 * count + 5 :]
        step = pl.program_id(0)

        @pl.when(step == 0)
        def _():
            for r in range(count):
                x[piece(place_ref, r, local_len), :] = sig[r][...]

        re = to_spectrum(ah, al, 0, x[...])
        im = to_spectrum(ah, al, 1, x[...])
        spec[0] = re
        spec[1] = im
        part = from_spectrum(th, re * fs[0] - im * fs[1], re * fs[1] + im * fs[0], length)

        @pl.when(step == 0)
        def _():
            acc[...] = part

        @pl.when(step != 0)
        def _():
            acc[...] += part

        @pl.when(step == pl.num_programs(0) - 1)
        def _():
            conv = acc[...].astype(bf16).astype(f32)
            inner_out[...] = conv + skip_ref[2:3, :] * x[...].astype(f32)
            for r in range(count):
                rows = piece(place_ref, r, local_len)
                grad_out[rows, :] = (cot[r][...].astype(f32) * inner_out[rows, :]).astype(bf16)

    by_row, by_col = table_specs(length, block)
    cols = pl.BlockSpec((local_len, width), lambda i, place_ref: (0, place_ref[0]))
    return pl.pallas_call(
        body,
        grid_spec=pltpu.PrefetchScalarGridSpec(
            num_scalar_prefetch=1,
            grid=(length // block,),
            in_specs=[cols] * count
            + [whole((local_len, width))] * count
            + [spectrum_block(width, block), by_row, by_row, by_col]
            + [whole(rows_of.shape)],
            out_specs=[
                spectrum_block(width, block),
                whole((length, width)),
                whole((length, width)),
            ],
            scratch_shapes=[VMEM((length, width), bf16), VMEM((length, width), f32)],
        ),
        out_shape=[
            struct((2, length, width), f32),
            struct((length, width), f32),
            struct((length, width), bf16),
        ],
        name="convolve",
        compiler_params=grant(
            [((6, block, length), 2), ((4, block, width), 4), ((3, length, width), 4)], length, width
        ),
    )(place, *signal_rel, *cot_rel, filt_spec, a_high, a_low, t_high, rows_of)


def grant(blocks, length, width):
    held = sum(math.prod(shape) * size for shape, size in blocks)
    need = 2 * held + 8 * length * width * 4 + (4 << 20)
    return pltpu.CompilerParams(vmem_limit_bytes=min(need, 60 << 20))


def smem():
    return pl.BlockSpec(memory_space=pltpu.SMEM)


def weight_grads(place, signal_rel, gate_grad, groups):
    count = len(signal_rel)
    local_len, channels = signal_rel[0].shape
    width = gate_grad.shape[1]
    rows = channels // sum(len(group) for group in groups)
    length = local_len * count

    def body(place_ref, *refs):
        sig = refs[:count]
        grad = refs[count]
        outs = refs[count + 1 :]
        right = jnp.concatenate(
            [grad[piece(place_ref, r, local_len), :] for r in range(count)], axis=0
        )
        for out, group in zip(outs, groups):
            for at, k in enumerate(group):
                start = pl.multiple_of((place_ref[1] ^ k) * rows, rows)
                left = jnp.concatenate(
                    [sig[r][:, pl.ds(start, rows)] for r in range(count)], axis=0
                )
                out[at] = dot_first(left, right).astype(bf16)

    return pl.pallas_call(
        body,
        in_specs=[smem()] + [pl.BlockSpec(memory_space=VMEM)] * (count + 1),
        out_specs=[pl.BlockSpec(memory_space=VMEM)] * len(groups),
        out_shape=[struct((len(group), rows, width), bf16) for group in groups],
        name="weight_grads",
        compiler_params=grant([((length, channels), 2), ((2, channels, width), 2)], length, width),
    )(place, *signal_rel, gate_grad)


def gating(place, signal_rel, weight_rel, cot_rel, inner):
    count = len(signal_rel)
    dp_count = len(weight_rel)
    local_len, channels = signal_rel[0].shape
    rows, width = weight_rel[0].shape
    length = local_len * count

    def body(place_ref, *refs):
        sig = refs[:count]
        weight = refs[count : count + dp_count]
        cot = refs[count + dp_count : 2 * count + dp_count]
        inner_ref = refs[2 * count + dp_count]
        outs = refs[2 * count + dp_count + 1 : -1]
        full = refs[-1]
        inner_grad_out, conv_grad_out, skip_out = outs[count:]
        for k in range(dp_count):
            start = pl.multiple_of((place_ref[1] ^ k) * rows, rows)
            full[pl.ds(start, rows), :] = weight[k][...]
        left = jnp.concatenate([sig[r][...] for r in range(count)], axis=0)
        gates = dot(left, full[...])
        skip_sum = jnp.zeros((1, width), f32)
        own = pl.multiple_of(place_ref[0] * width, width)
        for r in range(count):
            here = piece(place_ref, r, local_len)
            gate = gates[r * local_len : (r + 1) * local_len]
            outs[r][...] = (gate * inner_ref[here, :]).astype(bf16)
            inner_grad = cot[r][...].astype(f32) * gate
            inner_grad_out[here, :] = inner_grad
            conv_grad_out[here, :] = inner_grad.astype(bf16)
            signal = sig[r][:, pl.ds(own, width)].astype(f32)
            skip_sum += jnp.sum(inner_grad * signal, axis=0, keepdims=True)
        skip_out[...] = jnp.broadcast_to(skip_sum, (8, width))

    return pl.pallas_call(
        body,
        in_specs=[smem()] + [pl.BlockSpec(memory_space=VMEM)] * (2 * count + dp_count + 1),
        out_specs=[pl.BlockSpec(memory_space=VMEM)] * (count + 3),
        out_shape=[struct((local_len, width), bf16)] * count
        + [
            struct((length, width), f32),
            struct((length, width), bf16),
            struct((8, width), f32),
        ],
        scratch_shapes=[VMEM((channels, width), bf16)],
        name="gating",
        compiler_params=grant([((length, channels), 2), ((2, channels, width), 2)], length, width),
    )(place, *signal_rel, *weight_rel, *cot_rel, inner)


def packed_rows(order, table_rows, width):
    per_group = width // order
    groups = -(-(table_rows // 8) // per_group)
    return order + 8 + 8 * groups, per_group


def correlate_back(place, conv_grad, inner_grad, filt_spec, tables, rows_of, block):
    a_high, a_low, t_high = tables
    length, width = conv_grad.shape

    def body(place_ref, cg, ig, fs, ah, al, th, skip_ref, direct_out, spec, back):
        step = pl.program_id(0)
        re = to_spectrum(ah, al, 0, cg[...])
        im = to_spectrum(ah, al, 1, cg[...])
        spec[0] = re
        spec[1] = im
        term = from_spectrum(th, fs[0] * re + fs[1] * im, fs[0] * im - fs[1] * re, length)

        @pl.when(step == 0)
        def _():
            back[...] = term

        @pl.when(step != 0)
        def _():
            back[...] += term

        @pl.when(step == pl.num_programs(0) - 1)
        def _():
            direct_out[...] = ig[...] * skip_ref[2:3, :] + back[...].astype(bf16).astype(f32)

    by_row, by_col = table_specs(length, block)
    spec_block = spectrum_block(width, block)
    return pl.pallas_call(
        body,
        grid_spec=pltpu.PrefetchScalarGridSpec(
            num_scalar_prefetch=1,
            grid=(length // block,),
            in_specs=[
                whole((length, width)),
                whole((length, width)),
                spec_block,
                by_row,
                by_row,
                by_col,
                whole(rows_of.shape),
            ],
            out_specs=[whole((length, width)), spec_block],
            scratch_shapes=[VMEM((length, width), f32)],
        ),
        out_shape=[struct((length, width), f32), struct((2, length, width), f32)],
        name="correlate_back",
        compiler_params=grant(
            [((6, block, length), 2), ((4, block, width), 4), ((3, length, width), 4)], length, width
        ),
    )(place, conv_grad, inner_grad, filt_spec, a_high, a_low, t_high, rows_of)


def correlate_part(
    place, grad_spec, skip_sum, signal_spec, tables, env, hidden, filter_weight, cos_pre, table,
    block,
):
    t_high = tables[2]
    length, width = env.shape
    order = filter_weight.shape[0]
    feature_start = constant_rows(length)[8]
    table_rows = table.shape[0] - feature_start
    total_rows, per_group = packed_rows(order, table_rows, width)

    def body(
        place_ref, gs, skip_sum_ref, ss, th, env_ref, hid, fw, cp, tab, packed, part,
    ):
        step = pl.program_id(0)
        term = from_spectrum(
            th, ss[0] * gs[0] + ss[1] * gs[1], ss[0] * gs[1] - ss[1] * gs[0], length
        )

        @pl.when(step == 0)
        def _():
            part[...] = term

        @pl.when(step != 0)
        def _():
            part[...] += term

        @pl.when(step == pl.num_programs(0) - 1)
        def _():
            pre_grad = part[...].astype(bf16).astype(f32) * env_ref[...]
            packed[...] = jnp.zeros((total_rows, width), f32)
            packed[:order, :] = careful(dot_first, hid[...], pre_grad)
            packed[order : order + 8, :] = skip_sum_ref[...]
            act = careful(dot_last, pre_grad, fw[...]) * cp[...]
            small = careful(dot, tab[feature_start:, :], act)
            for b in range(table_rows // 8):
                row = order + 8 + 8 * (b // per_group)
                col = order * (b % per_group)
                packed[row : row + 8, col : col + order] = small[8 * b : 8 * b + 8]

    _, by_col = table_specs(length, block)
    spec_block = spectrum_block(width, block)
    return pl.pallas_call(
        body,
        grid_spec=pltpu.PrefetchScalarGridSpec(
            num_scalar_prefetch=1,
            grid=(length // block,),
            in_specs=[
                spec_block,
                whole((8, width)),
                spec_block,
                by_col,
                whole((length, width)),
                whole(hidden.shape),
                pl.BlockSpec((order, width), lambda i, place_ref: (0, place_ref[0])),
                whole(cos_pre.shape),
                whole(table.shape),
            ],
            out_specs=whole((total_rows, width)),
            scratch_shapes=[VMEM((length, width), f32)],
        ),
        out_shape=struct((total_rows, width), f32),
        name="correlate_part",
        compiler_params=grant(
            [((2, block, length), 2), ((4, block, width), 4), ((2, length, width), 4)], length, width
        ),
    )(
        place, grad_spec, skip_sum, signal_spec, t_high, env, hidden, filter_weight, cos_pre,
        table,
    )


def through_gate(place, gate_grad, weight_rel, direct, count):
    dp_count = len(weight_rel)
    rows, width = weight_rel[0].shape
    length = gate_grad.shape[0]
    local_len = length // count
    channels = rows * dp_count

    def body(place_ref, *refs):
        grad = refs[0]
        weight = refs[1 : 1 + dp_count]
        direct_ref = refs[1 + dp_count]
        outs = refs[2 + dp_count :]
        left = jnp.concatenate(
            [grad[piece(place_ref, r, local_len), :] for r in range(count)], axis=0
        )
        for k in range(dp_count):
            start = pl.multiple_of((place_ref[1] ^ k) * rows, rows)
            shift = start - place_ref[0] * width
            inside = jnp.logical_and(shift >= 0, shift < width)
            shift = pl.multiple_of(jnp.clip(shift, 0, width - rows), rows)
            scale = jnp.where(inside, 1.0, 0.0).astype(f32)
            terms = dot_last(left, weight[k][...])
            for r in range(count):
                term = terms[r * local_len : (r + 1) * local_len]
                term += scale * direct_ref[piece(place_ref, r, local_len), pl.ds(shift, rows)]
                outs[r][:, pl.ds(start, rows)] = term.astype(bf16)

    return pl.pallas_call(
        body,
        in_specs=[smem()] + [pl.BlockSpec(memory_space=VMEM)] * (dp_count + 2),
        out_specs=[pl.BlockSpec(memory_space=VMEM)] * count,
        out_shape=[struct((local_len, channels), bf16)] * count,
        name="through_gate",
        compiler_params=grant([((length, channels), 2), ((channels, width), 2)], length, width),
    )(place, gate_grad, *weight_rel, direct)


def assemble(place, pieces, kind):
    count = len(pieces)
    rows, width = pieces[0].shape

    def body(place_ref, *refs):
        out = refs[count]
        for r in range(count):
            start = pl.multiple_of((place_ref[0] ^ r) * width, width)
            out[:, pl.ds(start, width)] = refs[r][...].astype(kind)

    return pl.pallas_call(
        body,
        in_specs=[smem()] + [pl.BlockSpec(memory_space=VMEM)] * count,
        out_specs=pl.BlockSpec(memory_space=VMEM),
        out_shape=struct((rows, width * count), kind),
        name="assemble",
        compiler_params=grant([((rows, 2 * width * count), 4)], rows, width),
    )(place, *pieces)


def finish(place, pieces, order, emb_count):
    count = len(pieces)
    rows, width = pieces[0].shape
    table_rows = 8 * (emb_count // 8 + 1)
    _, per_group = packed_rows(order, table_rows, width)

    def body(place_ref, *refs):
        filter_out, skip_out, pos_out, bias_out = refs[count:]
        for r in range(count):
            cols = pl.ds(pl.multiple_of((place_ref[0] ^ r) * width, width), width)
            values = refs[r][...].astype(f32)
            filter_out[:, cols] = values[:order, :]
            skip_out[:, cols] = values[order : order + 1, :]
        tails = [refs[r][...].astype(f32)[order + 8 :, :] for r in range(count)]
        while len(tails) > 1:
            tails = [tails[i] + tails[i + 1] for i in range(0, len(tails), 2)]
        for b in range(table_rows // 8):
            row = 8 * (b // per_group)
            col = order * (b % per_group)
            found = tails[0][row : row + 8, col : col + order]
            low = 8 * b
            high = min(low + 8, emb_count)
            if high > low:
                pos_out[low:high, :] = found[: high - low]
            if low <= emb_count < low + 8:
                bias_out[...] = found[emb_count - low : emb_count - low + 1]

    return pl.pallas_call(
        body,
        in_specs=[smem()] + [pl.BlockSpec(memory_space=VMEM)] * count,
        out_specs=[pl.BlockSpec(memory_space=VMEM)] * 4,
        out_shape=[
            struct((order, width * count), f32),
            struct((1, width * count), f32),
            struct((emb_count, order), f32),
            struct((1, order), f32),
        ],
        name="finish",
        compiler_params=grant([((rows, 2 * width * count), 4)], rows, width),
    )(place, *pieces)


def swap(value, axis, offset):
    count = lax.axis_size(axis)
    return lax.ppermute(value, axis, [(i, i ^ offset) for i in range(count)])


def gather_rel(own, axis):
    count = lax.axis_size(axis)
    found = {0: own}
    bit = count // 2
    while bit:
        for r in list(found):
            found[r | bit] = swap(found[r], axis, bit)
        bit //= 2
    return [found[r] for r in range(count)]


def add_round(*terms):
    total = terms[0].astype(f32)
    for term in terms[1:]:
        total = total + term.astype(f32)
    return total.astype(bf16)


def shards(
    signal, gate_weight, pos_weight, pos_bias, filter_weight, decay_rate, skip_gain, grad_out
):
    seq_count = lax.axis_size("seq")
    dp_count = lax.axis_size("dp")
    signal_tok = signal[0]
    cot_tok = grad_out[0]
    local_len, channels = signal_tok.shape
    length = local_len * seq_count
    width = channels // seq_count
    emb_count, order = pos_weight.shape
    seq_at = lax.axis_index("seq")
    dp_at = lax.axis_index("dp")
    place = jnp.stack([seq_at, dp_at]).astype(jnp.int32)
    block = min(256, length)

    def own_cols(x, r=0):
        return lax.dynamic_slice_in_dim(x, (seq_at ^ r) * width, width, axis=x.ndim - 1)

    signal_rel = gather_rel(signal_tok, "seq")
    weight_rel = {0: own_cols(gate_weight)}
    for k in range(2, dp_count, 2):
        weight_rel[k] = swap(weight_rel[0], "dp", k)
    for k in range(0, dp_count, 2):
        weight_rel[k + 1] = swap(weight_rel[k], "dp", 1)
    weight_rel = [weight_rel[k] for k in range(dp_count)]
    cot_rel = [own_cols(cot_tok)] + [
        swap(own_cols(cot_tok, r), "seq", r) for r in range(1, seq_count)
    ]

    table = jnp.asarray(constants(length, emb_count))
    rates = decay_rate[None]
    norm = jnp.sqrt(jnp.expm1(-2.0 * rates * length) / jnp.expm1(-2.0 * rates))
    rows_of = jnp.concatenate([rates, norm, skip_gain[None]])
    a_high, a_low, t_high, filt_spec, env, hidden, cos_pre, rows_of = generate(
        place, table, pos_weight, pos_bias[None], filter_weight, rows_of, width, block
    )
    tables = (a_high, a_low, t_high)

    signal_spec, inner, gate_grad = convolve(
        place, signal_rel, cot_rel, filt_spec, tables, rows_of, block
    )

    far = list(reversed(range(0, dp_count, 2)))
    pairs = stages(dp_count)
    groups = [[k + 1 for k in pair] for pair in pairs] + pairs
    weight_parts = weight_grads(place, signal_rel, gate_grad, groups)
    sums = {}
    for i, pair in enumerate(pairs):
        met = swap(weight_parts[i], "dp", 1)
        for at, k in enumerate(pair):
            sums[k] = add_round(weight_parts[len(pairs) + i][at], met[at])
    row_sum = add_round(sums[0], *[swap(sums[k], "dp", k) for k in far[:-1]])
    row_rel = gather_rel(row_sum, "seq")
    grad_gate_weight = assemble(place, row_rel, f32)

    gated = gating(place, signal_rel, weight_rel, cot_rel, inner)
    out_rel = gated[:seq_count]
    inner_grad, conv_grad, skip_sum = gated[seq_count:]
    out_rel = [out_rel[0]] + [swap(out_rel[r], "seq", r) for r in range(1, seq_count)]
    output = assemble(place, out_rel, bf16)

    direct, grad_spec = correlate_back(
        place, conv_grad, inner_grad, filt_spec, tables, rows_of, block
    )
    packed = correlate_part(
        place, grad_spec, skip_sum, signal_spec, tables, env, hidden, filter_weight, cos_pre,
        table, block,
    )
    back_rel = through_gate(place, gate_grad, weight_rel, direct, seq_count)

    live = {r: back_rel[r] for r in range(seq_count)}
    bit = 1
    while bit < seq_count:
        met = {r: swap(live[r | bit], "seq", bit) for r in live if not r & bit}
        live = {r: add_round(live[r], met[r]) for r in met}
        bit *= 2
    grad_signal = live[0]

    met = swap(packed, "dp", 1)
    packed = (packed + met).astype(bf16)
    terms = [packed] + [swap(packed, "dp", k) for k in range(2, dp_count, 2)]
    terms = [term.astype(f32) for term in terms]
    while len(terms) > 1:
        terms = [terms[i] + terms[i + 1] for i in range(0, len(terms), 2)]
    packed_rel = gather_rel(terms[0].astype(bf16), "seq")
    grad_filter_weight, grad_skip, grad_pos_weight, grad_pos_bias = finish(
        place, packed_rel, order, emb_count
    )
    return (
        output[None],
        grad_signal[None],
        grad_gate_weight,
        grad_pos_weight,
        grad_pos_bias[0],
        grad_filter_weight,
        grad_skip[0],
    )


def stages(dp_count):
    far = list(reversed(range(0, dp_count, 2)))
    return [[k] for k in far[:-2]] + [far[-2:]]


def solution(mesh):
    step = mapped(shards, mesh)
    return step


def mapped(body, mesh):
    return jax.shard_map(
        body,
        mesh=mesh,
        in_specs=(
            P("dp", "seq", None),
            P("dp", None),
            P(),
            P(),
            P(),
            P(),
            P(),
            P("dp", "seq", None),
        ),
        out_specs=(P("dp", "seq", None), P("dp", "seq", None), P("dp", None), P(), P(), P(), P()),
        check_vma=False,
    )
```

```python
import functools
import math

import jax
import jax.numpy as jnp
import numpy as np
from jax import lax
from jax.experimental import pallas as pl
from jax.experimental.pallas import tpu as pltpu
from jax.sharding import PartitionSpec as P


f32 = jnp.float32
bf16 = jnp.bfloat16
VMEM = pltpu.VMEM


BASE = 16


@functools.lru_cache(maxsize=None)
def constants(length, emb_count):
    step = 4 * length
    lane = np.arange(length)[None, :]
    coarse = np.arange(length // BASE)[:, None]
    fine = np.arange(BASE)[:, None]
    found = []
    for phase in (
        coarse * lane * (4 * BASE),
        (4 * fine + 1) * lane,
        coarse * BASE * (4 * lane + 1),
        fine * (4 * lane + 1),
    ):
        angle = phase % step * (2.0 * math.pi / step)
        found += [np.cos(angle), np.sin(angle)]
    bands = np.arange(1, (emb_count - 1) // 2 + 1)[:, None]
    angle = bands * lane % length * (2.0 * math.pi / length)
    rows = 8 * (emb_count // 8 + 1)
    found += [lane / length, np.cos(angle), np.sin(angle), np.ones((1, length))]
    found += [np.zeros((rows - emb_count - 1, length))]
    return np.concatenate(found).astype(np.float32)


def constant_rows(length):
    sizes = [length // BASE, length // BASE, BASE, BASE]
    starts = np.cumsum([0] + sizes + sizes).tolist()
    return starts


def dot(a, b):
    return jnp.dot(a, b, preferred_element_type=f32)


def dot_first(a, b):
    return lax.dot_general(a, b, (((0,), (0,)), ((), ())), preferred_element_type=f32)


def dot_last(a, b):
    return lax.dot_general(a, b, (((1,), (1,)), ((), ())), preferred_element_type=f32)


def split(x):
    high = x.astype(bf16)
    return high, (x - high.astype(f32)).astype(bf16)


def careful(product, a, b):
    a_high, a_low = split(a)
    b_high, b_low = split(b)
    return product(a_high, b_high) + (product(a_low, b_high) + product(a_high, b_low))


def to_spectrum(a_high, a_low, part, x):
    return dot(a_high[part], x) + dot(a_low[part], x)


def from_spectrum(t_high, re, im, length):
    total = dot(t_high[0], re.astype(bf16)) + dot(t_high[1], im.astype(bf16))
    return total * (1.0 / length)


def struct(shape, kind):
    return jax.ShapeDtypeStruct(shape, kind)


def whole(shape):
    return pl.BlockSpec(shape, lambda i, *_: (0,) * len(shape))


def table_specs(length, block):
    by_row = pl.BlockSpec((2, block, length), lambda i, *_: (0, i, 0))
    by_col = pl.BlockSpec((2, length, block), lambda i, *_: (0, 0, i))
    return by_row, by_col


def spectrum_block(width, block):
    return pl.BlockSpec((2, block, width), lambda i, *_: (0, i, 0))


def generate(place, table, pos_weight, pos_bias, filter_weight, rows_of, width, block):
    highest = lax.Precision.HIGHEST
    length = table.shape[1]
    emb_count, order = pos_weight.shape
    starts = constant_rows(length)

    def body(place_ref, *refs):
        sources = refs[:5]
        ah, al, th, spec, env_out, hidden_out, pre_out, rows_out, filt, *held, done = refs[5:]
        tab, pw, pb, fw, vec = held
        step = pl.program_id(0)

        @pl.when(step == 0)
        def _():
            mine = pl.ds(pl.multiple_of(place_ref[0] * width, width), width)
            copies = [
                pltpu.make_async_copy(
                    source if i < 3 else source.at[:, mine], target, done.at[i]
                )
                for i, (source, target) in enumerate(zip(sources, held))
            ]
            for copy in copies:
                copy.start()
            for copy in copies:
                copy.wait()
            rows_out[...] = vec[...]
            feat = tab[starts[8] : starts[8] + emb_count, :]
            pre = pb[...] + lax.dot_general(
                feat, pw[...], (((0,), (0,)), ((), ())), precision=highest,
                preferred_element_type=f32,
            )
            hidden = jnp.sin(pre)
            hidden_out[...] = hidden
            pre_out[...] = pre
            at = lax.broadcasted_iota(jnp.int32, (length, width), 0).astype(f32)
            env = jnp.exp(-vec[0:1, :] * at) * (1.0 / vec[1:2, :])
            env_out[...] = env
            filt[...] = (jnp.dot(hidden, fw[...], precision=highest) * env).astype(bf16)

        def rows(at, store):
            cos_start, sin_start, fine_cos, fine_sin = starts[at : at + 4]
            cos_fine = tab[fine_cos : fine_cos + BASE, :]
            sin_fine = tab[fine_sin : fine_sin + BASE, :]

            def one(i, carry):
                here = step * (block // BASE) + i
                out = pl.ds(pl.multiple_of(i * BASE, BASE), BASE)
                cos = tab[pl.ds(cos_start + here, 1), :]
                sin = tab[pl.ds(sin_start + here, 1), :]
                store(out, 0, cos * cos_fine - sin * sin_fine)
                store(out, 1, sin * cos_fine + cos * sin_fine)
                return carry

            lax.fori_loop(0, block // BASE, one, 0)

        def store_both(out, part, value):
            high, low = split(value)
            ah[part, out, :] = high
            al[part, out, :] = low

        def store_high(out, part, value):
            th[part, out, :] = value.astype(bf16)

        rows(0, store_both)
        rows(4, store_high)
        spec[0] = to_spectrum(ah, al, 0, filt[...])
        spec[1] = to_spectrum(ah, al, 1, filt[...])

    by_row = pl.BlockSpec((2, block, length), lambda i, *_: (0, i, 0))
    return pl.pallas_call(
        body,
        grid_spec=pltpu.PrefetchScalarGridSpec(
            num_scalar_prefetch=1,
            grid=(length // block,),
            in_specs=[pl.BlockSpec(memory_space=pltpu.HBM)] * 5,
            out_specs=[by_row, by_row, by_row, spectrum_block(width, block)]
            + [whole((length, width)), whole((length, order)), whole((length, order))]
            + [whole((rows_of.shape[0], width))],
            scratch_shapes=[VMEM((length, width), bf16)]
            + [VMEM(x.shape, f32) for x in (table, pos_weight, pos_bias)]
            + [VMEM((order, width), f32), VMEM((rows_of.shape[0], width), f32)]
            + [pltpu.SemaphoreType.DMA((5,))],
        ),
        out_shape=[struct((2, length, length), bf16)] * 3
        + [struct((2, length, width), f32), struct((length, width), f32)]
        + [struct((length, order), f32)] * 2
        + [struct((rows_of.shape[0], width), f32)],
        name="generate",
        compiler_params=grant(
            [((6, block, length), 2), ((4, block, width), 4), ((2, length, width), 4)]
            + [(table.shape, 4)], length, width
        ),
    )(
        place,
        *[
            pltpu.with_memory_space_constraint(x, pltpu.HBM)
            for x in (table, pos_weight, pos_bias, filter_weight, rows_of)
        ],
    )


def piece(place_ref, r, rows):
    return pl.ds(pl.multiple_of((place_ref[0] ^ r) * rows, rows), rows)


def convolve(place, signal_rel, cot_rel, filt_spec, tables, rows_of, block):
    a_high, a_low, t_high = tables
    count = len(signal_rel)
    local_len, width = cot_rel[0].shape
    length = local_len * count

    def body(place_ref, *refs):
        sig = refs[:count]
        cot = refs[count : 2 * count]
        fs, ah, al, th, skip_ref = refs[2 * count : 2 * count + 5]
        spec, inner_out, grad_out, x, acc = refs[2 * count + 5 :]
        step = pl.program_id(0)

        @pl.when(step == 0)
        def _():
            for r in range(count):
                x[piece(place_ref, r, local_len), :] = sig[r][...]

        re = to_spectrum(ah, al, 0, x[...])
        im = to_spectrum(ah, al, 1, x[...])
        spec[0] = re
        spec[1] = im
        part = from_spectrum(th, re * fs[0] - im * fs[1], re * fs[1] + im * fs[0], length)

        @pl.when(step == 0)
        def _():
            acc[...] = part

        @pl.when(step != 0)
        def _():
            acc[...] += part

        @pl.when(step == pl.num_programs(0) - 1)
        def _():
            conv = acc[...].astype(bf16).astype(f32)
            inner_out[...] = conv + skip_ref[2:3, :] * x[...].astype(f32)
            for r in range(count):
                rows = piece(place_ref, r, local_len)
                grad_out[rows, :] = (cot[r][...].astype(f32) * inner_out[rows, :]).astype(bf16)

    by_row, by_col = table_specs(length, block)
    cols = pl.BlockSpec((local_len, width), lambda i, place_ref: (0, place_ref[0]))
    return pl.pallas_call(
        body,
        grid_spec=pltpu.PrefetchScalarGridSpec(
            num_scalar_prefetch=1,
            grid=(length // block,),
            in_specs=[cols] * count
            + [whole((local_len, width))] * count
            + [spectrum_block(width, block), by_row, by_row, by_col]
            + [whole(rows_of.shape)],
            out_specs=[
                spectrum_block(width, block),
                whole((length, width)),
                whole((length, width)),
            ],
            scratch_shapes=[VMEM((length, width), bf16), VMEM((length, width), f32)],
        ),
        out_shape=[
            struct((2, length, width), f32),
            struct((length, width), f32),
            struct((length, width), bf16),
        ],
        name="convolve",
        compiler_params=grant(
            [((6, block, length), 2), ((4, block, width), 4), ((3, length, width), 4)], length, width
        ),
    )(place, *signal_rel, *cot_rel, filt_spec, a_high, a_low, t_high, rows_of)


def grant(blocks, length, width):
    held = sum(math.prod(shape) * size for shape, size in blocks)
    need = 2 * held + 8 * length * width * 4 + (4 << 20)
    return pltpu.CompilerParams(vmem_limit_bytes=min(need, 60 << 20))


def smem():
    return pl.BlockSpec(memory_space=pltpu.SMEM)


def weight_grads(place, signal_rel, gate_grad, groups):
    count = len(signal_rel)
    local_len, channels = signal_rel[0].shape
    width = gate_grad.shape[1]
    rows = channels // sum(len(group) for group in groups)
    length = local_len * count

    def body(place_ref, *refs):
        sig = refs[:count]
        grad = refs[count]
        outs = refs[count + 1 :]
        right = jnp.concatenate(
            [grad[piece(place_ref, r, local_len), :] for r in range(count)], axis=0
        )
        for out, group in zip(outs, groups):
            for at, k in enumerate(group):
                start = pl.multiple_of((place_ref[1] ^ k) * rows, rows)
                left = jnp.concatenate(
                    [sig[r][:, pl.ds(start, rows)] for r in range(count)], axis=0
                )
                out[at] = dot_first(left, right).astype(bf16)

    return pl.pallas_call(
        body,
        in_specs=[smem()] + [pl.BlockSpec(memory_space=VMEM)] * (count + 1),
        out_specs=[pl.BlockSpec(memory_space=VMEM)] * len(groups),
        out_shape=[struct((len(group), rows, width), bf16) for group in groups],
        name="weight_grads",
        compiler_params=grant([((length, channels), 2), ((2, channels, width), 2)], length, width),
    )(place, *signal_rel, gate_grad)


def gating(place, signal_rel, weight_rel, cot_rel, inner):
    count = len(signal_rel)
    dp_count = len(weight_rel)
    local_len, channels = signal_rel[0].shape
    rows, width = weight_rel[0].shape
    length = local_len * count

    def body(place_ref, *refs):
        sig = refs[:count]
        weight = refs[count : count + dp_count]
        cot = refs[count + dp_count : 2 * count + dp_count]
        inner_ref = refs[2 * count + dp_count]
        outs = refs[2 * count + dp_count + 1 : -1]
        full = refs[-1]
        inner_grad_out, conv_grad_out, skip_out = outs[count:]
        for k in range(dp_count):
            start = pl.multiple_of((place_ref[1] ^ k) * rows, rows)
            full[pl.ds(start, rows), :] = weight[k][...]
        left = jnp.concatenate([sig[r][...] for r in range(count)], axis=0)
        gates = dot(left, full[...])
        skip_sum = jnp.zeros((1, width), f32)
        own = pl.multiple_of(place_ref[0] * width, width)
        for r in range(count):
            here = piece(place_ref, r, local_len)
            gate = gates[r * local_len : (r + 1) * local_len]
            outs[r][...] = (gate * inner_ref[here, :]).astype(bf16)
            inner_grad = cot[r][...].astype(f32) * gate
            inner_grad_out[here, :] = inner_grad
            conv_grad_out[here, :] = inner_grad.astype(bf16)
            signal = sig[r][:, pl.ds(own, width)].astype(f32)
            skip_sum += jnp.sum(inner_grad * signal, axis=0, keepdims=True)
        skip_out[...] = jnp.broadcast_to(skip_sum, (8, width))

    return pl.pallas_call(
        body,
        in_specs=[smem()] + [pl.BlockSpec(memory_space=VMEM)] * (2 * count + dp_count + 1),
        out_specs=[pl.BlockSpec(memory_space=VMEM)] * (count + 3),
        out_shape=[struct((local_len, width), bf16)] * count
        + [
            struct((length, width), f32),
            struct((length, width), bf16),
            struct((8, width), f32),
        ],
        scratch_shapes=[VMEM((channels, width), bf16)],
        name="gating",
        compiler_params=grant([((length, channels), 2), ((2, channels, width), 2)], length, width),
    )(place, *signal_rel, *weight_rel, *cot_rel, inner)


def packed_rows(order, table_rows, width):
    per_group = width // order
    groups = -(-(table_rows // 8) // per_group)
    return order + 8 + 8 * groups, per_group


def correlate_back(place, conv_grad, inner_grad, filt_spec, tables, rows_of, block):
    a_high, a_low, t_high = tables
    length, width = conv_grad.shape

    def body(place_ref, cg, ig, fs, ah, al, th, skip_ref, direct_out, spec, back):
        step = pl.program_id(0)
        re = to_spectrum(ah, al, 0, cg[...])
        im = to_spectrum(ah, al, 1, cg[...])
        spec[0] = re
        spec[1] = im
        term = from_spectrum(th, fs[0] * re + fs[1] * im, fs[0] * im - fs[1] * re, length)

        @pl.when(step == 0)
        def _():
            back[...] = term

        @pl.when(step != 0)
        def _():
            back[...] += term

        @pl.when(step == pl.num_programs(0) - 1)
        def _():
            direct_out[...] = ig[...] * skip_ref[2:3, :] + back[...].astype(bf16).astype(f32)

    by_row, by_col = table_specs(length, block)
    spec_block = spectrum_block(width, block)
    return pl.pallas_call(
        body,
        grid_spec=pltpu.PrefetchScalarGridSpec(
            num_scalar_prefetch=1,
            grid=(length // block,),
            in_specs=[
                whole((length, width)),
                whole((length, width)),
                spec_block,
                by_row,
                by_row,
                by_col,
                whole(rows_of.shape),
            ],
            out_specs=[whole((length, width)), spec_block],
            scratch_shapes=[VMEM((length, width), f32)],
        ),
        out_shape=[struct((length, width), f32), struct((2, length, width), f32)],
        name="correlate_back",
        compiler_params=grant(
            [((6, block, length), 2), ((4, block, width), 4), ((3, length, width), 4)], length, width
        ),
    )(place, conv_grad, inner_grad, filt_spec, a_high, a_low, t_high, rows_of)


def correlate_part(
    place, grad_spec, skip_sum, signal_spec, tables, env, hidden, filter_weight, pre, table,
    block,
):
    t_high = tables[2]
    length, width = env.shape
    order = filter_weight.shape[0]
    feature_start = constant_rows(length)[8]
    table_rows = table.shape[0] - feature_start
    total_rows, per_group = packed_rows(order, table_rows, width)

    def body(
        place_ref, gs, skip_sum_ref, ss, th, env_ref, hid, fw, pre_ref, tab, packed, part,
    ):
        step = pl.program_id(0)
        term = from_spectrum(
            th, ss[0] * gs[0] + ss[1] * gs[1], ss[0] * gs[1] - ss[1] * gs[0], length
        )

        @pl.when(step == 0)
        def _():
            part[...] = term

        @pl.when(step != 0)
        def _():
            part[...] += term

        @pl.when(step == pl.num_programs(0) - 1)
        def _():
            pre_grad = part[...].astype(bf16).astype(f32) * env_ref[...]
            packed[...] = jnp.zeros((total_rows, width), f32)
            packed[:order, :] = careful(dot_first, hid[...], pre_grad)
            packed[order : order + 8, :] = skip_sum_ref[...]
            act = careful(dot_last, pre_grad, fw[...]) * jnp.cos(pre_ref[...])
            small = careful(dot, tab[feature_start:, :], act)
            for b in range(table_rows // 8):
                row = order + 8 + 8 * (b // per_group)
                col = order * (b % per_group)
                packed[row : row + 8, col : col + order] = small[8 * b : 8 * b + 8]

    _, by_col = table_specs(length, block)
    spec_block = spectrum_block(width, block)
    return pl.pallas_call(
        body,
        grid_spec=pltpu.PrefetchScalarGridSpec(
            num_scalar_prefetch=1,
            grid=(length // block,),
            in_specs=[
                spec_block,
                whole((8, width)),
                spec_block,
                by_col,
                whole((length, width)),
                whole(hidden.shape),
                pl.BlockSpec((order, width), lambda i, place_ref: (0, place_ref[0])),
                whole(pre.shape),
                whole(table.shape),
            ],
            out_specs=whole((total_rows, width)),
            scratch_shapes=[VMEM((length, width), f32)],
        ),
        out_shape=struct((total_rows, width), f32),
        name="correlate_part",
        compiler_params=grant(
            [((2, block, length), 2), ((4, block, width), 4), ((2, length, width), 4)], length, width
        ),
    )(
        place, grad_spec, skip_sum, signal_spec, t_high, env, hidden, filter_weight, pre,
        table,
    )


def through_gate(place, gate_grad, weight_rel, direct, count):
    dp_count = len(weight_rel)
    rows, width = weight_rel[0].shape
    length = gate_grad.shape[0]
    local_len = length // count
    channels = rows * dp_count

    def body(place_ref, *refs):
        grad = refs[0]
        weight = refs[1 : 1 + dp_count]
        direct_ref = refs[1 + dp_count]
        outs = refs[2 + dp_count :]
        left = jnp.concatenate(
            [grad[piece(place_ref, r, local_len), :] for r in range(count)], axis=0
        )
        for k in range(dp_count):
            start = pl.multiple_of((place_ref[1] ^ k) * rows, rows)
            shift = start - place_ref[0] * width
            inside = jnp.logical_and(shift >= 0, shift < width)
            shift = pl.multiple_of(jnp.clip(shift, 0, width - rows), rows)
            scale = jnp.where(inside, 1.0, 0.0).astype(f32)
            terms = dot_last(left, weight[k][...])
            for r in range(count):
                term = terms[r * local_len : (r + 1) * local_len]
                term += scale * direct_ref[piece(place_ref, r, local_len), pl.ds(shift, rows)]
                outs[r][:, pl.ds(start, rows)] = term.astype(bf16)

    return pl.pallas_call(
        body,
        in_specs=[smem()] + [pl.BlockSpec(memory_space=VMEM)] * (dp_count + 2),
        out_specs=[pl.BlockSpec(memory_space=VMEM)] * count,
        out_shape=[struct((local_len, channels), bf16)] * count,
        name="through_gate",
        compiler_params=grant([((length, channels), 2), ((channels, width), 2)], length, width),
    )(place, gate_grad, *weight_rel, direct)


def assemble(place, pieces, kind):
    count = len(pieces)
    rows, width = pieces[0].shape

    def body(place_ref, *refs):
        out = refs[count]
        for r in range(count):
            start = pl.multiple_of((place_ref[0] ^ r) * width, width)
            out[:, pl.ds(start, width)] = refs[r][...].astype(kind)

    return pl.pallas_call(
        body,
        in_specs=[smem()] + [pl.BlockSpec(memory_space=VMEM)] * count,
        out_specs=pl.BlockSpec(memory_space=VMEM),
        out_shape=struct((rows, width * count), kind),
        name="assemble",
        compiler_params=grant([((rows, 2 * width * count), 4)], rows, width),
    )(place, *pieces)


def finish(place, pieces, order, emb_count):
    count = len(pieces)
    rows, width = pieces[0].shape
    table_rows = 8 * (emb_count // 8 + 1)
    _, per_group = packed_rows(order, table_rows, width)

    def body(place_ref, *refs):
        filter_out, skip_out, pos_out, bias_out = refs[count:]
        for r in range(count):
            cols = pl.ds(pl.multiple_of((place_ref[0] ^ r) * width, width), width)
            values = refs[r][...].astype(f32)
            filter_out[:, cols] = values[:order, :]
            skip_out[:, cols] = values[order : order + 1, :]
        tails = [refs[r][...].astype(f32)[order + 8 :, :] for r in range(count)]
        while len(tails) > 1:
            tails = [tails[i] + tails[i + 1] for i in range(0, len(tails), 2)]
        for b in range(table_rows // 8):
            row = 8 * (b // per_group)
            col = order * (b % per_group)
            found = tails[0][row : row + 8, col : col + order]
            low = 8 * b
            high = min(low + 8, emb_count)
            if high > low:
                pos_out[low:high, :] = found[: high - low]
            if low <= emb_count < low + 8:
                bias_out[...] = found[emb_count - low : emb_count - low + 1]

    return pl.pallas_call(
        body,
        in_specs=[smem()] + [pl.BlockSpec(memory_space=VMEM)] * count,
        out_specs=[pl.BlockSpec(memory_space=VMEM)] * 4,
        out_shape=[
            struct((order, width * count), f32),
            struct((1, width * count), f32),
            struct((emb_count, order), f32),
            struct((1, order), f32),
        ],
        name="finish",
        compiler_params=grant([((rows, 2 * width * count), 4)], rows, width),
    )(place, *pieces)


def swap(value, axis, offset):
    count = lax.axis_size(axis)
    return lax.ppermute(value, axis, [(i, i ^ offset) for i in range(count)])


def gather_rel(own, axis):
    count = lax.axis_size(axis)
    found = {0: own}
    bit = count // 2
    while bit:
        for r in list(found):
            found[r | bit] = swap(found[r], axis, bit)
        bit //= 2
    return [found[r] for r in range(count)]


def add_round(*terms):
    total = terms[0].astype(f32)
    for term in terms[1:]:
        total = total + term.astype(f32)
    return total.astype(bf16)


def shards(
    signal, gate_weight, pos_weight, pos_bias, filter_weight, decay_rate, skip_gain, grad_out
):
    seq_count = lax.axis_size("seq")
    dp_count = lax.axis_size("dp")
    signal_tok = signal[0]
    cot_tok = grad_out[0]
    local_len, channels = signal_tok.shape
    length = local_len * seq_count
    width = channels // seq_count
    emb_count, order = pos_weight.shape
    seq_at = lax.axis_index("seq")
    dp_at = lax.axis_index("dp")
    place = jnp.stack([seq_at, dp_at]).astype(jnp.int32)
    block = min(256, length)

    def own_cols(x, r=0):
        return lax.dynamic_slice_in_dim(x, (seq_at ^ r) * width, width, axis=x.ndim - 1)

    signal_rel = gather_rel(signal_tok, "seq")
    weight_rel = {0: own_cols(gate_weight)}
    for k in range(2, dp_count, 2):
        weight_rel[k] = swap(weight_rel[0], "dp", k)
    for k in range(0, dp_count, 2):
        weight_rel[k + 1] = swap(weight_rel[k], "dp", 1)
    weight_rel = [weight_rel[k] for k in range(dp_count)]
    cot_rel = [own_cols(cot_tok)] + [
        swap(own_cols(cot_tok, r), "seq", r) for r in range(1, seq_count)
    ]

    table = jnp.asarray(constants(length, emb_count))
    rates = decay_rate[None]
    norm = jnp.sqrt(jnp.expm1(-2.0 * rates * length) / jnp.expm1(-2.0 * rates))
    rows_of = jnp.concatenate([rates, norm, skip_gain[None]])
    a_high, a_low, t_high, filt_spec, env, hidden, pre, rows_of = generate(
        place, table, pos_weight, pos_bias[None], filter_weight, rows_of, width, block
    )
    tables = (a_high, a_low, t_high)

    signal_spec, inner, gate_grad = convolve(
        place, signal_rel, cot_rel, filt_spec, tables, rows_of, block
    )

    far = list(reversed(range(0, dp_count, 2)))
    pairs = stages(dp_count)
    groups = [[k + 1 for k in pair] for pair in pairs] + pairs
    weight_parts = weight_grads(place, signal_rel, gate_grad, groups)
    sums = {}
    for i, pair in enumerate(pairs):
        met = swap(weight_parts[i], "dp", 1)
        for at, k in enumerate(pair):
            sums[k] = add_round(weight_parts[len(pairs) + i][at], met[at])
    row_sum = add_round(sums[0], *[swap(sums[k], "dp", k) for k in far[:-1]])
    row_rel = gather_rel(row_sum, "seq")
    grad_gate_weight = assemble(place, row_rel, f32)

    gated = gating(place, signal_rel, weight_rel, cot_rel, inner)
    out_rel = gated[:seq_count]
    inner_grad, conv_grad, skip_sum = gated[seq_count:]
    out_rel = [out_rel[0]] + [swap(out_rel[r], "seq", r) for r in range(1, seq_count)]
    output = assemble(place, out_rel, bf16)

    direct, grad_spec = correlate_back(
        place, conv_grad, inner_grad, filt_spec, tables, rows_of, block
    )
    packed = correlate_part(
        place, grad_spec, skip_sum, signal_spec, tables, env, hidden, filter_weight, pre,
        table, block,
    )
    back_rel = through_gate(place, gate_grad, weight_rel, direct, seq_count)

    live = {r: back_rel[r] for r in range(seq_count)}
    bit = 1
    while bit < seq_count:
        met = {r: swap(live[r | bit], "seq", bit) for r in live if not r & bit}
        live = {r: add_round(live[r], met[r]) for r in met}
        bit *= 2
    grad_signal = live[0]

    met = swap(packed, "dp", 1)
    packed = (packed + met).astype(bf16)
    terms = [packed] + [swap(packed, "dp", k) for k in range(2, dp_count, 2)]
    terms = [term.astype(f32) for term in terms]
    while len(terms) > 1:
        terms = [terms[i] + terms[i + 1] for i in range(0, len(terms), 2)]
    packed_rel = gather_rel(terms[0].astype(bf16), "seq")
    grad_filter_weight, grad_skip, grad_pos_weight, grad_pos_bias = finish(
        place, packed_rel, order, emb_count
    )
    return (
        output[None],
        grad_signal[None],
        grad_gate_weight,
        grad_pos_weight,
        grad_pos_bias[0],
        grad_filter_weight,
        grad_skip[0],
    )


def stages(dp_count):
    far = list(reversed(range(0, dp_count, 2)))
    return [[k] for k in far[:-2]] + [far[-2:]]


def solution(mesh):
    step = mapped(shards, mesh)
    return step


def mapped(body, mesh):
    return jax.shard_map(
        body,
        mesh=mesh,
        in_specs=(
            P("dp", "seq", None),
            P("dp", None),
            P(),
            P(),
            P(),
            P(),
            P(),
            P("dp", "seq", None),
        ),
        out_specs=(P("dp", "seq", None), P("dp", "seq", None), P("dp", None), P(), P(), P(), P()),
        check_vma=False,
    )
```

```python
import functools
import math

import jax
import jax.numpy as jnp
import numpy as np
from jax import lax
from jax.experimental import pallas as pl
from jax.experimental.pallas import tpu as pltpu
from jax.sharding import PartitionSpec as P


f32 = jnp.float32
bf16 = jnp.bfloat16
VMEM = pltpu.VMEM


BASE = 16


@functools.lru_cache(maxsize=None)
def constants(length, emb_count):
    step = 4 * length
    lane = np.arange(length)[None, :]
    coarse = np.arange(length // BASE)[:, None]
    fine = np.arange(BASE)[:, None]
    found = []
    for phase in (
        coarse * lane * (4 * BASE),
        (4 * fine + 1) * lane,
        coarse * BASE * (4 * lane + 1),
        fine * (4 * lane + 1),
    ):
        angle = phase % step * (2.0 * math.pi / step)
        found += [np.cos(angle), np.sin(angle)]
    bands = np.arange(1, (emb_count - 1) // 2 + 1)[:, None]
    angle = bands * lane % length * (2.0 * math.pi / length)
    rows = 8 * (emb_count // 8 + 1)
    found += [lane / length, np.cos(angle), np.sin(angle), np.ones((1, length))]
    found += [np.zeros((rows - emb_count - 1, length))]
    return np.concatenate(found).astype(np.float32)


def constant_rows(length):
    sizes = [length // BASE, length // BASE, BASE, BASE]
    starts = np.cumsum([0] + sizes + sizes).tolist()
    return starts


def dot(a, b):
    return jnp.dot(a, b, preferred_element_type=f32)


def dot_first(a, b):
    return lax.dot_general(a, b, (((0,), (0,)), ((), ())), preferred_element_type=f32)


def dot_last(a, b):
    return lax.dot_general(a, b, (((1,), (1,)), ((), ())), preferred_element_type=f32)


def split(x):
    high = x.astype(bf16)
    return high, (x - high.astype(f32)).astype(bf16)


def careful(product, a, b):
    a_high, a_low = split(a)
    b_high, b_low = split(b)
    return product(a_high, b_high) + (product(a_low, b_high) + product(a_high, b_low))


def to_spectrum(a_high, a_low, part, x):
    return dot(a_high[part], x) + dot(a_low[part], x)


def from_spectrum(t_high, re, im, length):
    total = dot(t_high[0], re.astype(bf16)) + dot(t_high[1], im.astype(bf16))
    return total * (1.0 / length)


def struct(shape, kind):
    return jax.ShapeDtypeStruct(shape, kind)


def whole(shape):
    return pl.BlockSpec(shape, lambda i, *_: (0,) * len(shape))


def table_specs(length, block):
    by_row = pl.BlockSpec((2, block, length), lambda i, *_: (0, i, 0))
    by_col = pl.BlockSpec((2, length, block), lambda i, *_: (0, 0, i))
    return by_row, by_col


def spectrum_block(width, block):
    return pl.BlockSpec((2, block, width), lambda i, *_: (0, i, 0))


def generate(place, table, pos_weight, pos_bias, filter_weight, rows_of, width, block):
    highest = lax.Precision.HIGHEST
    length = table.shape[1]
    emb_count, order = pos_weight.shape
    starts = constant_rows(length)

    def body(place_ref, *refs):
        sources = refs[:5]
        ah, al, th, spec, env_out, hidden_out, cos_out, rows_out, filt, *held, done = refs[5:]
        tab, pw, pb, fw, vec = held
        step = pl.program_id(0)

        @pl.when(step == 0)
        def _():
            mine = pl.ds(pl.multiple_of(place_ref[0] * width, width), width)
            copies = [
                pltpu.make_async_copy(
                    source if i < 3 else source.at[:, mine], target, done.at[i]
                )
                for i, (source, target) in enumerate(zip(sources, held))
            ]
            for copy in copies:
                copy.start()
            for copy in copies:
                copy.wait()
            rows_out[...] = vec[...]
            feat = tab[starts[8] : starts[8] + emb_count, :]
            pre = pb[...] + lax.dot_general(
                feat, pw[...], (((0,), (0,)), ((), ())), precision=highest,
                preferred_element_type=f32,
            )
            hidden = jnp.sin(pre)
            hidden_out[...] = hidden
            cos_out[...] = jnp.cos(pre)
            at = lax.broadcasted_iota(jnp.int32, (length, width), 0).astype(f32)
            env = jnp.exp(-vec[0:1, :] * at) * (1.0 / vec[1:2, :])
            env_out[...] = env
            filt[...] = (jnp.dot(hidden, fw[...], precision=highest) * env).astype(bf16)

        def rows(at, store):
            cos_start, sin_start, fine_cos, fine_sin = starts[at : at + 4]
            cos_fine = tab[fine_cos : fine_cos + BASE, :]
            sin_fine = tab[fine_sin : fine_sin + BASE, :]

            def one(i, carry):
                here = step * (block // BASE) + i
                out = pl.ds(pl.multiple_of(i * BASE, BASE), BASE)
                cos = tab[pl.ds(cos_start + here, 1), :]
                sin = tab[pl.ds(sin_start + here, 1), :]
                store(out, 0, cos * cos_fine - sin * sin_fine)
                store(out, 1, sin * cos_fine + cos * sin_fine)
                return carry

            lax.fori_loop(0, block // BASE, one, 0, unroll=4)

        def store_both(out, part, value):
            high, low = split(value)
            ah[part, out, :] = high
            al[part, out, :] = low

        def store_high(out, part, value):
            th[part, out, :] = value.astype(bf16)

        rows(0, store_both)
        rows(4, store_high)
        spec[0] = to_spectrum(ah, al, 0, filt[...])
        spec[1] = to_spectrum(ah, al, 1, filt[...])

    by_row = pl.BlockSpec((2, block, length), lambda i, *_: (0, i, 0))
    return pl.pallas_call(
        body,
        grid_spec=pltpu.PrefetchScalarGridSpec(
            num_scalar_prefetch=1,
            grid=(length // block,),
            in_specs=[pl.BlockSpec(memory_space=pltpu.HBM)] * 5,
            out_specs=[by_row, by_row, by_row, spectrum_block(width, block)]
            + [whole((length, width)), whole((length, order)), whole((length, order))]
            + [whole((rows_of.shape[0], width))],
            scratch_shapes=[VMEM((length, width), bf16)]
            + [VMEM(x.shape, f32) for x in (table, pos_weight, pos_bias)]
            + [VMEM((order, width), f32), VMEM((rows_of.shape[0], width), f32)]
            + [pltpu.SemaphoreType.DMA((5,))],
        ),
        out_shape=[struct((2, length, length), bf16)] * 3
        + [struct((2, length, width), f32), struct((length, width), f32)]
        + [struct((length, order), f32)] * 2
        + [struct((rows_of.shape[0], width), f32)],
        name="generate",
        compiler_params=grant(
            [((6, block, length), 2), ((4, block, width), 4), ((2, length, width), 4)]
            + [(table.shape, 4)], length, width
        ),
    )(
        place,
        *[
            pltpu.with_memory_space_constraint(x, pltpu.HBM)
            for x in (table, pos_weight, pos_bias, filter_weight, rows_of)
        ],
    )


def piece(place_ref, r, rows):
    return pl.ds(pl.multiple_of((place_ref[0] ^ r) * rows, rows), rows)


def convolve(place, signal_rel, cot_rel, filt_spec, tables, rows_of, block):
    a_high, a_low, t_high = tables
    count = len(signal_rel)
    local_len, width = cot_rel[0].shape
    length = local_len * count

    def body(place_ref, *refs):
        sig = refs[:count]
        cot = refs[count : 2 * count]
        fs, ah, al, th, skip_ref = refs[2 * count : 2 * count + 5]
        spec, inner_out, grad_out, x, acc = refs[2 * count + 5 :]
        step = pl.program_id(0)

        @pl.when(step == 0)
        def _():
            for r in range(count):
                x[piece(place_ref, r, local_len), :] = sig[r][...]

        re = to_spectrum(ah, al, 0, x[...])
        im = to_spectrum(ah, al, 1, x[...])
        spec[0] = re
        spec[1] = im
        part = from_spectrum(th, re * fs[0] - im * fs[1], re * fs[1] + im * fs[0], length)

        @pl.when(step == 0)
        def _():
            acc[...] = part

        @pl.when(step != 0)
        def _():
            acc[...] += part

        @pl.when(step == pl.num_programs(0) - 1)
        def _():
            conv = acc[...].astype(bf16).astype(f32)
            inner_out[...] = conv + skip_ref[2:3, :] * x[...].astype(f32)
            for r in range(count):
                rows = piece(place_ref, r, local_len)
                grad_out[rows, :] = (cot[r][...].astype(f32) * inner_out[rows, :]).astype(bf16)

    by_row, by_col = table_specs(length, block)
    cols = pl.BlockSpec((local_len, width), lambda i, place_ref: (0, place_ref[0]))
    return pl.pallas_call(
        body,
        grid_spec=pltpu.PrefetchScalarGridSpec(
            num_scalar_prefetch=1,
            grid=(length // block,),
            in_specs=[cols] * count
            + [whole((local_len, width))] * count
            + [spectrum_block(width, block), by_row, by_row, by_col]
            + [whole(rows_of.shape)],
            out_specs=[
                spectrum_block(width, block),
                whole((length, width)),
                whole((length, width)),
            ],
            scratch_shapes=[VMEM((length, width), bf16), VMEM((length, width), f32)],
        ),
        out_shape=[
            struct((2, length, width), f32),
            struct((length, width), f32),
            struct((length, width), bf16),
        ],
        name="convolve",
        compiler_params=grant(
            [((6, block, length), 2), ((4, block, width), 4), ((3, length, width), 4)], length, width
        ),
    )(place, *signal_rel, *cot_rel, filt_spec, a_high, a_low, t_high, rows_of)


def grant(blocks, length, width):
    held = sum(math.prod(shape) * size for shape, size in blocks)
    need = 2 * held + 8 * length * width * 4 + (4 << 20)
    return pltpu.CompilerParams(vmem_limit_bytes=min(need, 60 << 20))


def smem():
    return pl.BlockSpec(memory_space=pltpu.SMEM)


def weight_grads(place, signal_rel, gate_grad, groups):
    count = len(signal_rel)
    local_len, channels = signal_rel[0].shape
    width = gate_grad.shape[1]
    rows = channels // sum(len(group) for group in groups)
    length = local_len * count

    def body(place_ref, *refs):
        sig = refs[:count]
        grad = refs[count]
        outs = refs[count + 1 :]
        right = jnp.concatenate(
            [grad[piece(place_ref, r, local_len), :] for r in range(count)], axis=0
        )
        for out, group in zip(outs, groups):
            for at, k in enumerate(group):
                start = pl.multiple_of((place_ref[1] ^ k) * rows, rows)
                left = jnp.concatenate(
                    [sig[r][:, pl.ds(start, rows)] for r in range(count)], axis=0
                )
                out[at] = dot_first(left, right).astype(bf16)

    return pl.pallas_call(
        body,
        in_specs=[smem()] + [pl.BlockSpec(memory_space=VMEM)] * (count + 1),
        out_specs=[pl.BlockSpec(memory_space=VMEM)] * len(groups),
        out_shape=[struct((len(group), rows, width), bf16) for group in groups],
        name="weight_grads",
        compiler_params=grant([((length, channels), 2), ((2, channels, width), 2)], length, width),
    )(place, *signal_rel, gate_grad)


def gating(place, signal_rel, weight_rel, cot_rel, inner):
    count = len(signal_rel)
    dp_count = len(weight_rel)
    local_len, channels = signal_rel[0].shape
    rows, width = weight_rel[0].shape
    length = local_len * count

    def body(place_ref, *refs):
        sig = refs[:count]
        weight = refs[count : count + dp_count]
        cot = refs[count + dp_count : 2 * count + dp_count]
        inner_ref = refs[2 * count + dp_count]
        outs = refs[2 * count + dp_count + 1 : -1]
        full = refs[-1]
        inner_grad_out, conv_grad_out, skip_out = outs[count:]
        for k in range(dp_count):
            start = pl.multiple_of((place_ref[1] ^ k) * rows, rows)
            full[pl.ds(start, rows), :] = weight[k][...]
        left = jnp.concatenate([sig[r][...] for r in range(count)], axis=0)
        gates = dot(left, full[...])
        skip_sum = jnp.zeros((1, width), f32)
        own = pl.multiple_of(place_ref[0] * width, width)
        for r in range(count):
            here = piece(place_ref, r, local_len)
            gate = gates[r * local_len : (r + 1) * local_len]
            outs[r][...] = (gate * inner_ref[here, :]).astype(bf16)
            inner_grad = cot[r][...].astype(f32) * gate
            inner_grad_out[here, :] = inner_grad
            conv_grad_out[here, :] = inner_grad.astype(bf16)
            signal = sig[r][:, pl.ds(own, width)].astype(f32)
            skip_sum += jnp.sum(inner_grad * signal, axis=0, keepdims=True)
        skip_out[...] = jnp.broadcast_to(skip_sum, (8, width))

    return pl.pallas_call(
        body,
        in_specs=[smem()] + [pl.BlockSpec(memory_space=VMEM)] * (2 * count + dp_count + 1),
        out_specs=[pl.BlockSpec(memory_space=VMEM)] * (count + 3),
        out_shape=[struct((local_len, width), bf16)] * count
        + [
            struct((length, width), f32),
            struct((length, width), bf16),
            struct((8, width), f32),
        ],
        scratch_shapes=[VMEM((channels, width), bf16)],
        name="gating",
        compiler_params=grant([((length, channels), 2), ((2, channels, width), 2)], length, width),
    )(place, *signal_rel, *weight_rel, *cot_rel, inner)


def packed_rows(order, table_rows, width):
    per_group = width // order
    groups = -(-(table_rows // 8) // per_group)
    return order + 8 + 8 * groups, per_group


def correlate_back(place, conv_grad, inner_grad, filt_spec, tables, rows_of, block):
    a_high, a_low, t_high = tables
    length, width = conv_grad.shape

    def body(place_ref, cg, ig, fs, ah, al, th, skip_ref, direct_out, spec, back):
        step = pl.program_id(0)
        re = to_spectrum(ah, al, 0, cg[...])
        im = to_spectrum(ah, al, 1, cg[...])
        spec[0] = re
        spec[1] = im
        term = from_spectrum(th, fs[0] * re + fs[1] * im, fs[0] * im - fs[1] * re, length)

        @pl.when(step == 0)
        def _():
            back[...] = term

        @pl.when(step != 0)
        def _():
            back[...] += term

        @pl.when(step == pl.num_programs(0) - 1)
        def _():
            direct_out[...] = ig[...] * skip_ref[2:3, :] + back[...].astype(bf16).astype(f32)

    by_row, by_col = table_specs(length, block)
    spec_block = spectrum_block(width, block)
    return pl.pallas_call(
        body,
        grid_spec=pltpu.PrefetchScalarGridSpec(
            num_scalar_prefetch=1,
            grid=(length // block,),
            in_specs=[
                whole((length, width)),
                whole((length, width)),
                spec_block,
                by_row,
                by_row,
                by_col,
                whole(rows_of.shape),
            ],
            out_specs=[whole((length, width)), spec_block],
            scratch_shapes=[VMEM((length, width), f32)],
        ),
        out_shape=[struct((length, width), f32), struct((2, length, width), f32)],
        name="correlate_back",
        compiler_params=grant(
            [((6, block, length), 2), ((4, block, width), 4), ((3, length, width), 4)], length, width
        ),
    )(place, conv_grad, inner_grad, filt_spec, a_high, a_low, t_high, rows_of)


def correlate_part(
    place, grad_spec, skip_sum, signal_spec, tables, env, hidden, filter_weight, cos_pre, table,
    block,
):
    t_high = tables[2]
    length, width = env.shape
    order = filter_weight.shape[0]
    feature_start = constant_rows(length)[8]
    table_rows = table.shape[0] - feature_start
    total_rows, per_group = packed_rows(order, table_rows, width)

    def body(
        place_ref, gs, skip_sum_ref, ss, th, env_ref, hid, fw, cp, tab, packed, part,
    ):
        step = pl.program_id(0)
        term = from_spectrum(
            th, ss[0] * gs[0] + ss[1] * gs[1], ss[0] * gs[1] - ss[1] * gs[0], length
        )

        @pl.when(step == 0)
        def _():
            part[...] = term

        @pl.when(step != 0)
        def _():
            part[...] += term

        @pl.when(step == pl.num_programs(0) - 1)
        def _():
            pre_grad = part[...].astype(bf16).astype(f32) * env_ref[...]
            packed[...] = jnp.zeros((total_rows, width), f32)
            packed[:order, :] = careful(dot_first, hid[...], pre_grad)
            packed[order : order + 8, :] = skip_sum_ref[...]
            act = careful(dot_last, pre_grad, fw[...]) * cp[...]
            small = careful(dot, tab[feature_start:, :], act)
            for b in range(table_rows // 8):
                row = order + 8 + 8 * (b // per_group)
                col = order * (b % per_group)
                packed[row : row + 8, col : col + order] = small[8 * b : 8 * b + 8]

    _, by_col = table_specs(length, block)
    spec_block = spectrum_block(width, block)
    return pl.pallas_call(
        body,
        grid_spec=pltpu.PrefetchScalarGridSpec(
            num_scalar_prefetch=1,
            grid=(length // block,),
            in_specs=[
                spec_block,
                whole((8, width)),
                spec_block,
                by_col,
                whole((length, width)),
                whole(hidden.shape),
                pl.BlockSpec((order, width), lambda i, place_ref: (0, place_ref[0])),
                whole(cos_pre.shape),
                whole(table.shape),
            ],
            out_specs=whole((total_rows, width)),
            scratch_shapes=[VMEM((length, width), f32)],
        ),
        out_shape=struct((total_rows, width), f32),
        name="correlate_part",
        compiler_params=grant(
            [((2, block, length), 2), ((4, block, width), 4), ((2, length, width), 4)], length, width
        ),
    )(
        place, grad_spec, skip_sum, signal_spec, t_high, env, hidden, filter_weight, cos_pre,
        table,
    )


def through_gate(place, gate_grad, weight_rel, direct, count):
    dp_count = len(weight_rel)
    rows, width = weight_rel[0].shape
    length = gate_grad.shape[0]
    local_len = length // count
    channels = rows * dp_count

    def body(place_ref, *refs):
        grad = refs[0]
        weight = refs[1 : 1 + dp_count]
        direct_ref = refs[1 + dp_count]
        outs = refs[2 + dp_count :]
        left = jnp.concatenate(
            [grad[piece(place_ref, r, local_len), :] for r in range(count)], axis=0
        )
        for k in range(dp_count):
            start = pl.multiple_of((place_ref[1] ^ k) * rows, rows)
            shift = start - place_ref[0] * width
            inside = jnp.logical_and(shift >= 0, shift < width)
            shift = pl.multiple_of(jnp.clip(shift, 0, width - rows), rows)
            scale = jnp.where(inside, 1.0, 0.0).astype(f32)
            terms = dot_last(left, weight[k][...])
            for r in range(count):
                term = terms[r * local_len : (r + 1) * local_len]
                term += scale * direct_ref[piece(place_ref, r, local_len), pl.ds(shift, rows)]
                outs[r][:, pl.ds(start, rows)] = term.astype(bf16)

    return pl.pallas_call(
        body,
        in_specs=[smem()] + [pl.BlockSpec(memory_space=VMEM)] * (dp_count + 2),
        out_specs=[pl.BlockSpec(memory_space=VMEM)] * count,
        out_shape=[struct((local_len, channels), bf16)] * count,
        name="through_gate",
        compiler_params=grant([((length, channels), 2), ((channels, width), 2)], length, width),
    )(place, gate_grad, *weight_rel, direct)


def assemble(place, pieces, kind):
    count = len(pieces)
    rows, width = pieces[0].shape

    def body(place_ref, *refs):
        out = refs[count]
        for r in range(count):
            start = pl.multiple_of((place_ref[0] ^ r) * width, width)
            out[:, pl.ds(start, width)] = refs[r][...].astype(kind)

    return pl.pallas_call(
        body,
        in_specs=[smem()] + [pl.BlockSpec(memory_space=VMEM)] * count,
        out_specs=pl.BlockSpec(memory_space=VMEM),
        out_shape=struct((rows, width * count), kind),
        name="assemble",
        compiler_params=grant([((rows, 2 * width * count), 4)], rows, width),
    )(place, *pieces)


def finish(place, pieces, order, emb_count):
    count = len(pieces)
    rows, width = pieces[0].shape
    table_rows = 8 * (emb_count // 8 + 1)
    _, per_group = packed_rows(order, table_rows, width)

    def body(place_ref, *refs):
        filter_out, skip_out, pos_out, bias_out = refs[count:]
        for r in range(count):
            cols = pl.ds(pl.multiple_of((place_ref[0] ^ r) * width, width), width)
            values = refs[r][...].astype(f32)
            filter_out[:, cols] = values[:order, :]
            skip_out[:, cols] = values[order : order + 1, :]
        tails = [refs[r][...].astype(f32)[order + 8 :, :] for r in range(count)]
        while len(tails) > 1:
            tails = [tails[i] + tails[i + 1] for i in range(0, len(tails), 2)]
        for b in range(table_rows // 8):
            row = 8 * (b // per_group)
            col = order * (b % per_group)
            found = tails[0][row : row + 8, col : col + order]
            low = 8 * b
            high = min(low + 8, emb_count)
            if high > low:
                pos_out[low:high, :] = found[: high - low]
            if low <= emb_count < low + 8:
                bias_out[...] = found[emb_count - low : emb_count - low + 1]

    return pl.pallas_call(
        body,
        in_specs=[smem()] + [pl.BlockSpec(memory_space=VMEM)] * count,
        out_specs=[pl.BlockSpec(memory_space=VMEM)] * 4,
        out_shape=[
            struct((order, width * count), f32),
            struct((1, width * count), f32),
            struct((emb_count, order), f32),
            struct((1, order), f32),
        ],
        name="finish",
        compiler_params=grant([((rows, 2 * width * count), 4)], rows, width),
    )(place, *pieces)


def swap(value, axis, offset):
    count = lax.axis_size(axis)
    return lax.ppermute(value, axis, [(i, i ^ offset) for i in range(count)])


def gather_rel(own, axis):
    count = lax.axis_size(axis)
    found = {0: own}
    bit = count // 2
    while bit:
        for r in list(found):
            found[r | bit] = swap(found[r], axis, bit)
        bit //= 2
    return [found[r] for r in range(count)]


def add_round(*terms):
    total = terms[0].astype(f32)
    for term in terms[1:]:
        total = total + term.astype(f32)
    return total.astype(bf16)


def shards(
    signal, gate_weight, pos_weight, pos_bias, filter_weight, decay_rate, skip_gain, grad_out
):
    seq_count = lax.axis_size("seq")
    dp_count = lax.axis_size("dp")
    signal_tok = signal[0]
    cot_tok = grad_out[0]
    local_len, channels = signal_tok.shape
    length = local_len * seq_count
    width = channels // seq_count
    emb_count, order = pos_weight.shape
    seq_at = lax.axis_index("seq")
    dp_at = lax.axis_index("dp")
    place = jnp.stack([seq_at, dp_at]).astype(jnp.int32)
    block = min(256, length)

    def own_cols(x, r=0):
        return lax.dynamic_slice_in_dim(x, (seq_at ^ r) * width, width, axis=x.ndim - 1)

    signal_rel = gather_rel(signal_tok, "seq")
    weight_rel = {0: own_cols(gate_weight)}
    for k in range(2, dp_count, 2):
        weight_rel[k] = swap(weight_rel[0], "dp", k)
    for k in range(0, dp_count, 2):
        weight_rel[k + 1] = swap(weight_rel[k], "dp", 1)
    weight_rel = [weight_rel[k] for k in range(dp_count)]
    cot_rel = [own_cols(cot_tok)] + [
        swap(own_cols(cot_tok, r), "seq", r) for r in range(1, seq_count)
    ]

    table = jnp.asarray(constants(length, emb_count))
    rates = decay_rate[None]
    norm = jnp.sqrt(jnp.expm1(-2.0 * rates * length) / jnp.expm1(-2.0 * rates))
    rows_of = jnp.concatenate([rates, norm, skip_gain[None]])
    a_high, a_low, t_high, filt_spec, env, hidden, cos_pre, rows_of = generate(
        place, table, pos_weight, pos_bias[None], filter_weight, rows_of, width, block
    )
    tables = (a_high, a_low, t_high)

    signal_spec, inner, gate_grad = convolve(
        place, signal_rel, cot_rel, filt_spec, tables, rows_of, block
    )

    far = list(reversed(range(0, dp_count, 2)))
    pairs = stages(dp_count)
    groups = [[k + 1 for k in pair] for pair in pairs] + pairs
    weight_parts = weight_grads(place, signal_rel, gate_grad, groups)
    sums = {}
    for i, pair in enumerate(pairs):
        met = swap(weight_parts[i], "dp", 1)
        for at, k in enumerate(pair):
            sums[k] = add_round(weight_parts[len(pairs) + i][at], met[at])
    row_sum = add_round(sums[0], *[swap(sums[k], "dp", k) for k in far[:-1]])
    row_rel = gather_rel(row_sum, "seq")
    grad_gate_weight = assemble(place, row_rel, f32)

    gated = gating(place, signal_rel, weight_rel, cot_rel, inner)
    out_rel = gated[:seq_count]
    inner_grad, conv_grad, skip_sum = gated[seq_count:]
    out_rel = [out_rel[0]] + [swap(out_rel[r], "seq", r) for r in range(1, seq_count)]
    output = assemble(place, out_rel, bf16)

    direct, grad_spec = correlate_back(
        place, conv_grad, inner_grad, filt_spec, tables, rows_of, block
    )
    packed = correlate_part(
        place, grad_spec, skip_sum, signal_spec, tables, env, hidden, filter_weight, cos_pre,
        table, block,
    )
    back_rel = through_gate(place, gate_grad, weight_rel, direct, seq_count)

    live = {r: back_rel[r] for r in range(seq_count)}
    bit = 1
    while bit < seq_count:
        met = {r: swap(live[r | bit], "seq", bit) for r in live if not r & bit}
        live = {r: add_round(live[r], met[r]) for r in met}
        bit *= 2
    grad_signal = live[0][None]

    met = swap(packed, "dp", 1)
    packed = (packed + met).astype(bf16)
    terms = [packed] + [swap(packed, "dp", k) for k in range(2, dp_count, 2)]
    terms = [term.astype(f32) for term in terms]
    while len(terms) > 1:
        terms = [terms[i] + terms[i + 1] for i in range(0, len(terms), 2)]
    packed = terms[0].astype(bf16)
    packed_rel = [packed] + [swap(packed, "seq", r) for r in range(1, seq_count)]
    grad_filter_weight, grad_skip, grad_pos_weight, grad_pos_bias = finish(
        place, packed_rel, order, emb_count
    )
    return (
        output[None],
        grad_signal,
        grad_gate_weight,
        grad_pos_weight,
        grad_pos_bias[0],
        grad_filter_weight,
        grad_skip[0],
    )


def stages(dp_count):
    far = list(reversed(range(0, dp_count, 2)))
    return [[k] for k in far[:-2]] + [far[-2:]]


def solution(mesh):
    step = mapped(shards, mesh)
    return step


def mapped(body, mesh):
    return jax.shard_map(
        body,
        mesh=mesh,
        in_specs=(
            P("dp", "seq", None),
            P("dp", None),
            P(),
            P(),
            P(),
            P(),
            P(),
            P("dp", "seq", None),
        ),
        out_specs=(P("dp", "seq", None), P("dp", "seq", None), P("dp", None), P(), P(), P(), P()),
        check_vma=False,
    )
```

```python
import functools
import math

import jax
import jax.numpy as jnp
import numpy as np
from jax import lax
from jax.experimental import pallas as pl
from jax.experimental.pallas import tpu as pltpu
from jax.sharding import PartitionSpec as P


f32 = jnp.float32
bf16 = jnp.bfloat16
VMEM = pltpu.VMEM


BASE = 16


@functools.lru_cache(maxsize=None)
def constants(length, emb_count):
    step = 4 * length
    lane = np.arange(length)[None, :]
    coarse = np.arange(length // BASE)[:, None]
    fine = np.arange(BASE)[:, None]
    found = []
    for phase in (
        coarse * lane * (4 * BASE),
        (4 * fine + 1) * lane,
        coarse * BASE * (4 * lane + 1),
        fine * (4 * lane + 1),
    ):
        angle = phase % step * (2.0 * math.pi / step)
        found += [np.cos(angle), np.sin(angle)]
    bands = np.arange(1, (emb_count - 1) // 2 + 1)[:, None]
    angle = bands * lane % length * (2.0 * math.pi / length)
    rows = 8 * (emb_count // 8 + 1)
    found += [lane / length, np.cos(angle), np.sin(angle), np.ones((1, length))]
    found += [np.zeros((rows - emb_count - 1, length))]
    return np.concatenate(found).astype(np.float32)


def constant_rows(length):
    sizes = [length // BASE, length // BASE, BASE, BASE]
    starts = np.cumsum([0] + sizes + sizes).tolist()
    return starts


def dot(a, b):
    return jnp.dot(a, b, preferred_element_type=f32)


def dot_first(a, b):
    return lax.dot_general(a, b, (((0,), (0,)), ((), ())), preferred_element_type=f32)


def dot_last(a, b):
    return lax.dot_general(a, b, (((1,), (1,)), ((), ())), preferred_element_type=f32)


def split(x):
    high = x.astype(bf16)
    return high, (x - high.astype(f32)).astype(bf16)


def careful(product, a, b):
    a_high, a_low = split(a)
    b_high, b_low = split(b)
    return product(a_high, b_high) + (product(a_low, b_high) + product(a_high, b_low))


def to_spectrum(a_high, a_low, part, x):
    return dot(a_high[part], x) + dot(a_low[part], x)


def from_spectrum(t_high, re, im, length):
    total = dot(t_high[0], re.astype(bf16)) + dot(t_high[1], im.astype(bf16))
    return total * (1.0 / length)


def struct(shape, kind):
    return jax.ShapeDtypeStruct(shape, kind)


def whole(shape):
    return pl.BlockSpec(shape, lambda i, *_: (0,) * len(shape))


def table_specs(length, block):
    by_row = pl.BlockSpec((2, block, length), lambda i, *_: (0, i, 0))
    by_col = pl.BlockSpec((2, length, block), lambda i, *_: (0, 0, i))
    return by_row, by_col


def spectrum_block(width, block):
    return pl.BlockSpec((2, block, width), lambda i, *_: (0, i, 0))


def generate(place, table, pos_weight, pos_bias, filter_weight, rows_of, width, block):
    highest = lax.Precision.HIGHEST
    length = table.shape[1]
    emb_count, order = pos_weight.shape
    starts = constant_rows(length)

    def body(place_ref, *refs):
        sources = refs[:5]
        ah, al, th, spec, env_out, hidden_out, cos_out, rows_out, filt, *held, done = refs[5:]
        tab, pw, pb, fw, vec = held
        step = pl.program_id(0)

        @pl.when(step == 0)
        def _():
            mine = pl.ds(pl.multiple_of(place_ref[0] * width, width), width)
            copies = [
                pltpu.make_async_copy(
                    source if i < 3 else source.at[:, mine], target, done.at[i]
                )
                for i, (source, target) in enumerate(zip(sources, held))
            ]
            for copy in copies:
                copy.start()
            for copy in copies:
                copy.wait()
            rows_out[...] = vec[...]
            feat = tab[starts[8] : starts[8] + emb_count, :]
            pre = pb[...] + lax.dot_general(
                feat, pw[...], (((0,), (0,)), ((), ())), precision=highest,
                preferred_element_type=f32,
            )
            hidden = jnp.sin(pre)
            hidden_out[...] = hidden
            cos_out[...] = jnp.cos(pre)
            at = lax.broadcasted_iota(jnp.int32, (length, width), 0).astype(f32)
            env = jnp.exp(-vec[0:1, :] * at) * (1.0 / vec[1:2, :])
            env_out[...] = env
            filt[...] = (jnp.dot(hidden, fw[...], precision=highest) * env).astype(bf16)

        def rows(at, store):
            cos_start, sin_start, fine_cos, fine_sin = starts[at : at + 4]
            cos_fine = tab[fine_cos : fine_cos + BASE, :]
            sin_fine = tab[fine_sin : fine_sin + BASE, :]

            def one(i, carry):
                here = step * (block // BASE) + i
                out = pl.ds(pl.multiple_of(i * BASE, BASE), BASE)
                cos = tab[pl.ds(cos_start + here, 1), :]
                sin = tab[pl.ds(sin_start + here, 1), :]
                store(out, 0, cos * cos_fine - sin * sin_fine)
                store(out, 1, sin * cos_fine + cos * sin_fine)
                return carry

            lax.fori_loop(0, block // BASE, one, 0, unroll=4)

        def store_both(out, part, value):
            high, low = split(value)
            ah[part, out, :] = high
            al[part, out, :] = low

        def store_high(out, part, value):
            th[part, out, :] = value.astype(bf16)

        rows(0, store_both)
        rows(4, store_high)
        spec[0] = to_spectrum(ah, al, 0, filt[...])
        spec[1] = to_spectrum(ah, al, 1, filt[...])

    by_row = pl.BlockSpec((2, block, length), lambda i, *_: (0, i, 0))
    return pl.pallas_call(
        body,
        grid_spec=pltpu.PrefetchScalarGridSpec(
            num_scalar_prefetch=1,
            grid=(length // block,),
            in_specs=[pl.BlockSpec(memory_space=pltpu.HBM)] * 5,
            out_specs=[by_row, by_row, by_row, spectrum_block(width, block)]
            + [whole((length, width)), whole((length, order)), whole((length, order))]
            + [whole((rows_of.shape[0], width))],
            scratch_shapes=[VMEM((length, width), bf16)]
            + [VMEM(x.shape, f32) for x in (table, pos_weight, pos_bias)]
            + [VMEM((order, width), f32), VMEM((rows_of.shape[0], width), f32)]
            + [pltpu.SemaphoreType.DMA((5,))],
        ),
        out_shape=[struct((2, length, length), bf16)] * 3
        + [struct((2, length, width), f32), struct((length, width), f32)]
        + [struct((length, order), f32)] * 2
        + [struct((rows_of.shape[0], width), f32)],
        name="generate",
        compiler_params=grant(
            [((6, block, length), 2), ((4, block, width), 4), ((2, length, width), 4)]
            + [(table.shape, 4)], length, width
        ),
    )(
        place,
        *[
            pltpu.with_memory_space_constraint(x, pltpu.HBM)
            for x in (table, pos_weight, pos_bias, filter_weight, rows_of)
        ],
    )


def piece(place_ref, r, rows):
    return pl.ds(pl.multiple_of((place_ref[0] ^ r) * rows, rows), rows)


def convolve(place, signal_rel, cot_rel, filt_spec, tables, rows_of, block):
    a_high, a_low, t_high = tables
    count = len(signal_rel)
    local_len, width = cot_rel[0].shape
    length = local_len * count

    def body(place_ref, *refs):
        sig = refs[:count]
        cot = refs[count : 2 * count]
        fs, ah, al, th, skip_ref = refs[2 * count : 2 * count + 5]
        spec, inner_out, grad_out, x, acc = refs[2 * count + 5 :]
        step = pl.program_id(0)

        @pl.when(step == 0)
        def _():
            for r in range(count):
                x[piece(place_ref, r, local_len), :] = sig[r][...]

        re = to_spectrum(ah, al, 0, x[...])
        im = to_spectrum(ah, al, 1, x[...])
        spec[0] = re
        spec[1] = im
        part = from_spectrum(th, re * fs[0] - im * fs[1], re * fs[1] + im * fs[0], length)

        @pl.when(step == 0)
        def _():
            acc[...] = part

        @pl.when(step != 0)
        def _():
            acc[...] += part

        @pl.when(step == pl.num_programs(0) - 1)
        def _():
            conv = acc[...].astype(bf16).astype(f32)
            inner_out[...] = conv + skip_ref[2:3, :] * x[...].astype(f32)
            for r in range(count):
                rows = piece(place_ref, r, local_len)
                grad_out[rows, :] = (cot[r][...].astype(f32) * inner_out[rows, :]).astype(bf16)

    by_row, by_col = table_specs(length, block)
    cols = pl.BlockSpec((local_len, width), lambda i, place_ref: (0, place_ref[0]))
    return pl.pallas_call(
        body,
        grid_spec=pltpu.PrefetchScalarGridSpec(
            num_scalar_prefetch=1,
            grid=(length // block,),
            in_specs=[cols] * count
            + [whole((local_len, width))] * count
            + [spectrum_block(width, block), by_row, by_row, by_col]
            + [whole(rows_of.shape)],
            out_specs=[
                spectrum_block(width, block),
                whole((length, width)),
                whole((length, width)),
            ],
            scratch_shapes=[VMEM((length, width), bf16), VMEM((length, width), f32)],
        ),
        out_shape=[
            struct((2, length, width), f32),
            struct((length, width), f32),
            struct((length, width), bf16),
        ],
        name="convolve",
        compiler_params=grant(
            [((6, block, length), 2), ((4, block, width), 4), ((3, length, width), 4)], length, width
        ),
    )(place, *signal_rel, *cot_rel, filt_spec, a_high, a_low, t_high, rows_of)


def grant(blocks, length, width):
    held = sum(math.prod(shape) * size for shape, size in blocks)
    need = 2 * held + 8 * length * width * 4 + (4 << 20)
    return pltpu.CompilerParams(vmem_limit_bytes=min(need, 60 << 20))


def smem():
    return pl.BlockSpec(memory_space=pltpu.SMEM)


def weight_grads(place, signal_rel, gate_grad, groups):
    count = len(signal_rel)
    local_len, channels = signal_rel[0].shape
    width = gate_grad.shape[1]
    rows = channels // sum(len(group) for group in groups)
    length = local_len * count

    def body(place_ref, *refs):
        sig = refs[:count]
        grad = refs[count]
        outs = refs[count + 1 :]
        right = jnp.concatenate(
            [grad[piece(place_ref, r, local_len), :] for r in range(count)], axis=0
        )
        for out, group in zip(outs, groups):
            for at, k in enumerate(group):
                start = pl.multiple_of((place_ref[1] ^ k) * rows, rows)
                left = jnp.concatenate(
                    [sig[r][:, pl.ds(start, rows)] for r in range(count)], axis=0
                )
                out[at] = dot_first(left, right).astype(bf16)

    return pl.pallas_call(
        body,
        in_specs=[smem()] + [pl.BlockSpec(memory_space=VMEM)] * (count + 1),
        out_specs=[pl.BlockSpec(memory_space=VMEM)] * len(groups),
        out_shape=[struct((len(group), rows, width), bf16) for group in groups],
        name="weight_grads",
        compiler_params=grant([((length, channels), 2), ((2, channels, width), 2)], length, width),
    )(place, *signal_rel, gate_grad)


def gating(place, signal_rel, weight_rel, cot_rel, inner):
    count = len(signal_rel)
    dp_count = len(weight_rel)
    local_len, channels = signal_rel[0].shape
    rows, width = weight_rel[0].shape
    length = local_len * count

    def body(place_ref, *refs):
        sig = refs[:count]
        weight = refs[count : count + dp_count]
        cot = refs[count + dp_count : 2 * count + dp_count]
        inner_ref = refs[2 * count + dp_count]
        outs = refs[2 * count + dp_count + 1 : -1]
        full = refs[-1]
        out, inner_grad_out, conv_grad_out, skip_out = outs
        for k in range(dp_count):
            start = pl.multiple_of((place_ref[1] ^ k) * rows, rows)
            full[pl.ds(start, rows), :] = weight[k][...]
        left = jnp.concatenate([sig[r][...] for r in range(count)], axis=0)
        gates = dot(left, full[...])
        skip_sum = jnp.zeros((1, width), f32)
        own = pl.multiple_of(place_ref[0] * width, width)
        for r in range(count):
            here = piece(place_ref, r, local_len)
            gate = gates[r * local_len : (r + 1) * local_len]
            out[here, :] = (gate * inner_ref[here, :]).astype(bf16)
            inner_grad = cot[r][...].astype(f32) * gate
            inner_grad_out[here, :] = inner_grad
            conv_grad_out[here, :] = inner_grad.astype(bf16)
            signal = sig[r][:, pl.ds(own, width)].astype(f32)
            skip_sum += jnp.sum(inner_grad * signal, axis=0, keepdims=True)
        skip_out[...] = jnp.broadcast_to(skip_sum, (8, width))

    return pl.pallas_call(
        body,
        in_specs=[smem()] + [pl.BlockSpec(memory_space=VMEM)] * (2 * count + dp_count + 1),
        out_specs=[pl.BlockSpec(memory_space=VMEM)] * 4,
        out_shape=[
            struct((length, width), bf16),
            struct((length, width), f32),
            struct((length, width), bf16),
            struct((8, width), f32),
        ],
        scratch_shapes=[VMEM((channels, width), bf16)],
        name="gating",
        compiler_params=grant([((length, channels), 2), ((2, channels, width), 2)], length, width),
    )(place, *signal_rel, *weight_rel, *cot_rel, inner)


def packed_rows(order, table_rows, width):
    per_group = width // order
    groups = -(-(table_rows // 8) // per_group)
    return order + 8 + 8 * groups, per_group


def correlate_back(
    place, out, conv_grad, inner_grad, filt_spec, tables, rows_of, count, block
):
    a_high, a_low, t_high = tables
    length, width = conv_grad.shape
    local_len = length // count

    def body(place_ref, out_ref, cg, ig, fs, ah, al, th, skip_ref, *refs):
        pieces = refs[:count]
        spec, back = refs[count:]
        step = pl.program_id(0)
        re = to_spectrum(ah, al, 0, cg[...])
        im = to_spectrum(ah, al, 1, cg[...])
        spec[0] = re
        spec[1] = im
        term = from_spectrum(th, fs[0] * re + fs[1] * im, fs[0] * im - fs[1] * re, length)

        @pl.when(step == 0)
        def _():
            back[...] = term

        @pl.when(step != 0)
        def _():
            back[...] += term

        @pl.when(step == pl.num_programs(0) - 1)
        def _():
            for r in range(count):
                rows = piece(place_ref, r, local_len)
                direct = ig[rows, :] * skip_ref[2:3, :]
                pieces[r][0] = out_ref[rows, :]
                pieces[r][1] = (direct + back[rows, :].astype(bf16).astype(f32)).astype(bf16)

    by_row, by_col = table_specs(length, block)
    spec_block = spectrum_block(width, block)
    return pl.pallas_call(
        body,
        grid_spec=pltpu.PrefetchScalarGridSpec(
            num_scalar_prefetch=1,
            grid=(length // block,),
            in_specs=[
                whole((length, width)),
                whole((length, width)),
                whole((length, width)),
                spec_block,
                by_row,
                by_row,
                by_col,
                whole(rows_of.shape),
            ],
            out_specs=[whole((2, local_len, width))] * count + [spec_block],
            scratch_shapes=[VMEM((length, width), f32)],
        ),
        out_shape=[struct((2, local_len, width), bf16)] * count
        + [struct((2, length, width), f32)],
        name="correlate_back",
        compiler_params=grant(
            [((6, block, length), 2), ((4, block, width), 4), ((3, length, width), 4)], length, width
        ),
    )(place, out, conv_grad, inner_grad, filt_spec, a_high, a_low, t_high, rows_of)


def correlate_part(
    place, grad_spec, skip_sum, signal_spec, tables, env, hidden, filter_weight, cos_pre, table,
    block,
):
    t_high = tables[2]
    length, width = env.shape
    order = filter_weight.shape[0]
    feature_start = constant_rows(length)[8]
    table_rows = table.shape[0] - feature_start
    total_rows, per_group = packed_rows(order, table_rows, width)

    def body(
        place_ref, gs, skip_sum_ref, ss, th, env_ref, hid, fw, cp, tab, packed, part,
    ):
        step = pl.program_id(0)
        term = from_spectrum(
            th, ss[0] * gs[0] + ss[1] * gs[1], ss[0] * gs[1] - ss[1] * gs[0], length
        )

        @pl.when(step == 0)
        def _():
            part[...] = term

        @pl.when(step != 0)
        def _():
            part[...] += term

        @pl.when(step == pl.num_programs(0) - 1)
        def _():
            pre_grad = part[...].astype(bf16).astype(f32) * env_ref[...]
            packed[...] = jnp.zeros((total_rows, width), f32)
            packed[:order, :] = careful(dot_first, hid[...], pre_grad)
            packed[order : order + 8, :] = skip_sum_ref[...]
            act = careful(dot_last, pre_grad, fw[...]) * cp[...]
            small = careful(dot, tab[feature_start:, :], act)
            for b in range(table_rows // 8):
                row = order + 8 + 8 * (b // per_group)
                col = order * (b % per_group)
                packed[row : row + 8, col : col + order] = small[8 * b : 8 * b + 8]

    _, by_col = table_specs(length, block)
    spec_block = spectrum_block(width, block)
    return pl.pallas_call(
        body,
        grid_spec=pltpu.PrefetchScalarGridSpec(
            num_scalar_prefetch=1,
            grid=(length // block,),
            in_specs=[
                spec_block,
                whole((8, width)),
                spec_block,
                by_col,
                whole((length, width)),
                whole(hidden.shape),
                pl.BlockSpec((order, width), lambda i, place_ref: (0, place_ref[0])),
                whole(cos_pre.shape),
                whole(table.shape),
            ],
            out_specs=whole((total_rows, width)),
            scratch_shapes=[VMEM((length, width), f32)],
        ),
        out_shape=struct((total_rows, width), f32),
        name="correlate_part",
        compiler_params=grant(
            [((2, block, length), 2), ((4, block, width), 4), ((2, length, width), 4)], length, width
        ),
    )(
        place, grad_spec, skip_sum, signal_spec, t_high, env, hidden, filter_weight, cos_pre,
        table,
    )


def through_gate(place, gate_grad, weight_rel, count):
    dp_count = len(weight_rel)
    rows, width = weight_rel[0].shape
    length = gate_grad.shape[0]
    local_len = length // count
    channels = rows * dp_count

    def body(place_ref, *refs):
        grad = refs[0]
        weight = refs[1 : 1 + dp_count]
        outs = refs[1 + dp_count :]
        left = jnp.concatenate(
            [grad[piece(place_ref, r, local_len), :] for r in range(count)], axis=0
        )
        for k in range(dp_count):
            start = pl.multiple_of((place_ref[1] ^ k) * rows, rows)
            terms = dot_last(left, weight[k][...])
            for r in range(count):
                term = terms[r * local_len : (r + 1) * local_len]
                outs[r][:, pl.ds(start, rows)] = term.astype(bf16)

    return pl.pallas_call(
        body,
        in_specs=[smem()] + [pl.BlockSpec(memory_space=VMEM)] * (dp_count + 1),
        out_specs=[pl.BlockSpec(memory_space=VMEM)] * count,
        out_shape=[struct((local_len, channels), bf16)] * count,
        name="through_gate",
        compiler_params=grant([((length, channels), 2), ((channels, width), 2)], length, width),
    )(place, gate_grad, *weight_rel)


def combine(place, pieces, near_part, far_part):
    count = len(pieces)
    _, rows, width = pieces[0].shape

    def body(place_ref, *refs):
        near, far, out, grad = refs[count:]
        for r in range(count):
            cols = pl.ds(pl.multiple_of((place_ref[0] ^ r) * width, width), width)
            out[:, cols] = refs[r][0]
            total = near[:, cols].astype(f32) + far[:, cols].astype(f32)
            grad[:, cols] = (total + refs[r][1].astype(f32)).astype(bf16)

    return pl.pallas_call(
        body,
        in_specs=[smem()] + [pl.BlockSpec(memory_space=VMEM)] * (count + 2),
        out_specs=[pl.BlockSpec(memory_space=VMEM)] * 2,
        out_shape=[struct((rows, width * count), bf16)] * 2,
        name="combine",
        compiler_params=grant([((rows, 6 * width * count), 2)], rows, width),
    )(place, *pieces, near_part, far_part)


def assemble(place, pieces, kind):
    count = len(pieces)
    rows, width = pieces[0].shape

    def body(place_ref, *refs):
        out = refs[count]
        for r in range(count):
            start = pl.multiple_of((place_ref[0] ^ r) * width, width)
            out[:, pl.ds(start, width)] = refs[r][...].astype(kind)

    return pl.pallas_call(
        body,
        in_specs=[smem()] + [pl.BlockSpec(memory_space=VMEM)] * count,
        out_specs=pl.BlockSpec(memory_space=VMEM),
        out_shape=struct((rows, width * count), kind),
        name="assemble",
        compiler_params=grant([((rows, 2 * width * count), 4)], rows, width),
    )(place, *pieces)


def finish(place, pieces, order, emb_count):
    count = len(pieces)
    rows, width = pieces[0].shape
    table_rows = 8 * (emb_count // 8 + 1)
    _, per_group = packed_rows(order, table_rows, width)

    def body(place_ref, *refs):
        filter_out, skip_out, pos_out, bias_out = refs[count:]
        for r in range(count):
            cols = pl.ds(pl.multiple_of((place_ref[0] ^ r) * width, width), width)
            values = refs[r][...].astype(f32)
            filter_out[:, cols] = values[:order, :]
            skip_out[:, cols] = values[order : order + 1, :]
        tails = [refs[r][...].astype(f32)[order + 8 :, :] for r in range(count)]
        while len(tails) > 1:
            tails = [tails[i] + tails[i + 1] for i in range(0, len(tails), 2)]
        for b in range(table_rows // 8):
            row = 8 * (b // per_group)
            col = order * (b % per_group)
            found = tails[0][row : row + 8, col : col + order]
            low = 8 * b
            high = min(low + 8, emb_count)
            if high > low:
                pos_out[low:high, :] = found[: high - low]
            if low <= emb_count < low + 8:
                bias_out[...] = found[emb_count - low : emb_count - low + 1]

    return pl.pallas_call(
        body,
        in_specs=[smem()] + [pl.BlockSpec(memory_space=VMEM)] * count,
        out_specs=[pl.BlockSpec(memory_space=VMEM)] * 4,
        out_shape=[
            struct((order, width * count), f32),
            struct((1, width * count), f32),
            struct((emb_count, order), f32),
            struct((1, order), f32),
        ],
        name="finish",
        compiler_params=grant([((rows, 2 * width * count), 4)], rows, width),
    )(place, *pieces)


def swap(value, axis, offset):
    count = lax.axis_size(axis)
    return lax.ppermute(value, axis, [(i, i ^ offset) for i in range(count)])


def gather_rel(own, axis):
    count = lax.axis_size(axis)
    found = {0: own}
    bit = count // 2
    while bit:
        for r in list(found):
            found[r | bit] = swap(found[r], axis, bit)
        bit //= 2
    return [found[r] for r in range(count)]


def add_round(*terms):
    total = terms[0].astype(f32)
    for term in terms[1:]:
        total = total + term.astype(f32)
    return total.astype(bf16)


def shards(
    signal, gate_weight, pos_weight, pos_bias, filter_weight, decay_rate, skip_gain, grad_out
):
    seq_count = lax.axis_size("seq")
    dp_count = lax.axis_size("dp")
    signal_tok = signal[0]
    cot_tok = grad_out[0]
    local_len, channels = signal_tok.shape
    length = local_len * seq_count
    width = channels // seq_count
    emb_count, order = pos_weight.shape
    seq_at = lax.axis_index("seq")
    dp_at = lax.axis_index("dp")
    place = jnp.stack([seq_at, dp_at]).astype(jnp.int32)
    block = min(256, length)

    def own_cols(x, r=0):
        return lax.dynamic_slice_in_dim(x, (seq_at ^ r) * width, width, axis=x.ndim - 1)

    signal_rel = gather_rel(signal_tok, "seq")
    weight_rel = {0: own_cols(gate_weight)}
    for k in range(2, dp_count, 2):
        weight_rel[k] = swap(weight_rel[0], "dp", k)
    for k in range(0, dp_count, 2):
        weight_rel[k + 1] = swap(weight_rel[k], "dp", 1)
    weight_rel = [weight_rel[k] for k in range(dp_count)]
    cot_rel = [own_cols(cot_tok)] + [
        swap(own_cols(cot_tok, r), "seq", r) for r in range(1, seq_count)
    ]

    table = jnp.asarray(constants(length, emb_count))
    rates = decay_rate[None]
    norm = jnp.sqrt(jnp.expm1(-2.0 * rates * length) / jnp.expm1(-2.0 * rates))
    rows_of = jnp.concatenate([rates, norm, skip_gain[None]])
    a_high, a_low, t_high, filt_spec, env, hidden, cos_pre, rows_of = generate(
        place, table, pos_weight, pos_bias[None], filter_weight, rows_of, width, block
    )
    tables = (a_high, a_low, t_high)

    signal_spec, inner, gate_grad = convolve(
        place, signal_rel, cot_rel, filt_spec, tables, rows_of, block
    )

    far = list(reversed(range(0, dp_count, 2)))
    pairs = stages(dp_count)
    groups = [[k + 1 for k in pair] for pair in pairs] + pairs
    weight_parts = weight_grads(place, signal_rel, gate_grad, groups)
    sums = {}
    for i, pair in enumerate(pairs):
        met = swap(weight_parts[i], "dp", 1)
        for at, k in enumerate(pair):
            sums[k] = add_round(weight_parts[len(pairs) + i][at], met[at])
    row_sum = add_round(sums[0], *[swap(sums[k], "dp", k) for k in far[:-1]])
    row_rel = gather_rel(row_sum, "seq")
    grad_gate_weight = assemble(place, row_rel, f32)

    back_rel = through_gate(place, gate_grad, weight_rel, seq_count)
    live = {r: back_rel[r] for r in range(seq_count)}
    bit = 1
    while bit < seq_count:
        met = {r: swap(live[r | bit], "seq", bit) for r in live if not r & bit}
        bit *= 2
        if bit < seq_count:
            live = {r: add_round(live[r], met[r]) for r in met}

    out, inner_grad, conv_grad, skip_sum = gating(
        place, signal_rel, weight_rel, cot_rel, inner
    )
    *pieces, grad_spec = correlate_back(
        place, out, conv_grad, inner_grad, filt_spec, tables, rows_of, seq_count, block
    )
    pieces = [pieces[0]] + [swap(pieces[r], "seq", r) for r in range(1, seq_count)]
    packed = correlate_part(
        place, grad_spec, skip_sum, signal_spec, tables, env, hidden, filter_weight, cos_pre,
        table, block,
    )
    output, grad_signal = combine(place, pieces, live[0], met[0])

    met = swap(packed, "dp", 1)
    packed = (packed + met).astype(bf16)
    terms = [packed] + [swap(packed, "dp", k) for k in range(2, dp_count, 2)]
    terms = [term.astype(f32) for term in terms]
    while len(terms) > 1:
        terms = [terms[i] + terms[i + 1] for i in range(0, len(terms), 2)]
    packed = terms[0].astype(bf16)
    packed_rel = [packed] + [swap(packed, "seq", r) for r in range(1, seq_count)]
    grad_filter_weight, grad_skip, grad_pos_weight, grad_pos_bias = finish(
        place, packed_rel, order, emb_count
    )
    return (
        output[None],
        grad_signal[None],
        grad_gate_weight,
        grad_pos_weight,
        grad_pos_bias[0],
        grad_filter_weight,
        grad_skip[0],
    )


def stages(dp_count):
    far = list(reversed(range(0, dp_count, 2)))
    return [[k] for k in far[:-2]] + [far[-2:]]


def solution(mesh):
    step = mapped(shards, mesh)
    return step


def mapped(body, mesh):
    return jax.shard_map(
        body,
        mesh=mesh,
        in_specs=(
            P("dp", "seq", None),
            P("dp", None),
            P(),
            P(),
            P(),
            P(),
            P(),
            P("dp", "seq", None),
        ),
        out_specs=(P("dp", "seq", None), P("dp", "seq", None), P("dp", None), P(), P(), P(), P()),
        check_vma=False,
    )
```

```python
import functools
import math

import jax
import jax.numpy as jnp
import numpy as np
from jax import lax
from jax.experimental import pallas as pl
from jax.experimental.pallas import tpu as pltpu
from jax.sharding import PartitionSpec as P


f32 = jnp.float32
bf16 = jnp.bfloat16
VMEM = pltpu.VMEM


BASE = 16


@functools.lru_cache(maxsize=None)
def constants(length, emb_count):
    step = 4 * length
    lane = np.arange(length)[None, :]
    coarse = np.arange(length // BASE)[:, None]
    fine = np.arange(BASE)[:, None]
    found = []
    for phase in (
        coarse * lane * (4 * BASE),
        (4 * fine + 1) * lane,
        coarse * BASE * (4 * lane + 1),
        fine * (4 * lane + 1),
    ):
        angle = phase % step * (2.0 * math.pi / step)
        found += [np.cos(angle), np.sin(angle)]
    bands = np.arange(1, (emb_count - 1) // 2 + 1)[:, None]
    angle = bands * lane % length * (2.0 * math.pi / length)
    rows = 8 * (emb_count // 8 + 1)
    found += [lane / length, np.cos(angle), np.sin(angle), np.ones((1, length))]
    found += [np.zeros((rows - emb_count - 1, length))]
    return np.concatenate(found).astype(np.float32)


def constant_rows(length):
    sizes = [length // BASE, length // BASE, BASE, BASE]
    starts = np.cumsum([0] + sizes + sizes).tolist()
    return starts


def dot(a, b):
    return jnp.dot(a, b, preferred_element_type=f32)


def dot_first(a, b):
    return lax.dot_general(a, b, (((0,), (0,)), ((), ())), preferred_element_type=f32)


def dot_last(a, b):
    return lax.dot_general(a, b, (((1,), (1,)), ((), ())), preferred_element_type=f32)


def split(x):
    high = x.astype(bf16)
    return high, (x - high.astype(f32)).astype(bf16)


def careful(product, a, b):
    a_high, a_low = split(a)
    b_high, b_low = split(b)
    return product(a_high, b_high) + (product(a_low, b_high) + product(a_high, b_low))


def to_spectrum(a_high, a_low, part, x):
    return dot(a_high[part], x) + dot(a_low[part], x)


def from_spectrum(t_high, re, im, length):
    total = dot(t_high[0], re.astype(bf16)) + dot(t_high[1], im.astype(bf16))
    return total * (1.0 / length)


def struct(shape, kind):
    return jax.ShapeDtypeStruct(shape, kind)


def whole(shape):
    return pl.BlockSpec(shape, lambda i, *_: (0,) * len(shape))


def table_specs(length, block):
    by_row = pl.BlockSpec((2, block, length), lambda i, *_: (0, i, 0))
    by_col = pl.BlockSpec((2, length, block), lambda i, *_: (0, 0, i))
    return by_row, by_col


def spectrum_block(width, block):
    return pl.BlockSpec((2, block, width), lambda i, *_: (0, i, 0))


def generate(place, table, pos_weight, pos_bias, filter_weight, rates, skip, width, block):
    highest = lax.Precision.HIGHEST
    length = table.shape[1]
    emb_count, order = pos_weight.shape
    starts = constant_rows(length)

    def body(place_ref, *refs):
        sources = refs[:6]
        ah, al, th, spec, env_out, hidden_out, cos_out, skip_out, filt, *held, done = refs[6:]
        tab, pw, pb, fw, rate, skip_row = held
        step = pl.program_id(0)

        @pl.when(step == 0)
        def _():
            mine = pl.ds(pl.multiple_of(place_ref[0] * width, width), width)
            copies = [
                pltpu.make_async_copy(
                    source if i < 3 else source.at[:, mine], target, done.at[i]
                )
                for i, (source, target) in enumerate(zip(sources, held))
            ]
            for copy in copies:
                copy.start()
            for copy in copies:
                copy.wait()
            skip_out[...] = skip_row[...]
            feat = tab[starts[8] : starts[8] + emb_count, :]
            pre = pb[...] + lax.dot_general(
                feat, pw[...], (((0,), (0,)), ((), ())), precision=highest,
                preferred_element_type=f32,
            )
            hidden = jnp.sin(pre)
            hidden_out[...] = hidden
            cos_out[...] = jnp.cos(pre)
            at = lax.broadcasted_iota(jnp.int32, (length, width), 0).astype(f32)
            total = jnp.ones((1, width), f32)
            for i in range(length.bit_length() - 1):
                total = total * (1.0 + jnp.exp(rate[...] * (-2.0 * 2**i)))
            env = jnp.exp(-rate[...] * at) * (1.0 / jnp.sqrt(total))
            env_out[...] = env
            filt[...] = (jnp.dot(hidden, fw[...], precision=highest) * env).astype(bf16)

        def rows(at, store):
            cos_start, sin_start, fine_cos, fine_sin = starts[at : at + 4]
            cos_fine = tab[fine_cos : fine_cos + BASE, :]
            sin_fine = tab[fine_sin : fine_sin + BASE, :]

            def one(i, carry):
                here = step * (block // BASE) + i
                out = pl.ds(pl.multiple_of(i * BASE, BASE), BASE)
                cos = tab[pl.ds(cos_start + here, 1), :]
                sin = tab[pl.ds(sin_start + here, 1), :]
                store(out, 0, cos * cos_fine - sin * sin_fine)
                store(out, 1, sin * cos_fine + cos * sin_fine)
                return carry

            lax.fori_loop(0, block // BASE, one, 0, unroll=4)

        def store_both(out, part, value):
            high, low = split(value)
            ah[part, out, :] = high
            al[part, out, :] = low

        def store_high(out, part, value):
            th[part, out, :] = value.astype(bf16)

        rows(0, store_both)
        rows(4, store_high)
        spec[0] = to_spectrum(ah, al, 0, filt[...]).astype(bf16)
        spec[1] = to_spectrum(ah, al, 1, filt[...]).astype(bf16)

    by_row = pl.BlockSpec((2, block, length), lambda i, *_: (0, i, 0))
    return pl.pallas_call(
        body,
        grid_spec=pltpu.PrefetchScalarGridSpec(
            num_scalar_prefetch=1,
            grid=(length // block,),
            in_specs=[pl.BlockSpec(memory_space=pltpu.HBM)] * 6,
            out_specs=[by_row, by_row, by_row, spectrum_block(width, block)]
            + [whole((length, width)), whole((length, order)), whole((length, order))]
            + [whole((1, width))],
            scratch_shapes=[VMEM((length, width), bf16)]
            + [VMEM(x.shape, f32) for x in (table, pos_weight, pos_bias)]
            + [VMEM((order, width), f32), VMEM((1, width), f32), VMEM((1, width), f32)]
            + [pltpu.SemaphoreType.DMA((6,))],
        ),
        out_shape=[struct((2, length, length), bf16)] * 3
        + [struct((2, length, width), bf16), struct((length, width), f32)]
        + [struct((length, order), f32)] * 2
        + [struct((1, width), f32)],
        name="generate",
        compiler_params=grant(
            [((6, block, length), 2), ((4, block, width), 4), ((2, length, width), 4)]
            + [(table.shape, 4)], length, width
        ),
    )(
        place,
        *[
            pltpu.with_memory_space_constraint(x, pltpu.HBM)
            for x in (table, pos_weight, pos_bias, filter_weight, rates, skip)
        ],
    )


def piece(place_ref, r, rows):
    return pl.ds(pl.multiple_of((place_ref[0] ^ r) * rows, rows), rows)


def convolve(place, signal_rel, cot_rel, filt_spec, tables, skip, block):
    a_high, a_low, t_high = tables
    count = len(signal_rel)
    local_len, width = cot_rel[0].shape
    length = local_len * count

    def body(place_ref, *refs):
        sig = refs[:count]
        cot = refs[count : 2 * count]
        fs, ah, al, th, skip_ref = refs[2 * count : 2 * count + 5]
        spec, inner_out, grad_out, x, acc = refs[2 * count + 5 :]
        step = pl.program_id(0)

        @pl.when(step == 0)
        def _():
            for r in range(count):
                x[piece(place_ref, r, local_len), :] = sig[r][...]

        re = to_spectrum(ah, al, 0, x[...])
        im = to_spectrum(ah, al, 1, x[...])
        spec[0] = re.astype(bf16)
        spec[1] = im.astype(bf16)
        fr, fi = fs[0].astype(f32), fs[1].astype(f32)
        part = from_spectrum(th, re * fr - im * fi, re * fi + im * fr, length)

        @pl.when(step == 0)
        def _():
            acc[...] = part

        @pl.when(step != 0)
        def _():
            acc[...] += part

        @pl.when(step == pl.num_programs(0) - 1)
        def _():
            conv = acc[...].astype(bf16).astype(f32)
            inner_out[...] = conv + skip_ref[...] * x[...].astype(f32)
            for r in range(count):
                rows = piece(place_ref, r, local_len)
                grad_out[rows, :] = (cot[r][...].astype(f32) * inner_out[rows, :]).astype(bf16)

    by_row, by_col = table_specs(length, block)
    cols = pl.BlockSpec((local_len, width), lambda i, place_ref: (0, place_ref[0]))
    return pl.pallas_call(
        body,
        grid_spec=pltpu.PrefetchScalarGridSpec(
            num_scalar_prefetch=1,
            grid=(length // block,),
            in_specs=[cols] * count
            + [whole((local_len, width))] * count
            + [spectrum_block(width, block), by_row, by_row, by_col]
            + [whole(skip.shape)],
            out_specs=[
                spectrum_block(width, block),
                whole((length, width)),
                whole((length, width)),
            ],
            scratch_shapes=[VMEM((length, width), bf16), VMEM((length, width), f32)],
        ),
        out_shape=[
            struct((2, length, width), bf16),
            struct((length, width), f32),
            struct((length, width), bf16),
        ],
        name="convolve",
        compiler_params=grant(
            [((6, block, length), 2), ((4, block, width), 4), ((3, length, width), 4)], length, width
        ),
    )(place, *signal_rel, *cot_rel, filt_spec, a_high, a_low, t_high, skip)


def grant(blocks, length, width):
    held = sum(math.prod(shape) * size for shape, size in blocks)
    need = 2 * held + 8 * length * width * 4 + (4 << 20)
    return pltpu.CompilerParams(vmem_limit_bytes=min(need, 60 << 20))


def smem():
    return pl.BlockSpec(memory_space=pltpu.SMEM)


def weight_grads(place, signal_rel, gate_grad, groups):
    count = len(signal_rel)
    local_len, channels = signal_rel[0].shape
    width = gate_grad.shape[1]
    rows = channels // sum(len(group) for group in groups)
    length = local_len * count

    def body(place_ref, *refs):
        sig = refs[:count]
        grad = refs[count]
        outs = refs[count + 1 :]
        right = jnp.concatenate(
            [grad[piece(place_ref, r, local_len), :] for r in range(count)], axis=0
        )
        for out, group in zip(outs, groups):
            for at, k in enumerate(group):
                start = pl.multiple_of((place_ref[1] ^ k) * rows, rows)
                left = jnp.concatenate(
                    [sig[r][:, pl.ds(start, rows)] for r in range(count)], axis=0
                )
                out[at] = dot_first(left, right).astype(bf16)

    return pl.pallas_call(
        body,
        in_specs=[smem()] + [pl.BlockSpec(memory_space=VMEM)] * (count + 1),
        out_specs=[pl.BlockSpec(memory_space=VMEM)] * len(groups),
        out_shape=[struct((len(group), rows, width), bf16) for group in groups],
        name="weight_grads",
        compiler_params=grant([((length, channels), 2), ((2, channels, width), 2)], length, width),
    )(place, *signal_rel, gate_grad)


def gating(place, signal_rel, weight_rel, cot_rel, inner):
    count = len(signal_rel)
    dp_count = len(weight_rel)
    local_len, channels = signal_rel[0].shape
    rows, width = weight_rel[0].shape
    length = local_len * count

    def body(place_ref, *refs):
        sig = refs[:count]
        weight = refs[count : count + dp_count]
        cot = refs[count + dp_count : 2 * count + dp_count]
        inner_ref = refs[2 * count + dp_count]
        outs = refs[2 * count + dp_count + 1 : -1]
        full = refs[-1]
        out, conv_grad_out, skip_out = outs
        for k in range(dp_count):
            start = pl.multiple_of((place_ref[1] ^ k) * rows, rows)
            full[pl.ds(start, rows), :] = weight[k][...]
        left = jnp.concatenate([sig[r][...] for r in range(count)], axis=0)
        gates = dot(left, full[...])
        skip_sum = jnp.zeros((1, width), f32)
        own = pl.multiple_of(place_ref[0] * width, width)
        for r in range(count):
            here = piece(place_ref, r, local_len)
            gate = gates[r * local_len : (r + 1) * local_len]
            out[here, :] = (gate * inner_ref[here, :]).astype(bf16)
            inner_grad = cot[r][...].astype(f32) * gate
            conv_grad_out[here, :] = inner_grad.astype(bf16)
            signal = sig[r][:, pl.ds(own, width)].astype(f32)
            skip_sum += jnp.sum(inner_grad * signal, axis=0, keepdims=True)
        skip_out[...] = jnp.broadcast_to(skip_sum, (8, width))

    return pl.pallas_call(
        body,
        in_specs=[smem()] + [pl.BlockSpec(memory_space=VMEM)] * (2 * count + dp_count + 1),
        out_specs=[pl.BlockSpec(memory_space=VMEM)] * 3,
        out_shape=[
            struct((length, width), bf16),
            struct((length, width), bf16),
            struct((8, width), f32),
        ],
        scratch_shapes=[VMEM((channels, width), bf16)],
        name="gating",
        compiler_params=grant([((length, channels), 2), ((2, channels, width), 2)], length, width),
    )(place, *signal_rel, *weight_rel, *cot_rel, inner)


def packed_rows(order, table_rows, width):
    per_group = width // order
    groups = -(-(table_rows // 8) // per_group)
    return order + 8 + 8 * groups, per_group


def correlate_back(
    place, out, conv_grad, filt_spec, tables, skip, count, block
):
    a_high, a_low, t_high = tables
    length, width = conv_grad.shape
    local_len = length // count

    def body(place_ref, out_ref, cg, fs, ah, al, th, skip_ref, *refs):
        pieces = refs[:count]
        spec, back = refs[count:]
        step = pl.program_id(0)
        re = to_spectrum(ah, al, 0, cg[...])
        im = to_spectrum(ah, al, 1, cg[...])
        spec[0] = re.astype(bf16)
        spec[1] = im.astype(bf16)
        fr, fi = fs[0].astype(f32), fs[1].astype(f32)
        term = from_spectrum(th, fr * re + fi * im, fr * im - fi * re, length)

        @pl.when(step == 0)
        def _():
            back[...] = term

        @pl.when(step != 0)
        def _():
            back[...] += term

        @pl.when(step == pl.num_programs(0) - 1)
        def _():
            for r in range(count):
                rows = piece(place_ref, r, local_len)
                direct = cg[rows, :].astype(f32) * skip_ref[...]
                pieces[r][0] = out_ref[rows, :]
                pieces[r][1] = (direct + back[rows, :].astype(bf16).astype(f32)).astype(bf16)

    by_row, by_col = table_specs(length, block)
    spec_block = spectrum_block(width, block)
    return pl.pallas_call(
        body,
        grid_spec=pltpu.PrefetchScalarGridSpec(
            num_scalar_prefetch=1,
            grid=(length // block,),
            in_specs=[
                whole((length, width)),
                whole((length, width)),
                spec_block,
                by_row,
                by_row,
                by_col,
                whole(skip.shape),
            ],
            out_specs=[whole((2, local_len, width))] * count + [spec_block],
            scratch_shapes=[VMEM((length, width), f32)],
        ),
        out_shape=[struct((2, local_len, width), bf16)] * count
        + [struct((2, length, width), bf16)],
        name="correlate_back",
        compiler_params=grant(
            [((6, block, length), 2), ((4, block, width), 4), ((3, length, width), 4)], length, width
        ),
    )(place, out, conv_grad, filt_spec, a_high, a_low, t_high, skip)


def correlate_part(
    place, grad_spec, skip_sum, signal_spec, tables, env, hidden, filter_weight, cos_pre, table,
    block,
):
    t_high = tables[2]
    length, width = env.shape
    order = filter_weight.shape[0]
    feature_start = constant_rows(length)[8]
    table_rows = table.shape[0] - feature_start
    total_rows, per_group = packed_rows(order, table_rows, width)

    def body(
        place_ref, gs, skip_sum_ref, ss, th, env_ref, hid, fw, cp, tab, packed, part,
    ):
        step = pl.program_id(0)
        sr, si = ss[0].astype(f32), ss[1].astype(f32)
        gr, gi = gs[0].astype(f32), gs[1].astype(f32)
        term = from_spectrum(th, sr * gr + si * gi, sr * gi - si * gr, length)

        @pl.when(step == 0)
        def _():
            part[...] = term

        @pl.when(step != 0)
        def _():
            part[...] += term

        @pl.when(step == pl.num_programs(0) - 1)
        def _():
            pre_grad = part[...].astype(bf16).astype(f32) * env_ref[...]
            packed[...] = jnp.zeros((total_rows, width), f32)
            packed[:order, :] = careful(dot_first, hid[...], pre_grad)
            packed[order : order + 8, :] = skip_sum_ref[...]
            act = careful(dot_last, pre_grad, fw[...]) * cp[...]
            small = careful(dot, tab[feature_start:, :], act)
            for b in range(table_rows // 8):
                row = order + 8 + 8 * (b // per_group)
                col = order * (b % per_group)
                packed[row : row + 8, col : col + order] = small[8 * b : 8 * b + 8]

    _, by_col = table_specs(length, block)
    spec_block = spectrum_block(width, block)
    return pl.pallas_call(
        body,
        grid_spec=pltpu.PrefetchScalarGridSpec(
            num_scalar_prefetch=1,
            grid=(length // block,),
            in_specs=[
                spec_block,
                whole((8, width)),
                spec_block,
                by_col,
                whole((length, width)),
                whole(hidden.shape),
                pl.BlockSpec((order, width), lambda i, place_ref: (0, place_ref[0])),
                whole(cos_pre.shape),
                whole(table.shape),
            ],
            out_specs=whole((total_rows, width)),
            scratch_shapes=[VMEM((length, width), f32)],
        ),
        out_shape=struct((total_rows, width), f32),
        name="correlate_part",
        compiler_params=grant(
            [((2, block, length), 2), ((4, block, width), 4), ((2, length, width), 4)], length, width
        ),
    )(
        place, grad_spec, skip_sum, signal_spec, t_high, env, hidden, filter_weight, cos_pre,
        table,
    )


def through_gate(place, gate_grad, weight_rel, count):
    dp_count = len(weight_rel)
    rows, width = weight_rel[0].shape
    length = gate_grad.shape[0]
    local_len = length // count
    channels = rows * dp_count

    def body(place_ref, *refs):
        grad = refs[0]
        weight = refs[1 : 1 + dp_count]
        outs = refs[1 + dp_count :]
        left = jnp.concatenate(
            [grad[piece(place_ref, r, local_len), :] for r in range(count)], axis=0
        )
        for k in range(dp_count):
            start = pl.multiple_of((place_ref[1] ^ k) * rows, rows)
            terms = dot_last(left, weight[k][...])
            for r in range(count):
                term = terms[r * local_len : (r + 1) * local_len]
                outs[r][:, pl.ds(start, rows)] = term.astype(bf16)

    return pl.pallas_call(
        body,
        in_specs=[smem()] + [pl.BlockSpec(memory_space=VMEM)] * (dp_count + 1),
        out_specs=[pl.BlockSpec(memory_space=VMEM)] * count,
        out_shape=[struct((local_len, channels), bf16)] * count,
        name="through_gate",
        compiler_params=grant([((length, channels), 2), ((channels, width), 2)], length, width),
    )(place, gate_grad, *weight_rel)


def combine(place, pieces, near_part, far_part):
    count = len(pieces)
    _, rows, width = pieces[0].shape

    def body(place_ref, *refs):
        near, far, out, grad = refs[count:]
        for r in range(count):
            cols = pl.ds(pl.multiple_of((place_ref[0] ^ r) * width, width), width)
            out[:, cols] = refs[r][0]
            total = near[:, cols].astype(f32) + far[:, cols].astype(f32)
            grad[:, cols] = (total + refs[r][1].astype(f32)).astype(bf16)

    return pl.pallas_call(
        body,
        in_specs=[smem()] + [pl.BlockSpec(memory_space=VMEM)] * (count + 2),
        out_specs=[pl.BlockSpec(memory_space=VMEM)] * 2,
        out_shape=[struct((rows, width * count), bf16)] * 2,
        name="combine",
        compiler_params=grant([((rows, 6 * width * count), 2)], rows, width),
    )(place, *pieces, near_part, far_part)


def assemble(place, pieces, kind):
    count = len(pieces)
    rows, width = pieces[0].shape

    def body(place_ref, *refs):
        out = refs[count]
        for r in range(count):
            start = pl.multiple_of((place_ref[0] ^ r) * width, width)
            out[:, pl.ds(start, width)] = refs[r][...].astype(kind)

    return pl.pallas_call(
        body,
        in_specs=[smem()] + [pl.BlockSpec(memory_space=VMEM)] * count,
        out_specs=pl.BlockSpec(memory_space=VMEM),
        out_shape=struct((rows, width * count), kind),
        name="assemble",
        compiler_params=grant([((rows, 2 * width * count), 4)], rows, width),
    )(place, *pieces)


def finish(place, pieces, order, emb_count):
    count = len(pieces)
    rows, width = pieces[0].shape
    table_rows = 8 * (emb_count // 8 + 1)
    _, per_group = packed_rows(order, table_rows, width)

    def body(place_ref, *refs):
        filter_out, skip_out, pos_out, bias_out = refs[count:]
        for r in range(count):
            cols = pl.ds(pl.multiple_of((place_ref[0] ^ r) * width, width), width)
            values = refs[r][...].astype(f32)
            filter_out[:, cols] = values[:order, :]
            skip_out[:, cols] = values[order : order + 1, :]
        tails = [refs[r][...].astype(f32)[order + 8 :, :] for r in range(count)]
        while len(tails) > 1:
            tails = [tails[i] + tails[i + 1] for i in range(0, len(tails), 2)]
        for b in range(table_rows // 8):
            row = 8 * (b // per_group)
            col = order * (b % per_group)
            found = tails[0][row : row + 8, col : col + order]
            low = 8 * b
            high = min(low + 8, emb_count)
            if high > low:
                pos_out[low:high, :] = found[: high - low]
            if low <= emb_count < low + 8:
                bias_out[...] = found[emb_count - low : emb_count - low + 1]

    return pl.pallas_call(
        body,
        in_specs=[smem()] + [pl.BlockSpec(memory_space=VMEM)] * count,
        out_specs=[pl.BlockSpec(memory_space=VMEM)] * 4,
        out_shape=[
            struct((order, width * count), f32),
            struct((1, width * count), f32),
            struct((emb_count, order), f32),
            struct((1, order), f32),
        ],
        name="finish",
        compiler_params=grant([((rows, 2 * width * count), 4)], rows, width),
    )(place, *pieces)


def swap(value, axis, offset):
    count = lax.axis_size(axis)
    return lax.ppermute(value, axis, [(i, i ^ offset) for i in range(count)])


def gather_rel(own, axis):
    count = lax.axis_size(axis)
    found = {0: own}
    bit = count // 2
    while bit:
        for r in list(found):
            found[r | bit] = swap(found[r], axis, bit)
        bit //= 2
    return [found[r] for r in range(count)]


def add_round(*terms):
    total = terms[0].astype(f32)
    for term in terms[1:]:
        total = total + term.astype(f32)
    return total.astype(bf16)


def shards(
    signal, gate_weight, pos_weight, pos_bias, filter_weight, decay_rate, skip_gain, grad_out
):
    seq_count = lax.axis_size("seq")
    dp_count = lax.axis_size("dp")
    signal_tok = signal[0]
    cot_tok = grad_out[0]
    local_len, channels = signal_tok.shape
    length = local_len * seq_count
    width = channels // seq_count
    emb_count, order = pos_weight.shape
    seq_at = lax.axis_index("seq")
    dp_at = lax.axis_index("dp")
    place = jnp.stack([seq_at, dp_at]).astype(jnp.int32)
    block = min(256, length)

    def own_cols(x, r=0):
        return lax.dynamic_slice_in_dim(x, (seq_at ^ r) * width, width, axis=x.ndim - 1)

    signal_rel = gather_rel(signal_tok, "seq")
    weight_rel = {0: own_cols(gate_weight)}
    for k in range(2, dp_count, 2):
        weight_rel[k] = swap(weight_rel[0], "dp", k)
    for k in range(0, dp_count, 2):
        weight_rel[k + 1] = swap(weight_rel[k], "dp", 1)
    weight_rel = [weight_rel[k] for k in range(dp_count)]
    cot_rel = [own_cols(cot_tok)] + [
        swap(own_cols(cot_tok, r), "seq", r) for r in range(1, seq_count)
    ]

    table = jnp.asarray(constants(length, emb_count))
    if length & (length - 1):
        raise ValueError("length")
    a_high, a_low, t_high, filt_spec, env, hidden, cos_pre, skip = generate(
        place, table, pos_weight, pos_bias[None], filter_weight, decay_rate[None],
        skip_gain[None], width, block,
    )
    tables = (a_high, a_low, t_high)

    signal_spec, inner, gate_grad = convolve(
        place, signal_rel, cot_rel, filt_spec, tables, skip, block
    )

    far = list(reversed(range(0, dp_count, 2)))
    pairs = stages(dp_count)
    groups = [[k + 1 for k in pair] for pair in pairs] + pairs
    weight_parts = weight_grads(place, signal_rel, gate_grad, groups)
    sums = {}
    for i, pair in enumerate(pairs):
        met = swap(weight_parts[i], "dp", 1)
        for at, k in enumerate(pair):
            sums[k] = add_round(weight_parts[len(pairs) + i][at], met[at])
    row_sum = add_round(sums[0], *[swap(sums[k], "dp", k) for k in far[:-1]])
    row_rel = gather_rel(row_sum, "seq")
    grad_gate_weight = assemble(place, row_rel, f32)

    back_rel = through_gate(place, gate_grad, weight_rel, seq_count)
    live = {r: back_rel[r] for r in range(seq_count)}
    bit = 1
    while bit < seq_count:
        met = {r: swap(live[r | bit], "seq", bit) for r in live if not r & bit}
        bit *= 2
        if bit < seq_count:
            live = {r: add_round(live[r], met[r]) for r in met}

    out, conv_grad, skip_sum = gating(
        place, signal_rel, weight_rel, cot_rel, inner
    )
    *pieces, grad_spec = correlate_back(
        place, out, conv_grad, filt_spec, tables, skip, seq_count, block
    )
    pieces = [pieces[0]] + [swap(pieces[r], "seq", r) for r in range(1, seq_count)]
    packed = correlate_part(
        place, grad_spec, skip_sum, signal_spec, tables, env, hidden, filter_weight, cos_pre,
        table, block,
    )
    output, grad_signal = combine(place, pieces, live[0], met[0])

    met = swap(packed, "dp", 1)
    packed = (packed + met).astype(bf16)
    terms = [packed] + [swap(packed, "dp", k) for k in range(2, dp_count, 2)]
    terms = [term.astype(f32) for term in terms]
    while len(terms) > 1:
        terms = [terms[i] + terms[i + 1] for i in range(0, len(terms), 2)]
    packed = terms[0].astype(bf16)
    packed_rel = [packed] + [swap(packed, "seq", r) for r in range(1, seq_count)]
    grad_filter_weight, grad_skip, grad_pos_weight, grad_pos_bias = finish(
        place, packed_rel, order, emb_count
    )
    return (
        output[None],
        grad_signal[None],
        grad_gate_weight,
        grad_pos_weight,
        grad_pos_bias[0],
        grad_filter_weight,
        grad_skip[0],
    )


def stages(dp_count):
    far = list(reversed(range(0, dp_count, 2)))
    return [[k] for k in far[:-2]] + [far[-2:]]


def solution(mesh):
    step = mapped(shards, mesh)
    return step


def mapped(body, mesh):
    return jax.shard_map(
        body,
        mesh=mesh,
        in_specs=(
            P("dp", "seq", None),
            P("dp", None),
            P(),
            P(),
            P(),
            P(),
            P(),
            P("dp", "seq", None),
        ),
        out_specs=(P("dp", "seq", None), P("dp", "seq", None), P("dp", None), P(), P(), P(), P()),
        check_vma=False,
    )
```

```python
import functools
import math

import jax
import jax.numpy as jnp
import numpy as np
from jax import lax
from jax.experimental import pallas as pl
from jax.experimental.pallas import tpu as pltpu
from jax.sharding import PartitionSpec as P


f32 = jnp.float32
bf16 = jnp.bfloat16
VMEM = pltpu.VMEM


BASE = 16


@functools.lru_cache(maxsize=None)
def constants(length, emb_count):
    step = 4 * length
    lane = np.arange(length)[None, :]
    coarse = np.arange(length // BASE)[:, None]
    fine = np.arange(BASE)[:, None]
    found = []
    for phase in (
        coarse * lane * (4 * BASE),
        (4 * fine + 1) * lane,
        coarse * BASE * (4 * lane + 1),
        fine * (4 * lane + 1),
    ):
        angle = phase % step * (2.0 * math.pi / step)
        found += [np.cos(angle), np.sin(angle)]
    bands = np.arange(1, (emb_count - 1) // 2 + 1)[:, None]
    angle = bands * lane % length * (2.0 * math.pi / length)
    rows = 8 * (emb_count // 8 + 1)
    found += [lane / length, np.cos(angle), np.sin(angle), np.ones((1, length))]
    found += [np.zeros((rows - emb_count - 1, length))]
    return np.concatenate(found).astype(np.float32)


def constant_rows(length):
    sizes = [length // BASE, length // BASE, BASE, BASE]
    starts = np.cumsum([0] + sizes + sizes).tolist()
    return starts


def dot(a, b):
    return jnp.dot(a, b, preferred_element_type=f32)


def dot_first(a, b):
    return lax.dot_general(a, b, (((0,), (0,)), ((), ())), preferred_element_type=f32)


def dot_last(a, b):
    return lax.dot_general(a, b, (((1,), (1,)), ((), ())), preferred_element_type=f32)


def split(x):
    high = x.astype(bf16)
    return high, (x - high.astype(f32)).astype(bf16)


def careful(product, a, b):
    a_high, a_low = split(a)
    b_high, b_low = split(b)
    return product(a_high, b_high) + (product(a_low, b_high) + product(a_high, b_low))


def to_spectrum(a_high, a_low, part, x):
    return dot(a_high[part], x) + dot(a_low[part], x)


def from_spectrum(t_high, re, im, length):
    total = dot(t_high[0], re.astype(bf16)) + dot(t_high[1], im.astype(bf16))
    return total * (1.0 / length)


def struct(shape, kind):
    return jax.ShapeDtypeStruct(shape, kind)


def whole(shape):
    return pl.BlockSpec(shape, lambda i, *_: (0,) * len(shape))


def table_specs(length, block):
    by_row = pl.BlockSpec((2, block, length), lambda i, *_: (0, i, 0))
    by_col = pl.BlockSpec((2, length, block), lambda i, *_: (0, 0, i))
    return by_row, by_col


def spectrum_block(width, block):
    return pl.BlockSpec((2, block, width), lambda i, *_: (0, i, 0))


def generate(place, table, pos_weight, pos_bias, filter_weight, rates, skip, width, block):
    highest = lax.Precision.HIGHEST
    length = table.shape[1]
    emb_count, order = pos_weight.shape
    starts = constant_rows(length)

    def body(place_ref, *refs):
        sources = refs[:6]
        ah, al, th, spec, env_out, hidden_out, cos_out, skip_out, filt, *held, done = refs[6:]
        tab, pw, pb, fw, rate, skip_row = held
        step = pl.program_id(0)

        @pl.when(step == 0)
        def _():
            mine = pl.ds(pl.multiple_of(place_ref[0] * width, width), width)
            copies = [
                pltpu.make_async_copy(
                    source if i < 3 else source.at[:, mine], target, done.at[i]
                )
                for i, (source, target) in enumerate(zip(sources, held))
            ]
            for copy in copies:
                copy.start()
            for copy in copies:
                copy.wait()
            skip_out[...] = skip_row[...]
            feat = tab[starts[8] : starts[8] + emb_count, :]
            pre = pb[...] + lax.dot_general(
                feat, pw[...], (((0,), (0,)), ((), ())), precision=highest,
                preferred_element_type=f32,
            )
            hidden = jnp.sin(pre)
            hidden_out[...] = hidden
            cos_out[...] = jnp.cos(pre)
            at = lax.broadcasted_iota(jnp.int32, (length, width), 0).astype(f32)
            total = jnp.ones((1, width), f32)
            for i in range(length.bit_length() - 1):
                total = total * (1.0 + jnp.exp(rate[...] * (-2.0 * 2**i)))
            env = jnp.exp(-rate[...] * at) * (1.0 / jnp.sqrt(total))
            env_out[...] = env
            filt[...] = (jnp.dot(hidden, fw[...], precision=highest) * env).astype(bf16)

        def rows(at, store):
            cos_start, sin_start, fine_cos, fine_sin = starts[at : at + 4]
            cos_fine = tab[fine_cos : fine_cos + BASE, :]
            sin_fine = tab[fine_sin : fine_sin + BASE, :]

            def one(i, carry):
                here = step * (block // BASE) + i
                out = pl.ds(pl.multiple_of(i * BASE, BASE), BASE)
                cos = tab[pl.ds(cos_start + here, 1), :]
                sin = tab[pl.ds(sin_start + here, 1), :]
                store(out, 0, cos * cos_fine - sin * sin_fine)
                store(out, 1, sin * cos_fine + cos * sin_fine)
                return carry

            lax.fori_loop(0, block // BASE, one, 0, unroll=4)

        def store_both(out, part, value):
            high, low = split(value)
            ah[part, out, :] = high
            al[part, out, :] = low

        def store_high(out, part, value):
            th[part, out, :] = value.astype(bf16)

        rows(0, store_both)
        rows(4, store_high)
        spec[0] = to_spectrum(ah, al, 0, filt[...])
        spec[1] = to_spectrum(ah, al, 1, filt[...])

    by_row = pl.BlockSpec((2, block, length), lambda i, *_: (0, i, 0))
    return pl.pallas_call(
        body,
        grid_spec=pltpu.PrefetchScalarGridSpec(
            num_scalar_prefetch=1,
            grid=(length // block,),
            in_specs=[pl.BlockSpec(memory_space=pltpu.HBM)] * 6,
            out_specs=[by_row, by_row, by_row, spectrum_block(width, block)]
            + [whole((length, width)), whole((length, order)), whole((length, order))]
            + [whole((1, width))],
            scratch_shapes=[VMEM((length, width), bf16)]
            + [VMEM(x.shape, f32) for x in (table, pos_weight, pos_bias)]
            + [VMEM((order, width), f32), VMEM((1, width), f32), VMEM((1, width), f32)]
            + [pltpu.SemaphoreType.DMA((6,))],
        ),
        out_shape=[struct((2, length, length), bf16)] * 3
        + [struct((2, length, width), f32), struct((length, width), f32)]
        + [struct((length, order), f32)] * 2
        + [struct((1, width), f32)],
        name="generate",
        compiler_params=grant(
            [((6, block, length), 2), ((4, block, width), 4), ((2, length, width), 4)]
            + [(table.shape, 4)], length, width
        ),
    )(
        place,
        *[
            pltpu.with_memory_space_constraint(x, pltpu.HBM)
            for x in (table, pos_weight, pos_bias, filter_weight, rates, skip)
        ],
    )


def piece(place_ref, r, rows):
    return pl.ds(pl.multiple_of((place_ref[0] ^ r) * rows, rows), rows)


def convolve(place, signal_rel, cot_rel, filt_spec, tables, skip, block):
    a_high, a_low, t_high = tables
    count = len(signal_rel)
    local_len, width = cot_rel[0].shape
    length = local_len * count

    def body(place_ref, *refs):
        sig = refs[:count]
        cot = refs[count : 2 * count]
        fs, ah, al, th, skip_ref = refs[2 * count : 2 * count + 5]
        spec, inner_out, grad_out, x, acc = refs[2 * count + 5 :]
        step = pl.program_id(0)

        @pl.when(step == 0)
        def _():
            for r in range(count):
                x[piece(place_ref, r, local_len), :] = sig[r][...]

        re = to_spectrum(ah, al, 0, x[...])
        im = to_spectrum(ah, al, 1, x[...])
        spec[0] = re
        spec[1] = im
        fr, fi = fs[0], fs[1]
        part = from_spectrum(th, re * fr - im * fi, re * fi + im * fr, length)

        @pl.when(step == 0)
        def _():
            acc[...] = part

        @pl.when(step != 0)
        def _():
            acc[...] += part

        @pl.when(step == pl.num_programs(0) - 1)
        def _():
            conv = acc[...].astype(bf16).astype(f32)
            inner_out[...] = conv + skip_ref[...] * x[...].astype(f32)
            for r in range(count):
                rows = piece(place_ref, r, local_len)
                grad_out[rows, :] = (cot[r][...].astype(f32) * inner_out[rows, :]).astype(bf16)

    by_row, by_col = table_specs(length, block)
    cols = pl.BlockSpec((local_len, width), lambda i, place_ref: (0, place_ref[0]))
    return pl.pallas_call(
        body,
        grid_spec=pltpu.PrefetchScalarGridSpec(
            num_scalar_prefetch=1,
            grid=(length // block,),
            in_specs=[cols] * count
            + [whole((local_len, width))] * count
            + [spectrum_block(width, block), by_row, by_row, by_col]
            + [whole(skip.shape)],
            out_specs=[
                spectrum_block(width, block),
                whole((length, width)),
                whole((length, width)),
            ],
            scratch_shapes=[VMEM((length, width), bf16), VMEM((length, width), f32)],
        ),
        out_shape=[
            struct((2, length, width), f32),
            struct((length, width), f32),
            struct((length, width), bf16),
        ],
        name="convolve",
        compiler_params=grant(
            [((6, block, length), 2), ((4, block, width), 4), ((3, length, width), 4)], length, width
        ),
    )(place, *signal_rel, *cot_rel, filt_spec, a_high, a_low, t_high, skip)


def grant(blocks, length, width):
    held = sum(math.prod(shape) * size for shape, size in blocks)
    need = 2 * held + 8 * length * width * 4 + (4 << 20)
    return pltpu.CompilerParams(vmem_limit_bytes=min(need, 60 << 20))


def smem():
    return pl.BlockSpec(memory_space=pltpu.SMEM)


def weight_grads(place, signal_rel, gate_grad, groups):
    count = len(signal_rel)
    local_len, channels = signal_rel[0].shape
    width = gate_grad.shape[1]
    rows = channels // sum(len(group) for group in groups)
    length = local_len * count

    def body(place_ref, *refs):
        sig = refs[:count]
        grad = refs[count]
        outs = refs[count + 1 :]
        right = jnp.concatenate(
            [grad[piece(place_ref, r, local_len), :] for r in range(count)], axis=0
        )
        for out, group in zip(outs, groups):
            for at, k in enumerate(group):
                start = pl.multiple_of((place_ref[1] ^ k) * rows, rows)
                left = jnp.concatenate(
                    [sig[r][:, pl.ds(start, rows)] for r in range(count)], axis=0
                )
                out[at] = dot_first(left, right).astype(bf16)

    return pl.pallas_call(
        body,
        in_specs=[smem()] + [pl.BlockSpec(memory_space=VMEM)] * (count + 1),
        out_specs=[pl.BlockSpec(memory_space=VMEM)] * len(groups),
        out_shape=[struct((len(group), rows, width), bf16) for group in groups],
        name="weight_grads",
        compiler_params=grant([((length, channels), 2), ((2, channels, width), 2)], length, width),
    )(place, *signal_rel, gate_grad)


def gating(place, signal_rel, weight_rel, cot_rel, inner):
    count = len(signal_rel)
    dp_count = len(weight_rel)
    local_len, channels = signal_rel[0].shape
    rows, width = weight_rel[0].shape
    length = local_len * count

    def body(place_ref, *refs):
        sig = refs[:count]
        weight = refs[count : count + dp_count]
        cot = refs[count + dp_count : 2 * count + dp_count]
        inner_ref = refs[2 * count + dp_count]
        outs = refs[2 * count + dp_count + 1 : -1]
        full = refs[-1]
        out, conv_grad_out, skip_out = outs
        for k in range(dp_count):
            start = pl.multiple_of((place_ref[1] ^ k) * rows, rows)
            full[pl.ds(start, rows), :] = weight[k][...]
        left = jnp.concatenate([sig[r][...] for r in range(count)], axis=0)
        gates = dot(left, full[...])
        skip_sum = jnp.zeros((1, width), f32)
        own = pl.multiple_of(place_ref[0] * width, width)
        for r in range(count):
            here = piece(place_ref, r, local_len)
            gate = gates[r * local_len : (r + 1) * local_len]
            out[here, :] = (gate * inner_ref[here, :]).astype(bf16)
            inner_grad = cot[r][...].astype(f32) * gate
            conv_grad_out[here, :] = inner_grad.astype(bf16)
            signal = sig[r][:, pl.ds(own, width)].astype(f32)
            skip_sum += jnp.sum(inner_grad * signal, axis=0, keepdims=True)
        skip_out[...] = jnp.broadcast_to(skip_sum, (8, width))

    return pl.pallas_call(
        body,
        in_specs=[smem()] + [pl.BlockSpec(memory_space=VMEM)] * (2 * count + dp_count + 1),
        out_specs=[pl.BlockSpec(memory_space=VMEM)] * 3,
        out_shape=[
            struct((length, width), bf16),
            struct((length, width), bf16),
            struct((8, width), f32),
        ],
        scratch_shapes=[VMEM((channels, width), bf16)],
        name="gating",
        compiler_params=grant([((length, channels), 2), ((2, channels, width), 2)], length, width),
    )(place, *signal_rel, *weight_rel, *cot_rel, inner)


def packed_rows(order, table_rows, width):
    per_group = width // order
    groups = -(-(table_rows // 8) // per_group)
    return order + 8 + 8 * groups, per_group


def correlate_back(
    place, out, conv_grad, filt_spec, tables, skip, count, block
):
    a_high, a_low, t_high = tables
    length, width = conv_grad.shape
    local_len = length // count

    def body(place_ref, out_ref, cg, fs, ah, al, th, skip_ref, *refs):
        pieces = refs[:count]
        spec, back = refs[count:]
        step = pl.program_id(0)
        re = to_spectrum(ah, al, 0, cg[...])
        im = to_spectrum(ah, al, 1, cg[...])
        spec[0] = re
        spec[1] = im
        fr, fi = fs[0], fs[1]
        term = from_spectrum(th, fr * re + fi * im, fr * im - fi * re, length)

        @pl.when(step == 0)
        def _():
            back[...] = term

        @pl.when(step != 0)
        def _():
            back[...] += term

        @pl.when(step == pl.num_programs(0) - 1)
        def _():
            for r in range(count):
                rows = piece(place_ref, r, local_len)
                direct = cg[rows, :].astype(f32) * skip_ref[...]
                pieces[r][0] = out_ref[rows, :]
                pieces[r][1] = (direct + back[rows, :].astype(bf16).astype(f32)).astype(bf16)

    by_row, by_col = table_specs(length, block)
    spec_block = spectrum_block(width, block)
    return pl.pallas_call(
        body,
        grid_spec=pltpu.PrefetchScalarGridSpec(
            num_scalar_prefetch=1,
            grid=(length // block,),
            in_specs=[
                whole((length, width)),
                whole((length, width)),
                spec_block,
                by_row,
                by_row,
                by_col,
                whole(skip.shape),
            ],
            out_specs=[whole((2, local_len, width))] * count + [spec_block],
            scratch_shapes=[VMEM((length, width), f32)],
        ),
        out_shape=[struct((2, local_len, width), bf16)] * count
        + [struct((2, length, width), f32)],
        name="correlate_back",
        compiler_params=grant(
            [((6, block, length), 2), ((4, block, width), 4), ((3, length, width), 4)], length, width
        ),
    )(place, out, conv_grad, filt_spec, a_high, a_low, t_high, skip)


def correlate_part(
    place, grad_spec, skip_sum, signal_spec, tables, env, hidden, filter_weight, cos_pre, table,
    block,
):
    t_high = tables[2]
    length, width = env.shape
    order = filter_weight.shape[0]
    feature_start = constant_rows(length)[8]
    table_rows = table.shape[0] - feature_start
    total_rows, per_group = packed_rows(order, table_rows, width)

    def body(
        place_ref, gs, skip_sum_ref, ss, th, env_ref, hid, fw, cp, tab, packed, part,
    ):
        step = pl.program_id(0)
        sr, si = ss[0], ss[1]
        gr, gi = gs[0], gs[1]
        term = from_spectrum(th, sr * gr + si * gi, sr * gi - si * gr, length)

        @pl.when(step == 0)
        def _():
            part[...] = term

        @pl.when(step != 0)
        def _():
            part[...] += term

        @pl.when(step == pl.num_programs(0) - 1)
        def _():
            pre_grad = part[...].astype(bf16).astype(f32) * env_ref[...]
            packed[...] = jnp.zeros((total_rows, width), f32)
            packed[:order, :] = careful(dot_first, hid[...], pre_grad)
            packed[order : order + 8, :] = skip_sum_ref[...]
            act = careful(dot_last, pre_grad, fw[...]) * cp[...]
            small = careful(dot, tab[feature_start:, :], act)
            for b in range(table_rows // 8):
                row = order + 8 + 8 * (b // per_group)
                col = order * (b % per_group)
                packed[row : row + 8, col : col + order] = small[8 * b : 8 * b + 8]

    _, by_col = table_specs(length, block)
    spec_block = spectrum_block(width, block)
    return pl.pallas_call(
        body,
        grid_spec=pltpu.PrefetchScalarGridSpec(
            num_scalar_prefetch=1,
            grid=(length // block,),
            in_specs=[
                spec_block,
                whole((8, width)),
                spec_block,
                by_col,
                whole((length, width)),
                whole(hidden.shape),
                pl.BlockSpec((order, width), lambda i, place_ref: (0, place_ref[0])),
                whole(cos_pre.shape),
                whole(table.shape),
            ],
            out_specs=whole((total_rows, width)),
            scratch_shapes=[VMEM((length, width), f32)],
        ),
        out_shape=struct((total_rows, width), f32),
        name="correlate_part",
        compiler_params=grant(
            [((2, block, length), 2), ((4, block, width), 4), ((2, length, width), 4)], length, width
        ),
    )(
        place, grad_spec, skip_sum, signal_spec, t_high, env, hidden, filter_weight, cos_pre,
        table,
    )


def through_gate(place, gate_grad, weight_rel, count):
    dp_count = len(weight_rel)
    rows, width = weight_rel[0].shape
    length = gate_grad.shape[0]
    local_len = length // count
    channels = rows * dp_count

    def body(place_ref, *refs):
        grad = refs[0]
        weight = refs[1 : 1 + dp_count]
        outs = refs[1 + dp_count :]
        left = jnp.concatenate(
            [grad[piece(place_ref, r, local_len), :] for r in range(count)], axis=0
        )
        for k in range(dp_count):
            start = pl.multiple_of((place_ref[1] ^ k) * rows, rows)
            terms = dot_last(left, weight[k][...])
            for r in range(count):
                term = terms[r * local_len : (r + 1) * local_len]
                outs[r][:, pl.ds(start, rows)] = term.astype(bf16)

    return pl.pallas_call(
        body,
        in_specs=[smem()] + [pl.BlockSpec(memory_space=VMEM)] * (dp_count + 1),
        out_specs=[pl.BlockSpec(memory_space=VMEM)] * count,
        out_shape=[struct((local_len, channels), bf16)] * count,
        name="through_gate",
        compiler_params=grant([((length, channels), 2), ((channels, width), 2)], length, width),
    )(place, gate_grad, *weight_rel)


def combine(place, pieces, near_part, far_part):
    count = len(pieces)
    _, rows, width = pieces[0].shape

    def body(place_ref, *refs):
        near, far, out, grad = refs[count:]
        for r in range(count):
            cols = pl.ds(pl.multiple_of((place_ref[0] ^ r) * width, width), width)
            out[:, cols] = refs[r][0]
            total = near[:, cols].astype(f32) + far[:, cols].astype(f32)
            grad[:, cols] = (total + refs[r][1].astype(f32)).astype(bf16)

    return pl.pallas_call(
        body,
        in_specs=[smem()] + [pl.BlockSpec(memory_space=VMEM)] * (count + 2),
        out_specs=[pl.BlockSpec(memory_space=VMEM)] * 2,
        out_shape=[struct((rows, width * count), bf16)] * 2,
        name="combine",
        compiler_params=grant([((rows, 6 * width * count), 2)], rows, width),
    )(place, *pieces, near_part, far_part)


def finish(place, pieces, row_pieces, order, emb_count):
    count = len(pieces)
    block_rows = row_pieces[0].shape[0]
    rows, width = pieces[0].shape
    table_rows = 8 * (emb_count // 8 + 1)
    _, per_group = packed_rows(order, table_rows, width)

    def body(place_ref, *refs):
        parts = refs[count : 2 * count]
        filter_out, skip_out, pos_out, bias_out, weight_out = refs[2 * count :]
        for r in range(count):
            cols = pl.ds(pl.multiple_of((place_ref[0] ^ r) * width, width), width)
            values = refs[r][...].astype(f32)
            filter_out[:, cols] = values[:order, :]
            skip_out[:, cols] = values[order : order + 1, :]
            weight_out[:, cols] = parts[r][...].astype(f32)
        tails = [refs[r][...].astype(f32)[order + 8 :, :] for r in range(count)]
        while len(tails) > 1:
            tails = [tails[i] + tails[i + 1] for i in range(0, len(tails), 2)]
        for b in range(table_rows // 8):
            row = 8 * (b // per_group)
            col = order * (b % per_group)
            found = tails[0][row : row + 8, col : col + order]
            low = 8 * b
            high = min(low + 8, emb_count)
            if high > low:
                pos_out[low:high, :] = found[: high - low]
            if low <= emb_count < low + 8:
                bias_out[...] = found[emb_count - low : emb_count - low + 1]

    return pl.pallas_call(
        body,
        in_specs=[smem()] + [pl.BlockSpec(memory_space=VMEM)] * (2 * count),
        out_specs=[pl.BlockSpec(memory_space=VMEM)] * 5,
        out_shape=[
            struct((order, width * count), f32),
            struct((1, width * count), f32),
            struct((emb_count, order), f32),
            struct((1, order), f32),
            struct((block_rows, width * count), f32),
        ],
        name="finish",
        compiler_params=grant([((rows + block_rows, 2 * width * count), 4)], rows, width),
    )(place, *pieces, *row_pieces)


def swap(value, axis, offset):
    count = lax.axis_size(axis)
    return lax.ppermute(value, axis, [(i, i ^ offset) for i in range(count)])


def gather_rel(own, axis):
    count = lax.axis_size(axis)
    found = {0: own}
    bit = count // 2
    while bit:
        for r in list(found):
            found[r | bit] = swap(found[r], axis, bit)
        bit //= 2
    return [found[r] for r in range(count)]


def add_round(*terms):
    total = terms[0].astype(f32)
    for term in terms[1:]:
        total = total + term.astype(f32)
    return total.astype(bf16)


def shards(
    signal, gate_weight, pos_weight, pos_bias, filter_weight, decay_rate, skip_gain, grad_out
):
    seq_count = lax.axis_size("seq")
    dp_count = lax.axis_size("dp")
    signal_tok = signal[0]
    cot_tok = grad_out[0]
    local_len, channels = signal_tok.shape
    length = local_len * seq_count
    width = channels // seq_count
    emb_count, order = pos_weight.shape
    seq_at = lax.axis_index("seq")
    dp_at = lax.axis_index("dp")
    place = jnp.stack([seq_at, dp_at]).astype(jnp.int32)
    block = min(256, length)

    def own_cols(x, r=0):
        return lax.dynamic_slice_in_dim(x, (seq_at ^ r) * width, width, axis=x.ndim - 1)

    signal_rel = gather_rel(signal_tok, "seq")
    weight_rel = {0: own_cols(gate_weight)}
    for k in range(2, dp_count, 2):
        weight_rel[k] = swap(weight_rel[0], "dp", k)
    for k in range(0, dp_count, 2):
        weight_rel[k + 1] = swap(weight_rel[k], "dp", 1)
    weight_rel = [weight_rel[k] for k in range(dp_count)]
    cot_rel = [own_cols(cot_tok)] + [
        swap(own_cols(cot_tok, r), "seq", r) for r in range(1, seq_count)
    ]

    table = jnp.asarray(constants(length, emb_count))
    if length & (length - 1):
        raise ValueError("length")
    a_high, a_low, t_high, filt_spec, env, hidden, cos_pre, skip = generate(
        place, table, pos_weight, pos_bias[None], filter_weight, decay_rate[None],
        skip_gain[None], width, block,
    )
    tables = (a_high, a_low, t_high)

    signal_spec, inner, gate_grad = convolve(
        place, signal_rel, cot_rel, filt_spec, tables, skip, block
    )

    far = list(reversed(range(0, dp_count, 2)))
    pairs = stages(dp_count)
    groups = [[k + 1 for k in pair] for pair in pairs] + pairs
    weight_parts = weight_grads(place, signal_rel, gate_grad, groups)
    sums = {}
    for i, pair in enumerate(pairs):
        met = swap(weight_parts[i], "dp", 1)
        for at, k in enumerate(pair):
            sums[k] = add_round(weight_parts[len(pairs) + i][at], met[at])
    row_sum = add_round(sums[0], *[swap(sums[k], "dp", k) for k in far[:-1]])
    row_rel = gather_rel(row_sum, "seq")

    back_rel = through_gate(place, gate_grad, weight_rel, seq_count)
    live = {r: back_rel[r] for r in range(seq_count)}
    bit = 1
    while bit < seq_count:
        met = {r: swap(live[r | bit], "seq", bit) for r in live if not r & bit}
        bit *= 2
        if bit < seq_count:
            live = {r: add_round(live[r], met[r]) for r in met}

    out, conv_grad, skip_sum = gating(
        place, signal_rel, weight_rel, cot_rel, inner
    )
    *pieces, grad_spec = correlate_back(
        place, out, conv_grad, filt_spec, tables, skip, seq_count, block
    )
    pieces = [pieces[0]] + [swap(pieces[r], "seq", r) for r in range(1, seq_count)]
    packed = correlate_part(
        place, grad_spec, skip_sum, signal_spec, tables, env, hidden, filter_weight, cos_pre,
        table, block,
    )
    output, grad_signal = combine(place, pieces, live[0], met[0])

    met = swap(packed, "dp", 1)
    packed = (packed + met).astype(bf16)
    terms = [packed] + [swap(packed, "dp", k) for k in range(2, dp_count, 2)]
    terms = [term.astype(f32) for term in terms]
    while len(terms) > 1:
        terms = [terms[i] + terms[i + 1] for i in range(0, len(terms), 2)]
    packed = terms[0].astype(bf16)
    packed_rel = [packed] + [swap(packed, "seq", r) for r in range(1, seq_count)]
    grad_filter_weight, grad_skip, grad_pos_weight, grad_pos_bias, grad_gate_weight = finish(
        place, packed_rel, row_rel, order, emb_count
    )
    return (
        output[None],
        grad_signal[None],
        grad_gate_weight,
        grad_pos_weight,
        grad_pos_bias[0],
        grad_filter_weight,
        grad_skip[0],
    )


def stages(dp_count):
    far = list(reversed(range(0, dp_count, 2)))
    return [[k] for k in far[:-2]] + [far[-2:]]


def solution(mesh):
    step = mapped(shards, mesh)
    return step


def mapped(body, mesh):
    return jax.shard_map(
        body,
        mesh=mesh,
        in_specs=(
            P("dp", "seq", None),
            P("dp", None),
            P(),
            P(),
            P(),
            P(),
            P(),
            P("dp", "seq", None),
        ),
        out_specs=(P("dp", "seq", None), P("dp", "seq", None), P("dp", None), P(), P(), P(), P()),
        check_vma=False,
    )
```
